32 devices in a mesh: grp: 2 (over y), tm: 2 (over core), row: 8 (over z, x).
Axes of the slice: x: 2, y: 2, z: 4, core: 2. Of those that a mesh axis runs over, the one named last changes fastest.
Arguments:
- inputs: bfloat16 [8, 8, 43008], P(('grp', 'tm'), 'row'), parts along dimension 0, may hold values from -6 to 6
- weight: bfloat16 [5184, 192], replicated, may hold values from -0.078125 to 0.078125
- cotangent: bfloat16 [8, 8, 43008], P(('grp', 'tm'), 'row'), parts along dimension 0, may hold values from -6 to 6
Outputs:
- output: bfloat16 [8, 8, 43008], P(('grp', 'tm'), 'row'), parts along dimension 0
- input_grad: bfloat16 [8, 8, 43008], P(('grp', 'tm'), 'row'), parts along dimension 0
- filter_grad: bfloat16 [1990656], P(('grp', 'tm', 'row')), parts along dimension 0
The draws below stay inside these ranges and needn't reach their ends.
There are 2 independent parts, one for each index of `grp`. The reference program is written for one: setup_inputs(seed, part) draws one part's arguments, and reference() takes and returns one part's arrays. A program takes and returns all parts, laid end to end along the dimension named above; an argument that names none is the same for every part. Nothing has to cross between parts.
All inputs are finite; a program needn't handle non-finite values.
Results may differ from the reference program's by a relative error of at most 0.0051.
Values may be sent and summed in bfloat16 or wider, within the bound.
A program may use at most 64 MiB of HBM per device.

```python
import jax
import jax.numpy as jnp
from jax import lax

CH = 192
WIDTH = 224
FRAMES = 4
ROWS = 8


def levels(own_key, shape, split, least, largest):
    level, own = 1.0, jax.random.fold_in(own_key, 6)
    for position, shards_of in split:
        draws = jnp.exp(jax.random.uniform(jax.random.fold_in(own, position), (shards_of,), jnp.float32, least / len(split), largest / len(split)))
        level = level * jnp.repeat(draws, shape[position] // shards_of).reshape([-1 if axis == position else 1 for axis in range(len(shape))])
    return level


def scatter_about(key, dims, spread, limit, shards=(), held_as=jnp.bfloat16):
    level = levels(key, dims, shards, -0.22, 0.18) if shards else 1.0
    array = jax.random.normal(key, dims, jnp.float32) * spread * level
    return jnp.minimum(jnp.maximum(array, -limit), limit).astype(held_as)


def setup_inputs(seed: int = 0, part: int = 0) -> dict:
    key_of = jax.random.split(jax.random.key(seed), 4)
    own_keys = jax.random.split(jax.random.fold_in(key_of[3], part), 4)
    inputs = scatter_about(own_keys[0], (FRAMES, ROWS, WIDTH * CH), 1.0, 6.0, ((0, 2), (1, 8)))
    weight = scatter_about(key_of[1], (27 * CH, CH), (27 * CH) ** -0.5, 0.078125)
    cotangent = scatter_about(own_keys[2], (FRAMES, ROWS, WIDTH * CH), 1.0, 6.0, ((0, 2), (1, 8)))
    return dict(inputs=inputs, weight=weight, cotangent=cotangent)


def reference(inputs, weight, cotangent):
    frames = inputs.shape[0]
    rows = inputs.shape[1]
    x_four = inputs.reshape(frames, rows, WIDTH, CH)
    cot_four = cotangent.reshape(frames, rows, WIDTH, CH)
    act = jax.nn.silu(x_four.astype(jnp.float32)).astype(jnp.bfloat16)
    act_pad = jnp.pad(act, ((2, 0), (1, 1), (1, 1), (0, 0)))
    cot_pad = jnp.pad(cot_four, ((0, 2), (1, 1), (1, 1), (0, 0)))
    cot_flat = cot_four.reshape(-1, CH)
    output = jnp.zeros((frames * rows * WIDTH, CH), jnp.float32)
    grad_act = jnp.zeros((frames * rows * WIDTH, CH), jnp.float32)
    blocks = []
    for step_t in range(3):
        for step_h in range(3):
            for step_w in range(3):
                offset = ((step_t * 3 + step_h) * 3 + step_w) * CH
                kernel = weight[offset:offset + CH]
                piece = act_pad[step_t:step_t + frames, step_h:step_h + rows, step_w:step_w + WIDTH].reshape(-1, CH)
                output = output + jnp.dot(piece, kernel, preferred_element_type=jnp.float32)
                back_piece = cot_pad[2 - step_t:2 - step_t + frames, 2 - step_h:2 - step_h + rows, 2 - step_w:2 - step_w + WIDTH].reshape(-1, CH)
                grad_act = grad_act + lax.dot_general(back_piece, kernel, (((1,), (1,)), ((), ())), preferred_element_type=jnp.float32)
                blocks.append(lax.dot_general(piece, cot_flat, (((0,), (0,)), ((), ())), preferred_element_type=jnp.float32))
    x_float = x_four.reshape(-1, CH).astype(jnp.float32)
    sigma = jax.nn.sigmoid(x_float)
    input_grad = (grad_act * sigma * (1.0 + x_float * (1.0 - sigma))).astype(jnp.bfloat16)
    filter_grad = (jnp.concatenate(blocks, 0).reshape(-1) / (FRAMES * ROWS)).astype(jnp.bfloat16)
    shape = (frames, rows, WIDTH * CH)
    return output.astype(jnp.bfloat16).reshape(shape), input_grad.reshape(shape), filter_grad
```

```python
import functools

import jax
import jax.numpy as jnp
from jax import lax
from jax.experimental import pallas as pl
from jax.experimental.pallas import tpu as pltpu
from jax.sharding import PartitionSpec as P

CH = 192
WIDTH = 224
TAPS = 27
BLOCK = 2 * WIDTH
PACKED = 3 * WIDTH
PAIRS = 4
CHUNK = TAPS * CH // (4 * PAIRS)
TALL = CHUNK + 12
CUT = 176
PIECE = TALL + CUT
PITCH = 256


def fused_kernel(
    scale, x_ref, w_ref, c_ref, out_ref, ig_ref, fg_ref,
    act, cot, packed, weight_in, taps, act_t, shifted, filt, outgoing, passing, incoming, fwd, bwd, pad,
    weight_sem, send_sem, recv_sem, piece_send, pass_recv, piece_recv,
):
    f32, bf16 = jnp.float32, jnp.bfloat16
    grp, tm, row = lax.axis_index("grp"), lax.axis_index("tm"), lax.axis_index("row")
    pair, side = row // 2, row % 2
    own, other_slot = 1 + side, 2 - side

    def device(t, r):
        return (grp, t, r)

    barrier = pltpu.get_barrier_semaphore()

    def greet(target):
        pl.semaphore_signal(barrier, inc=1, device_id=target, device_id_type=pl.DeviceIdType.MESH)

    sibling = device(1 - tm, row)
    partner = device(tm, 2 * pair + 1 - side)
    greet(sibling)
    greet(partner)
    for step in range(1, PAIRS):
        greet(device(tm, 2 * ((pair + step) % PAIRS) + side))

    fetch = pltpu.make_async_copy(w_ref, weight_in, weight_sem)
    fetch.start()

    def half_of(array, slot, half):
        if array == 0:
            return act, pl.multiple_of((half + 1) * BLOCK, 16)
        return cot, pl.multiple_of(half * BLOCK, 16)

    def pack(array, slot, half, value):
        packed[array, slot, half, 0:BLOCK, :] = value[:, 0:128]
        packed[array, slot, half, BLOCK:PACKED, :] = jnp.concatenate(
            [value[0:WIDTH, 128:CH], value[WIDTH:BLOCK, 128:CH]], axis=1
        )

    def transpose(slot, half):
        for frame in range(2):
            rows_of = pl.ds(pl.multiple_of((half + 1) * BLOCK + frame * WIDTH, 16), WIDTH)
            value = jnp.concatenate(
                [act[slot, rows_of, :], jnp.zeros((PITCH - WIDTH, CH), bf16)], axis=0
            )
            lanes = pl.ds(pl.multiple_of((2 * half + 2 + frame) * PITCH, 128), PITCH)
            act_t[slot, :, lanes] = value.T

    def unpack(array, slot, half):
        ref, base = half_of(array, slot, half)
        ref[slot, pl.ds(base, BLOCK), 0:128] = packed[array, slot, half, 0:BLOCK, :]
        high = packed[array, slot, half, BLOCK:PACKED, :]
        ref[slot, pl.ds(base, WIDTH), 128:CH] = high[:, 0:64]
        ref[slot, pl.ds(pl.multiple_of(base + WIDTH, 16), WIDTH), 128:CH] = high[:, 64:128]
        if array == 0:
            transpose(slot, half)

    def move(array, src_slot, dst_slot, half, lane, target):
        return pltpu.make_async_remote_copy(
            src_ref=packed.at[array, src_slot, half],
            dst_ref=packed.at[array, dst_slot, half],
            send_sem=send_sem.at[lane],
            recv_sem=recv_sem.at[array, dst_slot, half],
            device_id=target,
            device_id_type=pl.DeviceIdType.MESH,
        )

    def arrived(array, slot, half):
        move(array, slot, slot, half, 0, sibling).wait_recv()

    outer_pair = pair + 2 * side - 1
    inner_pair = pair + 1 - 2 * side
    has_outer = jnp.logical_and(outer_pair >= 0, outer_pair < PAIRS)
    has_inner = jnp.logical_and(inner_pair >= 0, inner_pair < PAIRS)
    outer_same = device(tm, 2 * outer_pair + side)
    inner_same = device(tm, 2 * inner_pair + side)
    near_slot, far_slot = 3 * (1 - side), 3 * side
    has_before, has_after = pair > 0, pair < PAIRS - 1

    straight = [
        move(0, own, own, tm, 0, partner),
        move(0, own, own, tm, 1, sibling),
        move(1, own, own, tm, 2, partner),
        move(1, own, own, tm, 3, sibling),
    ]
    outward = move(0, own, near_slot, tm, 4, outer_same)
    relayed = [move(i, other_slot, far_slot, tm, 5 + i, inner_same) for i in range(2)]
    onward = [move(i, other_slot, other_slot, tm, 7 + i, sibling) for i in range(2)]
    near = move(0, near_slot, near_slot, tm, 9, sibling)
    far = [move(i, far_slot, far_slot, tm, 10 + i, sibling) for i in range(2)]

    x = x_ref[...].astype(f32)
    value = (x * (1.0 / (1.0 + jnp.exp(-x)))).astype(bf16)
    act[own, pl.ds(pl.multiple_of((tm + 1) * BLOCK, 16), BLOCK), :] = value
    pack(0, own, tm, value)
    pl.semaphore_wait(barrier, PAIRS + 1)
    straight[0].start()
    straight[1].start()

    @pl.when(has_outer)
    def _():
        outward.start()

    value = c_ref[...]
    cot[own, pl.ds(pl.multiple_of(tm * BLOCK, 16), BLOCK), :] = value
    pack(1, own, tm, value)
    straight[2].start()
    straight[3].start()

    for slot in range(4):
        act[slot, 0:BLOCK, :] = jnp.zeros((BLOCK, CH), bf16)
        cot[slot, 2 * BLOCK : 3 * BLOCK, :] = jnp.zeros((BLOCK, CH), bf16)
        act_t[slot, :, 0 : 2 * PITCH] = jnp.zeros((CH, 2 * PITCH), bf16)

    for slot, present in ((0, has_before), (3, has_after)):

        @pl.when(jnp.logical_not(present))
        def _():
            act[slot, BLOCK : 3 * BLOCK, :] = jnp.zeros((2 * BLOCK, CH), bf16)
            cot[slot, 0 : 2 * BLOCK, :] = jnp.zeros((2 * BLOCK, CH), bf16)
            act_t[slot, :, 2 * PITCH : 6 * PITCH] = jnp.zeros((CH, 4 * PITCH), bf16)

    pad[0:8, :] = jnp.zeros((8, CH), f32)
    pad[WIDTH + 8 : WIDTH + 16, :] = jnp.zeros((8, CH), f32)
    for frame in range(4):
        shifted[:, :, frame * PITCH + WIDTH : (frame + 1) * PITCH, :] = jnp.zeros(
            (3, 2, PITCH - WIDTH, CH), bf16
        )

    fetch.wait()
    for tap in range(TAPS):
        taps[tap] = weight_in[:, tap * CH : (tap + 1) * CH]
    transpose(own, tm)

    def convolve(act_h, cot_h, first):
        for step_w in range(3):
            y = z = None
            for step_t in range(3):
                a = act[side + act_h, pl.ds(pl.multiple_of((2 * tm + step_t) * WIDTH, 16), BLOCK), :]
                c = cot[
                    side + 2 - cot_h,
                    pl.ds(pl.multiple_of((2 * tm + 2 - step_t) * WIDTH, 16), BLOCK),
                    :,
                ]
                more_y = lax.dot_general(
                    a,
                    taps[(step_t * 3 + act_h) * 3 + step_w],
                    (((1,), (1,)), ((), ())),
                    preferred_element_type=f32,
                )
                more_z = jnp.dot(
                    c, taps[(step_t * 3 + cot_h) * 3 + step_w], preferred_element_type=f32
                )
                y = more_y if y is None else y + more_y
                z = more_z if z is None else z + more_z
            if first:
                fwd[step_w] = y
                bwd[step_w] = z
            else:
                fwd[step_w] += y
                bwd[step_w] += z

    def shift(h):
        for frame in range(4):
            value = cot[1 + h, frame * WIDTH : (frame + 1) * WIDTH, :]
            rows_of = pl.ds(frame * PITCH, WIDTH)
            pad[8 : WIDTH + 8, :] = value.astype(f32)
            shifted[0, h, rows_of, :] = pad[9 : WIDTH + 9, :].astype(bf16)
            shifted[1, h, rows_of, :] = value
            shifted[2, h, rows_of, :] = pad[7 : WIDTH + 7, :].astype(bf16)

    for array in range(2):
        arrived(array, own, 1 - tm)
        unpack(array, own, 1 - tm)
    convolve(1, 1, True)
    shift(side)

    arrived(0, other_slot, tm)
    onward[0].start()

    @pl.when(has_inner)
    def _():
        relayed[0].start()

    unpack(0, other_slot, tm)

    @pl.when(has_inner)
    def _():
        arrived(0, near_slot, tm)
        near.start()
        unpack(0, near_slot, tm)
        arrived(0, near_slot, 1 - tm)
        unpack(0, near_slot, 1 - tm)

    arrived(0, other_slot, 1 - tm)
    unpack(0, other_slot, 1 - tm)
    arrived(1, other_slot, tm)
    onward[1].start()

    @pl.when(has_inner)
    def _():
        relayed[1].start()

    unpack(1, other_slot, tm)
    arrived(1, other_slot, 1 - tm)
    unpack(1, other_slot, 1 - tm)
    shift(1 - side)

    @pl.when(has_outer)
    def _():
        arrived(0, far_slot, tm)
        far[0].start()
        unpack(0, far_slot, tm)
        arrived(0, far_slot, 1 - tm)
        unpack(0, far_slot, 1 - tm)

    part = pair // 2
    inner = (pair + part) % 2 == 1
    mate_pair = pair + 1 - 2 * (pair % 2)
    owners = (3 * (1 - part), 2 - part, mate_pair, pair)

    def shard(owner):
        return tm * 2 * PAIRS + 2 * owner + side

    def filter_sum(k):
        block = shard(owners[k]) * CHUNK // 16
        first_tap = block // (CH // 16)
        base = pl.multiple_of(block % (CH // 16) * 16, 16)

        def term(n):
            tap = first_tap + n
            step_t, step_h, step_w = tap // 9, tap // 3 % 3, tap % 3
            lanes = pl.ds(pl.multiple_of(step_t * PITCH, 128), 4 * PITCH)
            filt[k, n * CH : (n + 1) * CH, :] = jnp.dot(
                act_t[step_h, :, lanes], shifted[step_w, 0], preferred_element_type=f32
            ) + jnp.dot(act_t[step_h + 1, :, lanes], shifted[step_w, 1], preferred_element_type=f32)

        term(0)
        term(1)

        @pl.when(base + TALL > 2 * CH)
        def _():
            term(2)

        return base

    def folded(k, base):
        high = filt[k, pl.ds(base, TALL), 128:CH]
        return jnp.concatenate(
            [
                filt[k, pl.ds(base, TALL), 0:128],
                jnp.concatenate(
                    [
                        high[0:CUT],
                        jnp.concatenate([high[CUT:TALL], jnp.zeros((2 * CUT - TALL, 64), f32)], axis=0),
                    ],
                    axis=1,
                ),
            ],
            axis=0,
        )

    def piece(k, ref, slot, recv, owner):
        return pltpu.make_async_remote_copy(
            src_ref=outgoing.at[k],
            dst_ref=ref.at[slot],
            send_sem=piece_send.at[k],
            recv_sem=recv.at[slot],
            device_id=device(tm, 2 * owner + side),
            device_id_type=pl.DeviceIdType.MESH,
        )

    first_stage = [piece(k, passing, k, pass_recv, mate_pair) for k in range(2)]
    second_stage = [piece(k, incoming, 1, piece_recv, owners[k]) for k in range(2)]
    to_mate = piece(2, incoming, 0, piece_recv, mate_pair)
    bases = []
    for k in range(4):
        base = filter_sum(k)
        bases.append(base)
        if k < 2:

            @pl.when(jnp.logical_not(inner))
            def _():
                outgoing[k] = folded(k, base).astype(bf16)
                first_stage[k].start()

        elif k == 2:
            outgoing[k] = folded(k, base).astype(bf16)
            to_mate.start()

    convolve(2 - 2 * side, 2 * side, False)

    @pl.when(has_outer)
    def _():
        arrived(1, far_slot, tm)
        far[1].start()
        unpack(1, far_slot, tm)

    def second(k):
        @pl.when(inner)
        def _():
            first_stage[k].wait_recv()
            outgoing[k] = (folded(k, bases[k]) + passing[k].astype(f32)).astype(bf16)
            second_stage[k].start()

    second(0)

    @pl.when(has_outer)
    def _():
        arrived(1, far_slot, 1 - tm)
        unpack(1, far_slot, 1 - tm)

    convolve(2 * side, 2 - 2 * side, False)
    second(1)

    for frame in range(2):
        span = pl.ds(frame * WIDTH, WIDTH)
        inside = pl.ds(8, WIDTH)
        pad[inside, :] = fwd[0, span, :]
        value = fwd[1, span, :] + pad[7 : WIDTH + 7, :]
        pad[inside, :] = fwd[2, span, :]
        value = value + pad[9 : WIDTH + 9, :]
        out_ref[span, :] = value.astype(bf16)
        pad[inside, :] = bwd[0, span, :]
        value = bwd[1, span, :] + pad[9 : WIDTH + 9, :]
        pad[inside, :] = bwd[2, span, :]
        value = value + pad[7 : WIDTH + 7, :]
        x = x_ref[span, :].astype(f32)
        sigma = 1.0 / (1.0 + jnp.exp(-x))
        ig_ref[span, :] = (value * sigma * (1.0 + x * (1.0 - sigma))).astype(bf16)

    to_mate.wait_recv()
    total = folded(3, bases[3]) + incoming[0].astype(f32)
    second_stage[0].wait_recv()
    total = (total + incoming[1].astype(f32)) / scale
    filt[0, 0:TALL, 0:128] = total[0:TALL]
    filt[0, 0:CUT, 128:CH] = total[TALL:PIECE, 0:64]
    filt[0, CUT:TALL, 128:CH] = total[TALL : 2 * TALL - CUT, 64:128]
    for q in range(4):

        @pl.when(shard(pair) % 4 == q)
        def _():
            fg_ref[...] = filt[0, 4 * q : 4 * q + CHUNK, :].astype(bf16)

    for copy in straight + onward:
        copy.wait_send()

    @pl.when(has_outer)
    def _():
        outward.wait_send()
        for copy in far:
            copy.wait_send()

    @pl.when(has_inner)
    def _():
        near.wait_send()
        for copy in relayed:
            copy.wait_send()

    @pl.when(inner)
    def _():
        for copy in second_stage:
            copy.wait_send()

    @pl.when(jnp.logical_not(inner))
    def _():
        for copy in first_stage:
            copy.wait_send()

    to_mate.wait_send()


def fused(inputs, weight, cotangent):
    frames, rows = inputs.shape[:2]
    scale = frames * lax.axis_size("tm") * rows * lax.axis_size("row")
    vmem = pl.BlockSpec(memory_space=pltpu.VMEM)
    bf16, f32 = jnp.bfloat16, jnp.float32
    out, ig, fg = pl.pallas_call(
        functools.partial(fused_kernel, float(scale)),
        out_shape=(
            jax.ShapeDtypeStruct((BLOCK, CH), bf16),
            jax.ShapeDtypeStruct((BLOCK, CH), bf16),
            jax.ShapeDtypeStruct((CHUNK, CH), bf16),
        ),
        in_specs=[vmem, pl.BlockSpec(memory_space=pltpu.HBM), vmem],
        out_specs=(vmem, vmem, vmem),
        scratch_shapes=[
            pltpu.VMEM((4, 3 * BLOCK, CH), bf16),
            pltpu.VMEM((4, 3 * BLOCK, CH), bf16),
            pltpu.VMEM((2, 4, 2, PACKED, 128), bf16),
            pltpu.VMEM((CH, TAPS * CH), bf16),
            pltpu.VMEM((TAPS, CH, CH), bf16),
            pltpu.VMEM((4, CH, 6 * PITCH), bf16),
            pltpu.VMEM((3, 2, 4 * PITCH, CH), bf16),
            pltpu.VMEM((4, 3 * CH, CH), f32),
            pltpu.VMEM((3, PIECE, 128), bf16),
            pltpu.VMEM((2, PIECE, 128), bf16),
            pltpu.VMEM((2, PIECE, 128), bf16),
            pltpu.VMEM((3, BLOCK, CH), f32),
            pltpu.VMEM((3, BLOCK, CH), f32),
            pltpu.VMEM((WIDTH + 16, CH), f32),
            pltpu.SemaphoreType.DMA,
            pltpu.SemaphoreType.DMA((12,)),
            pltpu.SemaphoreType.DMA((2, 4, 2)),
            pltpu.SemaphoreType.DMA((3,)),
            pltpu.SemaphoreType.DMA((2,)),
            pltpu.SemaphoreType.DMA((2,)),
        ],
        compiler_params=pltpu.CompilerParams(
            collective_id=0, has_side_effects=True, vmem_limit_bytes=48 * 1024 * 1024
        ),
    )(inputs.reshape(BLOCK, CH), weight.T, cotangent.reshape(BLOCK, CH))
    shape = (frames, rows, WIDTH * CH)
    return out.reshape(shape), ig.reshape(shape), fg.reshape(-1)


def passed_along(array, axis, by):
    length = lax.axis_size(axis)
    pairs = [(i, i + by) for i in range(length) if 0 <= i + by < length]
    return lax.ppermute(array, axis, pairs)


def with_halo(array, sides, width):
    for axis, dim in sides:
        size, length = (lax.axis_size(axis), array.shape[dim])
        up = [(i, (i + 1) % size) for i in range(size - 1)]
        down = [(j, i) for i, j in up]
        last = lax.slice_in_dim(array, length - width, length, axis=dim)
        first = lax.slice_in_dim(array, 0, width, axis=dim)
        before = lax.ppermute(last, axis, up)
        after = lax.ppermute(first, axis, down)
        array = jnp.concatenate([before, array, after], axis=dim)
    return array


def on_device(inputs, weight, cotangent):
    frames = inputs.shape[0]
    rows = inputs.shape[1]
    act = jax.nn.silu(inputs.astype(jnp.float32)).astype(jnp.bfloat16)
    earlier = passed_along(act, "tm", 1)
    extended = jnp.concatenate([earlier, act], 0)
    extended = with_halo(extended, (("row", 1),), 1)
    extended = extended.reshape(frames + 2, rows + 2, WIDTH, CH)
    act_pad = jnp.pad(extended, ((0, 0), (0, 0), (1, 1), (0, 0)))
    cot_four = cotangent.reshape(frames, rows, WIDTH, CH)
    cot_flat = cot_four.reshape(-1, CH)
    output = jnp.zeros((frames * rows * WIDTH, CH), jnp.float32)
    blocks = []
    for step_t in range(3):
        for step_h in range(3):
            for step_w in range(3):
                offset = ((step_t * 3 + step_h) * 3 + step_w) * CH
                kernel = weight[offset : offset + CH]
                piece = act_pad[
                    step_t : step_t + frames, step_h : step_h + rows, step_w : step_w + WIDTH
                ].reshape(-1, CH)
                output = output + jnp.dot(piece, kernel, preferred_element_type=jnp.float32)
                blocks.append(
                    lax.dot_general(
                        piece,
                        cot_flat,
                        (((0,), (0,)), ((), ())),
                        preferred_element_type=jnp.float32,
                    )
                )
    spread = jnp.zeros((frames + 2, rows + 2, WIDTH + 2, CH), jnp.float32)
    for step_t in range(3):
        slab_weight = weight[step_t * 9 * CH : (step_t + 1) * 9 * CH]
        terms = lax.dot_general(
            cot_flat, slab_weight, (((1,), (1,)), ((), ())), preferred_element_type=jnp.float32
        )
        terms = terms.reshape(frames, rows, WIDTH, 9, CH)
        slab = jnp.zeros((frames, rows + 2, WIDTH + 2, CH), jnp.float32)
        for step_h in range(3):
            for step_w in range(3):
                slab = slab + jnp.pad(
                    terms[:, :, :, step_h * 3 + step_w],
                    ((0, 0), (step_h, 2 - step_h), (step_w, 2 - step_w), (0, 0)),
                )
        spread = spread + jnp.pad(slab, ((step_t, 2 - step_t), (0, 0), (0, 0), (0, 0)))
    inner = spread[:, :, 1 : WIDTH + 1]
    from_next = passed_along(inner[:, 0:1], "row", -1)
    from_prev = passed_along(inner[:, rows + 1 : rows + 2], "row", 1)
    center = inner[:, 1 : rows + 1]
    center = center.at[:, rows - 1 : rows].add(from_next)
    center = center.at[:, 0:1].add(from_prev)
    returned = passed_along(center[0:2], "tm", -1)
    grad_act = center[2:].at[frames - 2 :].add(returned).reshape(-1, CH)
    x_float = inputs.reshape(-1, CH).astype(jnp.float32)
    sigma = jax.nn.sigmoid(x_float)
    input_grad = (grad_act * sigma * (1.0 + x_float * (1.0 - sigma))).astype(jnp.bfloat16)
    local_filter = jnp.concatenate(blocks, 0).reshape(-1)
    frame_blocks = lax.axis_size("tm")
    row_blocks = lax.axis_size("row")
    scale = frames * frame_blocks * rows * row_blocks
    share = lax.psum_scatter(local_filter, ("tm", "row"), scatter_dimension=0, tiled=True)
    filter_grad = (share / scale).astype(jnp.bfloat16)
    shape = (frames, rows, WIDTH * CH)
    return (output.astype(jnp.bfloat16).reshape(shape), input_grad.reshape(shape), filter_grad)


def either(mesh, inputs, weight, cotangent):
    size = mesh.shape["row"]
    if mesh.shape["tm"] == 2 and size == 2 * PAIRS and inputs.shape[:2] == (2, 1):
        return fused(inputs, weight, cotangent)
    return on_device(inputs, weight, cotangent)


def solution(mesh):
    placed = (P(("grp", "tm"), "row", None), P(), P(("grp", "tm"), "row", None))
    return jax.shard_map(
        functools.partial(either, mesh),
        mesh=mesh,
        in_specs=placed,
        out_specs=(
            P(("grp", "tm"), "row", None),
            P(("grp", "tm"), "row", None),
            P(("grp", "tm", "row")),
        ),
        check_vma=False,
    )
```

```python
import functools

import jax
import jax.numpy as jnp
from jax import lax
from jax.experimental import pallas as pl
from jax.experimental.pallas import tpu as pltpu
from jax.sharding import PartitionSpec as P

CH = 192
WIDTH = 224
TAPS = 27
HALF = WIDTH // 2
PAIRS = 4
CHUNK = TAPS * CH // (4 * PAIRS)
TALL = CHUNK + 12
CUT = 176
PIECE = TALL + CUT
PITCH = 256


def fused_kernel(
    scale, x_ref, w_ref, c_ref, out_ref, ig_ref, fg_ref,
    x_in, c_in, weight_in, wide, factor, act, cot, fwd_even, fwd_odd, bwd_taps, act_t, shifted, filt,
    outgoing, passing, incoming, fwd, bwd, pad, sums,
    fetch_sem, send_sem, recv_sem, piece_send, pass_recv, piece_recv,
):
    f32, bf16 = jnp.float32, jnp.bfloat16
    grp, tm, row = lax.axis_index("grp"), lax.axis_index("tm"), lax.axis_index("row")
    pair, side = row // 2, row % 2
    own, other_slot = 1 + side, 2 - side

    def device(t, r):
        return (grp, t, r)

    barrier = pltpu.get_barrier_semaphore()

    def greet(target):
        pl.semaphore_signal(barrier, inc=1, device_id=target, device_id_type=pl.DeviceIdType.MESH)

    fetches = [
        pltpu.make_async_copy(src, dst, fetch_sem.at[i])
        for i, (src, dst) in enumerate(((x_ref, x_in), (c_ref, c_in), (w_ref, weight_in)))
    ]
    for fetch in fetches:
        fetch.start()

    sibling = device(1 - tm, row)
    partner = device(tm, 2 * pair + 1 - side)
    greet(sibling)
    greet(partner)
    for step in range(1, PAIRS):
        greet(device(tm, 2 * ((pair + step) % PAIRS) + side))

    def block(index):
        return pl.ds(pl.multiple_of(index * HALF, 16), HALF)

    def move(array, src_slot, dst_slot, half, lane, target):
        ref = cot if array else act
        span = pl.ds(pl.multiple_of((2 * half + 2 * (1 - array)) * HALF, 16), 2 * HALF)
        return pltpu.make_async_remote_copy(
            src_ref=ref.at[src_slot, :, span],
            dst_ref=ref.at[dst_slot, :, span],
            send_sem=send_sem.at[lane],
            recv_sem=recv_sem.at[array, dst_slot, half],
            device_id=target,
            device_id_type=pl.DeviceIdType.MESH,
        )

    def arrived(array, slot, half):
        move(array, slot, slot, half, 0, sibling).wait_recv()

    outer_pair = pair + 2 * side - 1
    inner_pair = pair + 1 - 2 * side
    has_outer = jnp.logical_and(outer_pair >= 0, outer_pair < PAIRS)
    has_inner = jnp.logical_and(inner_pair >= 0, inner_pair < PAIRS)
    outer_same = device(tm, 2 * outer_pair + side)
    inner_same = device(tm, 2 * inner_pair + side)
    near_slot, far_slot = 3 * (1 - side), 3 * side
    has_before, has_after = pair > 0, pair < PAIRS - 1

    straight = [
        move(0, own, own, tm, 0, partner),
        move(0, own, own, tm, 1, sibling),
        move(1, own, own, tm, 2, partner),
        move(1, own, own, tm, 3, sibling),
    ]
    outward = move(0, own, near_slot, tm, 4, outer_same)
    relayed = [move(i, other_slot, far_slot, tm, 5 + i, inner_same) for i in range(2)]
    onward = [move(i, other_slot, other_slot, tm, 7 + i, sibling) for i in range(2)]
    near = move(0, near_slot, near_slot, tm, 9, sibling)
    far = [move(i, far_slot, far_slot, tm, 10 + i, sibling) for i in range(2)]

    fetches[0].wait()
    wide[0] = x_in[...].astype(f32)
    for j in range(3):
        for frame in range(2):
            x = wide[0, pl.ds(2 * j + frame, HALF, stride=6), :]
            sigma = 1.0 / (1.0 + jnp.exp(-x))
            act[own, j, block(2 * tm + 2 + frame), :] = (x * sigma).astype(bf16)
            factor[j, frame] = sigma * (1.0 + x * (1.0 - sigma))
    fetches[1].wait()
    wide[1] = c_in[...].astype(f32)
    for j in range(3):
        for frame in range(2):
            value = wide[1, pl.ds(2 * j + frame, HALF, stride=6), :]
            cot[own, j, block(2 * tm + frame), :] = value.astype(bf16)

    pl.semaphore_wait(barrier, PAIRS + 1)
    straight[0].start()
    straight[1].start()

    @pl.when(has_outer)
    def _():
        outward.start()

    straight[2].start()
    straight[3].start()

    for slot in range(4):
        act[slot, :, 0 : 2 * HALF, :] = jnp.zeros((3, 2 * HALF, 128), bf16)
        cot[slot, :, 4 * HALF : 6 * HALF, :] = jnp.zeros((3, 2 * HALF, 128), bf16)
        act_t[slot, :, 0 : 2 * PITCH] = jnp.zeros((CH, 2 * PITCH), bf16)

    for slot, present in ((0, has_before), (3, has_after)):

        @pl.when(jnp.logical_not(present))
        def _():
            act[slot, :, 2 * HALF : 6 * HALF, :] = jnp.zeros((3, 4 * HALF, 128), bf16)
            cot[slot, :, 0 : 4 * HALF, :] = jnp.zeros((3, 4 * HALF, 128), bf16)
            act_t[slot, :, 2 * PITCH : 6 * PITCH] = jnp.zeros((CH, 4 * PITCH), bf16)

    pad[:, 0:8, :] = jnp.zeros((2, 8, CH), f32)
    pad[:, HALF + 8 : HALF + 16, :] = jnp.zeros((2, 8, CH), f32)
    for part in range(8):
        shifted[:, :, part * 128 + HALF : (part + 1) * 128, :] = jnp.zeros(
            (3, 2, 128 - HALF, CH), bf16
        )
    bwd_taps[:, 0:64, :] = jnp.zeros((TAPS, 64, CH), bf16)
    bwd_taps[:, 64 + CH : 128 + CH, :] = jnp.zeros((TAPS, 64, CH), bf16)

    fetches[2].wait()
    for tap in range(TAPS):
        value = weight_in[:, tap * CH : (tap + 1) * CH]
        fwd_even[tap] = jnp.concatenate([value, jnp.zeros((CH, 64), bf16)], axis=1)
        fwd_odd[tap] = jnp.concatenate([jnp.zeros((CH, 64), bf16), value], axis=1)
        bwd_taps[tap, 64 : 64 + CH, :] = value

    def transpose(slot, half):
        for frame in range(2):
            lane = (2 * half + 2 + frame) * PITCH
            even = pl.ds(pl.multiple_of(lane, 128), 128)
            odd = pl.ds(pl.multiple_of(lane + 128, 128), 128)

            def turned(j):
                value = act[slot, j, block(2 * half + 2 + frame), :]
                return jnp.concatenate([value, jnp.zeros((128 - HALF, 128), bf16)], axis=0).T

            act_t[slot, 0:128, even] = turned(0)
            both = turned(1)
            act_t[slot, 128:CH, even] = both[0:64]
            act_t[slot, 0:64, odd] = both[64:128]
            act_t[slot, 64:CH, odd] = turned(2)

    transpose(own, tm)

    def dots(ref, slot, starts, weights, out, first):
        def side_of(start, j):
            rows_of = pl.ds(pl.multiple_of(start, 16), 2 * HALF)
            return jnp.concatenate([ref[slot, j, rows_of, :], ref[slot, j + 1, rows_of, :]], axis=1)

        for i, terms in enumerate((((0, 1), (1, 2)), ((1, 1), (0, 0)), ((0, 2),), ((1, 0),))):
            total = None
            for step_t in range(3):
                for odd, step_w in terms:
                    more = weights(side_of(starts[step_t], odd), odd, step_t, step_w)
                    total = more if total is None else total + more
            if first:
                out[i] = total
            else:
                out[i] += total

    def convolve(act_h, cot_h, first):
        def forward(value, odd, step_t, step_w):
            taps = fwd_odd if odd else fwd_even
            return lax.dot_general(
                value,
                taps[(step_t * 3 + act_h) * 3 + step_w],
                (((1,), (1,)), ((), ())),
                preferred_element_type=f32,
            )

        def backward(value, odd, step_t, step_w):
            first_row = 0 if odd else 64
            return jnp.dot(
                value,
                bwd_taps[(step_t * 3 + cot_h) * 3 + 2 - step_w, first_row : first_row + 256, :],
                preferred_element_type=f32,
            )

        starts = [(2 * tm + step_t) * HALF for step_t in range(3)]
        dots(act, side + act_h, starts, forward, fwd, first)
        dots(cot, side + 2 - cot_h, starts[::-1], backward, bwd, first)

    def shift(h):
        for frame in range(4):
            rows_of = slice(frame * HALF, (frame + 1) * HALF)
            mid = cot[1 + h, 1, rows_of, :]
            even = jnp.concatenate([cot[1 + h, 0, rows_of, :], mid[:, 0:64]], axis=1)
            odd = jnp.concatenate([mid[:, 64:128], cot[1 + h, 2, rows_of, :]], axis=1)
            pad[0, 8 : HALF + 8, :] = even.astype(f32)
            pad[1, 8 : HALF + 8, :] = odd.astype(f32)
            at = frame * PITCH
            shifted[0, h, at : at + HALF, :] = odd
            shifted[0, h, at + 128 : at + 128 + HALF, :] = pad[0, 9 : HALF + 9, :].astype(bf16)
            shifted[1, h, at : at + HALF, :] = even
            shifted[1, h, at + 128 : at + 128 + HALF, :] = odd
            shifted[2, h, at : at + HALF, :] = pad[1, 7 : HALF + 7, :].astype(bf16)
            shifted[2, h, at + 128 : at + 128 + HALF, :] = even

    arrived(0, own, 1 - tm)
    arrived(1, own, 1 - tm)
    convolve(1, 1, True)
    transpose(own, 1 - tm)
    shift(side)

    arrived(0, other_slot, tm)
    onward[0].start()

    @pl.when(has_inner)
    def _():
        relayed[0].start()

    transpose(other_slot, tm)

    @pl.when(has_inner)
    def _():
        arrived(0, near_slot, tm)
        near.start()
        transpose(near_slot, tm)
        arrived(0, near_slot, 1 - tm)
        transpose(near_slot, 1 - tm)

    arrived(0, other_slot, 1 - tm)
    transpose(other_slot, 1 - tm)
    arrived(1, other_slot, tm)
    onward[1].start()

    @pl.when(has_inner)
    def _():
        relayed[1].start()

    arrived(1, other_slot, 1 - tm)
    shift(1 - side)

    @pl.when(has_outer)
    def _():
        arrived(0, far_slot, tm)
        far[0].start()
        transpose(far_slot, tm)
        arrived(0, far_slot, 1 - tm)
        transpose(far_slot, 1 - tm)

    part = pair // 2
    inner = (pair + part) % 2 == 1
    mate_pair = pair + 1 - 2 * (pair % 2)
    owners = (3 * (1 - part), 2 - part, mate_pair, pair)

    def shard(owner):
        return tm * 2 * PAIRS + 2 * owner + side

    def filter_sum(k):
        first_block = shard(owners[k]) * CHUNK // 16
        first_tap = first_block // (CH // 16)
        base = pl.multiple_of(first_block % (CH // 16) * 16, 16)

        def term(n):
            tap = first_tap + n
            step_t, step_h, step_w = tap // 9, tap // 3 % 3, tap % 3
            lanes = pl.ds(pl.multiple_of(step_t * PITCH, 128), 4 * PITCH)
            filt[k, n * CH : (n + 1) * CH, :] = jnp.dot(
                act_t[step_h, :, lanes], shifted[step_w, 0], preferred_element_type=f32
            ) + jnp.dot(act_t[step_h + 1, :, lanes], shifted[step_w, 1], preferred_element_type=f32)

        term(0)
        term(1)

        @pl.when(base + TALL > 2 * CH)
        def _():
            term(2)

        return base

    def folded(k, base):
        high = filt[k, pl.ds(base, TALL), 128:CH]
        return jnp.concatenate(
            [
                filt[k, pl.ds(base, TALL), 0:128],
                jnp.concatenate(
                    [
                        high[0:CUT],
                        jnp.concatenate([high[CUT:TALL], jnp.zeros((2 * CUT - TALL, 64), f32)], axis=0),
                    ],
                    axis=1,
                ),
            ],
            axis=0,
        )

    def piece(k, ref, slot, recv, owner):
        return pltpu.make_async_remote_copy(
            src_ref=outgoing.at[k],
            dst_ref=ref.at[slot],
            send_sem=piece_send.at[k],
            recv_sem=recv.at[slot],
            device_id=device(tm, 2 * owner + side),
            device_id_type=pl.DeviceIdType.MESH,
        )

    first_stage = [piece(k, passing, k, pass_recv, mate_pair) for k in range(2)]
    second_stage = [piece(k, incoming, 1, piece_recv, owners[k]) for k in range(2)]
    to_mate = piece(2, incoming, 0, piece_recv, mate_pair)
    bases = []
    for k in range(4):
        base = filter_sum(k)
        bases.append(base)
        if k < 2:

            @pl.when(jnp.logical_not(inner))
            def _():
                outgoing[k] = folded(k, base).astype(bf16)
                first_stage[k].start()

        elif k == 2:
            outgoing[k] = folded(k, base).astype(bf16)
            to_mate.start()

    convolve(2 - 2 * side, 2 * side, False)

    @pl.when(has_outer)
    def _():
        arrived(1, far_slot, tm)
        far[1].start()

    def second(k):
        @pl.when(inner)
        def _():
            first_stage[k].wait_recv()
            outgoing[k] = (folded(k, bases[k]) + passing[k].astype(f32)).astype(bf16)
            second_stage[k].start()

    second(0)

    @pl.when(has_outer)
    def _():
        arrived(1, far_slot, 1 - tm)

    convolve(2 * side, 2 - 2 * side, False)
    second(1)

    def finish(total, slot, weighted):
        for frame in range(2):
            span = slice(frame * HALF, (frame + 1) * HALF)
            pad[0, 8 : HALF + 8, :] = total[3, span, :]
            pad[1, 8 : HALF + 8, :] = total[2, span, :]
            even = total[0, span, :] + pad[0, 7 : HALF + 7, :]
            odd = total[1, span, :] + pad[1, 9 : HALF + 9, :]
            lanes = (
                even[:, 0:128],
                jnp.concatenate([even[:, 128:CH], odd[:, 0:64]], axis=1),
                odd[:, 64:CH],
            )
            for j in range(3):
                value = lanes[j] * factor[j, frame] if weighted else lanes[j]
                wide[slot, pl.ds(2 * j + frame, HALF, stride=6), :] = value

    finish(fwd, 0, False)
    out_ref[...] = wide[0].astype(bf16)
    finish(bwd, 1, True)
    ig_ref[...] = wide[1].astype(bf16)

    to_mate.wait_recv()
    total = folded(3, bases[3]) + incoming[0].astype(f32)
    second_stage[0].wait_recv()
    total = (total + incoming[1].astype(f32)) / scale
    sums[0, 0:TALL, :] = total[0:TALL]
    sums[1, 0:CUT, 0:64] = total[TALL:PIECE, 0:64]
    sums[1, CUT:TALL, 0:64] = total[TALL : 2 * TALL - CUT, 64:128]
    for q in range(4):

        @pl.when(shard(pair) % 4 == q)
        def _():
            even, odd = (pl.ds(4 * q + i, CHUNK // 2, stride=2) for i in range(2))
            low = sums[0, odd, :]
            lanes = (
                sums[0, even, :],
                jnp.concatenate([sums[1, even, :][:, 0:64], low[:, 0:64]], axis=1),
                jnp.concatenate([low[:, 64:128], sums[1, odd, :][:, 0:64]], axis=1),
            )
            for j in range(3):
                wide[0, pl.ds(j, CHUNK // 2, stride=3), :] = lanes[j]

    fg_ref[...] = wide[0, 0 : CHUNK // 2 * 3, :].astype(bf16)

    for copy in straight + onward:
        copy.wait_send()

    @pl.when(has_outer)
    def _():
        outward.wait_send()
        for copy in far:
            copy.wait_send()

    @pl.when(has_inner)
    def _():
        near.wait_send()
        for copy in relayed:
            copy.wait_send()

    @pl.when(inner)
    def _():
        for copy in second_stage:
            copy.wait_send()

    @pl.when(jnp.logical_not(inner))
    def _():
        for copy in first_stage:
            copy.wait_send()

    to_mate.wait_send()


def fused(inputs, weight, cotangent):
    frames, rows = inputs.shape[:2]
    scale = frames * lax.axis_size("tm") * rows * lax.axis_size("row")
    lines = WIDTH * CH // 128
    vmem, hbm = (pl.BlockSpec(memory_space=m) for m in (pltpu.VMEM, pltpu.HBM))
    bf16, f32 = jnp.bfloat16, jnp.float32

    def interleaved(array):
        return array.reshape(2, lines, 128).transpose(1, 0, 2).reshape(2 * lines, 128)

    def parted(array):
        return array.reshape(lines, 2, 128).transpose(1, 0, 2).reshape(2, 1, lines * 128)

    out, ig, fg = pl.pallas_call(
        functools.partial(fused_kernel, float(scale)),
        out_shape=(
            jax.ShapeDtypeStruct((2 * lines, 128), bf16),
            jax.ShapeDtypeStruct((2 * lines, 128), bf16),
            jax.ShapeDtypeStruct((CHUNK // 2 * 3, 128), bf16),
        ),
        in_specs=[hbm, hbm, hbm],
        out_specs=(vmem, vmem, vmem),
        scratch_shapes=[
            pltpu.VMEM((2 * lines, 128), bf16),
            pltpu.VMEM((2 * lines, 128), bf16),
            pltpu.VMEM((CH, TAPS * CH), bf16),
            pltpu.VMEM((2, 2 * lines, 128), f32),
            pltpu.VMEM((3, 2, HALF, 128), f32),
            pltpu.VMEM((4, 3, 6 * HALF, 128), bf16),
            pltpu.VMEM((4, 3, 6 * HALF, 128), bf16),
            pltpu.VMEM((TAPS, CH, 256), bf16),
            pltpu.VMEM((TAPS, CH, 256), bf16),
            pltpu.VMEM((TAPS, CH + 128, CH), bf16),
            pltpu.VMEM((4, CH, 6 * PITCH), bf16),
            pltpu.VMEM((3, 2, 4 * PITCH, CH), bf16),
            pltpu.VMEM((4, 3 * CH, CH), f32),
            pltpu.VMEM((3, PIECE, 128), bf16),
            pltpu.VMEM((2, PIECE, 128), bf16),
            pltpu.VMEM((2, PIECE, 128), bf16),
            pltpu.VMEM((4, 2 * HALF, CH), f32),
            pltpu.VMEM((4, 2 * HALF, CH), f32),
            pltpu.VMEM((2, HALF + 16, CH), f32),
            pltpu.VMEM((2, TALL, 128), f32),
            pltpu.SemaphoreType.DMA((3,)),
            pltpu.SemaphoreType.DMA((12,)),
            pltpu.SemaphoreType.DMA((2, 4, 2)),
            pltpu.SemaphoreType.DMA((3,)),
            pltpu.SemaphoreType.DMA((2,)),
            pltpu.SemaphoreType.DMA((2,)),
        ],
        compiler_params=pltpu.CompilerParams(
            collective_id=0, has_side_effects=True, vmem_limit_bytes=60 * 1024 * 1024
        ),
    )(interleaved(inputs), weight.T, interleaved(cotangent))
    return parted(out), parted(ig), fg.reshape(-1)


def passed_along(array, axis, by):
    length = lax.axis_size(axis)
    pairs = [(i, i + by) for i in range(length) if 0 <= i + by < length]
    return lax.ppermute(array, axis, pairs)


def with_halo(array, sides, width):
    for axis, dim in sides:
        size, length = (lax.axis_size(axis), array.shape[dim])
        up = [(i, (i + 1) % size) for i in range(size - 1)]
        down = [(j, i) for i, j in up]
        last = lax.slice_in_dim(array, length - width, length, axis=dim)
        first = lax.slice_in_dim(array, 0, width, axis=dim)
        before = lax.ppermute(last, axis, up)
        after = lax.ppermute(first, axis, down)
        array = jnp.concatenate([before, array, after], axis=dim)
    return array


def on_device(inputs, weight, cotangent):
    frames = inputs.shape[0]
    rows = inputs.shape[1]
    act = jax.nn.silu(inputs.astype(jnp.float32)).astype(jnp.bfloat16)
    earlier = passed_along(act, "tm", 1)
    extended = jnp.concatenate([earlier, act], 0)
    extended = with_halo(extended, (("row", 1),), 1)
    extended = extended.reshape(frames + 2, rows + 2, WIDTH, CH)
    act_pad = jnp.pad(extended, ((0, 0), (0, 0), (1, 1), (0, 0)))
    cot_four = cotangent.reshape(frames, rows, WIDTH, CH)
    cot_flat = cot_four.reshape(-1, CH)
    output = jnp.zeros((frames * rows * WIDTH, CH), jnp.float32)
    blocks = []
    for step_t in range(3):
        for step_h in range(3):
            for step_w in range(3):
                offset = ((step_t * 3 + step_h) * 3 + step_w) * CH
                kernel = weight[offset : offset + CH]
                piece = act_pad[
                    step_t : step_t + frames, step_h : step_h + rows, step_w : step_w + WIDTH
                ].reshape(-1, CH)
                output = output + jnp.dot(piece, kernel, preferred_element_type=jnp.float32)
                blocks.append(
                    lax.dot_general(
                        piece,
                        cot_flat,
                        (((0,), (0,)), ((), ())),
                        preferred_element_type=jnp.float32,
                    )
                )
    spread = jnp.zeros((frames + 2, rows + 2, WIDTH + 2, CH), jnp.float32)
    for step_t in range(3):
        slab_weight = weight[step_t * 9 * CH : (step_t + 1) * 9 * CH]
        terms = lax.dot_general(
            cot_flat, slab_weight, (((1,), (1,)), ((), ())), preferred_element_type=jnp.float32
        )
        terms = terms.reshape(frames, rows, WIDTH, 9, CH)
        slab = jnp.zeros((frames, rows + 2, WIDTH + 2, CH), jnp.float32)
        for step_h in range(3):
            for step_w in range(3):
                slab = slab + jnp.pad(
                    terms[:, :, :, step_h * 3 + step_w],
                    ((0, 0), (step_h, 2 - step_h), (step_w, 2 - step_w), (0, 0)),
                )
        spread = spread + jnp.pad(slab, ((step_t, 2 - step_t), (0, 0), (0, 0), (0, 0)))
    inner = spread[:, :, 1 : WIDTH + 1]
    from_next = passed_along(inner[:, 0:1], "row", -1)
    from_prev = passed_along(inner[:, rows + 1 : rows + 2], "row", 1)
    center = inner[:, 1 : rows + 1]
    center = center.at[:, rows - 1 : rows].add(from_next)
    center = center.at[:, 0:1].add(from_prev)
    returned = passed_along(center[0:2], "tm", -1)
    grad_act = center[2:].at[frames - 2 :].add(returned).reshape(-1, CH)
    x_float = inputs.reshape(-1, CH).astype(jnp.float32)
    sigma = jax.nn.sigmoid(x_float)
    input_grad = (grad_act * sigma * (1.0 + x_float * (1.0 - sigma))).astype(jnp.bfloat16)
    local_filter = jnp.concatenate(blocks, 0).reshape(-1)
    frame_blocks = lax.axis_size("tm")
    row_blocks = lax.axis_size("row")
    scale = frames * frame_blocks * rows * row_blocks
    share = lax.psum_scatter(local_filter, ("tm", "row"), scatter_dimension=0, tiled=True)
    filter_grad = (share / scale).astype(jnp.bfloat16)
    shape = (frames, rows, WIDTH * CH)
    return (output.astype(jnp.bfloat16).reshape(shape), input_grad.reshape(shape), filter_grad)


def either(mesh, inputs, weight, cotangent):
    size = mesh.shape["row"]
    if mesh.shape["tm"] == 2 and size == 2 * PAIRS and inputs.shape[:2] == (2, 1):
        return fused(inputs, weight, cotangent)
    return on_device(inputs, weight, cotangent)


def solution(mesh):
    placed = (P(("grp", "tm"), "row", None), P(), P(("grp", "tm"), "row", None))
    return jax.shard_map(
        functools.partial(either, mesh),
        mesh=mesh,
        in_specs=placed,
        out_specs=(
            P(("grp", "tm"), "row", None),
            P(("grp", "tm"), "row", None),
            P(("grp", "tm", "row")),
        ),
        check_vma=False,
    )
```

```python
import functools

import jax
import jax.numpy as jnp
from jax import lax
from jax.experimental import pallas as pl
from jax.experimental.pallas import tpu as pltpu
from jax.sharding import PartitionSpec as P

CH = 192
WIDTH = 224
TAPS = 27
HALF = WIDTH // 2
PAIRS = 4
CHUNK = TAPS * CH // (4 * PAIRS)
TALL = CHUNK + 12
CUT = 176
PIECE = TALL + CUT
PITCH = 256


def fused_kernel(
    scale, x_ref, w_ref, c_ref, out_ref, ig_ref, fg_ref,
    x_in, c_in, weight_in, wide, factor, act, cot, fwd_even, fwd_odd, bwd_taps, act_t, shifted, filt,
    outgoing, passing, incoming, fwd, bwd, pad, sums,
    fetch_sem, send_sem, recv_sem, piece_send, pass_recv, piece_recv,
):
    f32, bf16 = jnp.float32, jnp.bfloat16
    grp, tm, row = lax.axis_index("grp"), lax.axis_index("tm"), lax.axis_index("row")
    pair, side = row // 2, row % 2
    own, other_slot = 1 + side, 2 - side

    def device(t, r):
        return (grp, t, r)

    barrier = pltpu.get_barrier_semaphore()

    def greet(target):
        pl.semaphore_signal(barrier, inc=1, device_id=target, device_id_type=pl.DeviceIdType.MESH)

    fetches = [
        pltpu.make_async_copy(src, dst, fetch_sem.at[i])
        for i, (src, dst) in enumerate(((x_ref, x_in), (c_ref, c_in), (w_ref, weight_in)))
    ]
    for fetch in fetches:
        fetch.start()

    sibling = device(1 - tm, row)
    partner = device(tm, 2 * pair + 1 - side)
    greet(sibling)
    greet(partner)
    for step in range(1, PAIRS):
        greet(device(tm, 2 * ((pair + step) % PAIRS) + side))

    def block(index):
        return pl.ds(pl.multiple_of(index * HALF, 16), HALF)

    def move(array, src_slot, dst_slot, half, lane, target):
        ref = cot if array else act
        span = pl.ds(pl.multiple_of((2 * half + 2 * (1 - array)) * HALF, 16), 2 * HALF)
        return pltpu.make_async_remote_copy(
            src_ref=ref.at[src_slot, :, span],
            dst_ref=ref.at[dst_slot, :, span],
            send_sem=send_sem.at[lane],
            recv_sem=recv_sem.at[array, dst_slot, half],
            device_id=target,
            device_id_type=pl.DeviceIdType.MESH,
        )

    def arrived(array, slot, half):
        move(array, slot, slot, half, 0, sibling).wait_recv()

    outer_pair = pair + 2 * side - 1
    inner_pair = pair + 1 - 2 * side
    has_outer = jnp.logical_and(outer_pair >= 0, outer_pair < PAIRS)
    has_inner = jnp.logical_and(inner_pair >= 0, inner_pair < PAIRS)
    outer_same = device(tm, 2 * outer_pair + side)
    inner_same = device(tm, 2 * inner_pair + side)
    near_slot, far_slot = 3 * (1 - side), 3 * side
    has_before, has_after = pair > 0, pair < PAIRS - 1

    straight = [
        move(0, own, own, tm, 0, partner),
        move(0, own, own, tm, 1, sibling),
        move(1, own, own, tm, 2, partner),
        move(1, own, own, tm, 3, sibling),
    ]
    outward = move(0, own, near_slot, tm, 4, outer_same)
    relayed = [move(i, other_slot, far_slot, tm, 5 + i, inner_same) for i in range(2)]
    onward = [move(i, other_slot, other_slot, tm, 7 + i, sibling) for i in range(2)]
    near = move(0, near_slot, near_slot, tm, 9, sibling)
    far = [move(i, far_slot, far_slot, tm, 10 + i, sibling) for i in range(2)]

    fetches[0].wait()
    wide[0] = x_in[...].astype(f32)
    for j in range(3):
        for frame in range(2):
            x = wide[0, pl.ds(2 * j + frame, HALF, stride=6), :]
            sigma = 1.0 / (1.0 + jnp.exp(-x))
            act[own, j, block(2 * tm + 2 + frame), :] = (x * sigma).astype(bf16)
            factor[j, frame] = sigma * (1.0 + x * (1.0 - sigma))
    fetches[1].wait()
    wide[1] = c_in[...].astype(f32)
    for j in range(3):
        for frame in range(2):
            value = wide[1, pl.ds(2 * j + frame, HALF, stride=6), :]
            cot[own, j, block(2 * tm + frame), :] = value.astype(bf16)

    pl.semaphore_wait(barrier, PAIRS + 1)
    straight[0].start()
    straight[1].start()

    @pl.when(has_outer)
    def _():
        outward.start()

    straight[2].start()
    straight[3].start()

    for slot in range(4):
        act[slot, :, 0 : 2 * HALF, :] = jnp.zeros((3, 2 * HALF, 128), bf16)
        cot[slot, :, 4 * HALF : 6 * HALF, :] = jnp.zeros((3, 2 * HALF, 128), bf16)
        act_t[slot, :, 0 : 2 * PITCH] = jnp.zeros((CH, 2 * PITCH), bf16)

    for slot, present in ((0, has_before), (3, has_after)):

        @pl.when(jnp.logical_not(present))
        def _():
            act[slot, :, 2 * HALF : 6 * HALF, :] = jnp.zeros((3, 4 * HALF, 128), bf16)
            cot[slot, :, 0 : 4 * HALF, :] = jnp.zeros((3, 4 * HALF, 128), bf16)
            act_t[slot, :, 2 * PITCH : 6 * PITCH] = jnp.zeros((CH, 4 * PITCH), bf16)

    pad[:, 0:8, :] = jnp.zeros((2, 8, CH), f32)
    pad[:, HALF + 8 : HALF + 16, :] = jnp.zeros((2, 8, CH), f32)
    for part in range(8):
        shifted[:, :, part * 128 + HALF : (part + 1) * 128, :] = jnp.zeros(
            (3, 2, 128 - HALF, CH), bf16
        )
    bwd_taps[:, 0:64, :] = jnp.zeros((TAPS, 64, CH), bf16)
    bwd_taps[:, 64 + CH : 128 + CH, :] = jnp.zeros((TAPS, 64, CH), bf16)

    fetches[2].wait()
    for tap in range(TAPS):
        value = weight_in[:, tap * CH : (tap + 1) * CH]
        fwd_even[tap] = jnp.concatenate([value, jnp.zeros((CH, 64), bf16)], axis=1)
        fwd_odd[tap] = jnp.concatenate([jnp.zeros((CH, 64), bf16), value], axis=1)
        bwd_taps[tap, 64 : 64 + CH, :] = value

    def transpose(slot, half):
        for frame in range(2):
            lane = (2 * half + 2 + frame) * PITCH
            even = pl.ds(pl.multiple_of(lane, 128), 128)
            odd = pl.ds(pl.multiple_of(lane + 128, 128), 128)

            def turned(j):
                value = act[slot, j, block(2 * half + 2 + frame), :]
                return jnp.concatenate([value, jnp.zeros((128 - HALF, 128), bf16)], axis=0).T

            act_t[slot, 0:128, even] = turned(0)
            both = turned(1)
            act_t[slot, 128:CH, even] = both[0:64]
            act_t[slot, 0:64, odd] = both[64:128]
            act_t[slot, 64:CH, odd] = turned(2)

    transpose(own, tm)

    def dots(ref, slot, starts, weights, out, first):
        def side_of(start, j):
            rows_of = pl.ds(pl.multiple_of(start, 16), 2 * HALF)
            return jnp.concatenate([ref[slot, j, rows_of, :], ref[slot, j + 1, rows_of, :]], axis=1)

        for i, terms in enumerate((((0, 1), (1, 2)), ((1, 1), (0, 0)), ((0, 2),), ((1, 0),))):
            total = None
            for step_t in range(3):
                for odd, step_w in terms:
                    more = weights(side_of(starts[step_t], odd), odd, step_t, step_w)
                    total = more if total is None else total + more
            if first:
                out[i] = total
            else:
                out[i] += total

    def convolve(act_h, cot_h, first):
        def forward(value, odd, step_t, step_w):
            taps = fwd_odd if odd else fwd_even
            return lax.dot_general(
                value,
                taps[(step_t * 3 + act_h) * 3 + step_w],
                (((1,), (1,)), ((), ())),
                preferred_element_type=f32,
            )

        def backward(value, odd, step_t, step_w):
            first_row = 0 if odd else 64
            return jnp.dot(
                value,
                bwd_taps[(step_t * 3 + cot_h) * 3 + 2 - step_w, first_row : first_row + 256, :],
                preferred_element_type=f32,
            )

        starts = [(2 * tm + step_t) * HALF for step_t in range(3)]
        dots(act, side + act_h, starts, forward, fwd, first)
        dots(cot, side + 2 - cot_h, starts[::-1], backward, bwd, first)

    def shift(h):
        for frame in range(4):
            rows_of = slice(frame * HALF, (frame + 1) * HALF)
            mid = cot[1 + h, 1, rows_of, :]
            even = jnp.concatenate([cot[1 + h, 0, rows_of, :], mid[:, 0:64]], axis=1)
            odd = jnp.concatenate([mid[:, 64:128], cot[1 + h, 2, rows_of, :]], axis=1)
            pad[0, 8 : HALF + 8, :] = even.astype(f32)
            pad[1, 8 : HALF + 8, :] = odd.astype(f32)
            at = frame * PITCH
            shifted[0, h, at : at + HALF, :] = odd
            shifted[0, h, at + 128 : at + 128 + HALF, :] = pad[0, 9 : HALF + 9, :].astype(bf16)
            shifted[1, h, at : at + HALF, :] = even
            shifted[1, h, at + 128 : at + 128 + HALF, :] = odd
            shifted[2, h, at : at + HALF, :] = pad[1, 7 : HALF + 7, :].astype(bf16)
            shifted[2, h, at + 128 : at + 128 + HALF, :] = even

    arrived(0, own, 1 - tm)
    arrived(1, own, 1 - tm)
    convolve(1, 1, True)
    transpose(own, 1 - tm)
    shift(side)

    arrived(0, other_slot, tm)
    onward[0].start()

    @pl.when(has_inner)
    def _():
        relayed[0].start()

    transpose(other_slot, tm)

    @pl.when(has_inner)
    def _():
        arrived(0, near_slot, tm)
        near.start()
        transpose(near_slot, tm)
        arrived(0, near_slot, 1 - tm)
        transpose(near_slot, 1 - tm)

    arrived(0, other_slot, 1 - tm)
    transpose(other_slot, 1 - tm)
    arrived(1, other_slot, tm)
    onward[1].start()

    @pl.when(has_inner)
    def _():
        relayed[1].start()

    arrived(1, other_slot, 1 - tm)
    shift(1 - side)

    @pl.when(has_outer)
    def _():
        arrived(0, far_slot, tm)
        far[0].start()
        transpose(far_slot, tm)
        arrived(0, far_slot, 1 - tm)
        transpose(far_slot, 1 - tm)

    part = pair // 2
    inner = (pair + part) % 2 == 1
    mate_pair = pair + 1 - 2 * (pair % 2)
    owners = (3 * (1 - part), 2 - part, mate_pair, pair)

    def shard(owner):
        return tm * 2 * PAIRS + 2 * owner + side

    def filter_sum(k):
        first_block = shard(owners[k]) * CHUNK // 16
        first_tap = first_block // (CH // 16)
        base = pl.multiple_of(first_block % (CH // 16) * 16, 16)

        def term(n):
            tap = first_tap + n
            step_t, step_h, step_w = tap // 9, tap // 3 % 3, tap % 3
            lanes = pl.ds(pl.multiple_of(step_t * PITCH, 128), 4 * PITCH)
            filt[k, n * CH : (n + 1) * CH, :] = jnp.dot(
                act_t[step_h, :, lanes], shifted[step_w, 0], preferred_element_type=f32
            ) + jnp.dot(act_t[step_h + 1, :, lanes], shifted[step_w, 1], preferred_element_type=f32)

        term(0)
        term(1)

        @pl.when(base + TALL > 2 * CH)
        def _():
            term(2)

        return base

    def folded(k, base):
        high = filt[k, pl.ds(base, TALL), 128:CH]
        return jnp.concatenate(
            [
                filt[k, pl.ds(base, TALL), 0:128],
                jnp.concatenate(
                    [
                        high[0:CUT],
                        jnp.concatenate([high[CUT:TALL], jnp.zeros((2 * CUT - TALL, 64), f32)], axis=0),
                    ],
                    axis=1,
                ),
            ],
            axis=0,
        )

    def piece(k, ref, slot, recv, owner):
        return pltpu.make_async_remote_copy(
            src_ref=outgoing.at[k],
            dst_ref=ref.at[slot],
            send_sem=piece_send.at[k],
            recv_sem=recv.at[slot],
            device_id=device(tm, 2 * owner + side),
            device_id_type=pl.DeviceIdType.MESH,
        )

    first_stage = [piece(k, passing, k, pass_recv, mate_pair) for k in range(2)]
    second_stage = [piece(k, incoming, 1, piece_recv, owners[k]) for k in range(2)]
    to_mate = piece(2, incoming, 0, piece_recv, mate_pair)
    bases = []
    for k in range(4):
        base = filter_sum(k)
        bases.append(base)
        if k < 2:

            @pl.when(jnp.logical_not(inner))
            def _():
                outgoing[k] = folded(k, base).astype(bf16)
                first_stage[k].start()

        elif k == 2:
            outgoing[k] = folded(k, base).astype(bf16)
            to_mate.start()

    convolve(2 - 2 * side, 2 * side, False)

    @pl.when(has_outer)
    def _():
        arrived(1, far_slot, tm)
        far[1].start()

    def second(k):
        @pl.when(inner)
        def _():
            first_stage[k].wait_recv()
            outgoing[k] = (folded(k, bases[k]) + passing[k].astype(f32)).astype(bf16)
            second_stage[k].start()

    second(0)

    @pl.when(has_outer)
    def _():
        arrived(1, far_slot, 1 - tm)

    convolve(2 * side, 2 - 2 * side, False)
    second(1)

    def finish(total, slot, weighted):
        for frame in range(2):
            span = slice(frame * HALF, (frame + 1) * HALF)
            pad[0, 8 : HALF + 8, :] = total[3, span, :]
            pad[1, 8 : HALF + 8, :] = total[2, span, :]
            even = total[0, span, :] + pad[0, 7 : HALF + 7, :]
            odd = total[1, span, :] + pad[1, 9 : HALF + 9, :]
            lanes = (
                even[:, 0:128],
                jnp.concatenate([even[:, 128:CH], odd[:, 0:64]], axis=1),
                odd[:, 64:CH],
            )
            for j in range(3):
                value = lanes[j] * factor[j, frame] if weighted else lanes[j]
                wide[slot, pl.ds(2 * j + frame, HALF, stride=6), :] = value

    finish(fwd, 0, False)
    out_ref[...] = wide[0].astype(bf16)
    finish(bwd, 1, True)
    ig_ref[...] = wide[1].astype(bf16)

    to_mate.wait_recv()
    total = folded(3, bases[3]) + incoming[0].astype(f32)
    second_stage[0].wait_recv()
    total = (total + incoming[1].astype(f32)) / scale
    sums[0, 0:TALL, :] = total[0:TALL]
    sums[1, 0:CUT, 0:64] = total[TALL:PIECE, 0:64]
    sums[1, CUT:TALL, 0:64] = total[TALL : 2 * TALL - CUT, 64:128]
    for q in range(4):

        @pl.when(shard(pair) % 4 == q)
        def _():
            even, odd = (pl.ds(4 * q + i, CHUNK // 2, stride=2) for i in range(2))
            low = sums[0, odd, :]
            lanes = (
                sums[0, even, :],
                jnp.concatenate([sums[1, even, :][:, 0:64], low[:, 0:64]], axis=1),
                jnp.concatenate([low[:, 64:128], sums[1, odd, :][:, 0:64]], axis=1),
            )
            for j in range(3):
                wide[0, pl.ds(j, CHUNK // 2, stride=3), :] = lanes[j]

    fg_ref[...] = wide[0, 0 : CHUNK // 2 * 3, :].astype(bf16)

    for copy in straight + onward:
        copy.wait_send()

    @pl.when(has_outer)
    def _():
        outward.wait_send()
        for copy in far:
            copy.wait_send()

    @pl.when(has_inner)
    def _():
        near.wait_send()
        for copy in relayed:
            copy.wait_send()

    @pl.when(inner)
    def _():
        for copy in second_stage:
            copy.wait_send()

    @pl.when(jnp.logical_not(inner))
    def _():
        for copy in first_stage:
            copy.wait_send()

    to_mate.wait_send()


def hand_over(*refs):
    copies = [
        pltpu.make_async_copy(refs[i], refs[3 + i], refs[6].at[i]) for i in range(3)
    ]
    for copy in copies:
        copy.start()
    for copy in copies:
        copy.wait()


def fused(inputs, weight, cotangent):
    frames, rows = inputs.shape[:2]
    scale = frames * lax.axis_size("tm") * rows * lax.axis_size("row")
    lines = WIDTH * CH // 128
    vmem, hbm = (pl.BlockSpec(memory_space=m) for m in (pltpu.VMEM, pltpu.HBM))
    bf16, f32 = jnp.bfloat16, jnp.float32

    def interleaved(array):
        return array.reshape(2, lines, 128).transpose(1, 0, 2).reshape(2 * lines, 128)

    def parted(array):
        return array.reshape(lines, 2, 128).transpose(1, 0, 2).reshape(2, 1, lines * 128)

    out, ig, fg = pl.pallas_call(
        functools.partial(fused_kernel, float(scale)),
        out_shape=(
            jax.ShapeDtypeStruct((2 * lines, 128), bf16),
            jax.ShapeDtypeStruct((2 * lines, 128), bf16),
            jax.ShapeDtypeStruct((CHUNK // 2 * 3, 128), bf16),
        ),
        in_specs=[hbm, hbm, hbm],
        out_specs=(vmem, vmem, vmem),
        scratch_shapes=[
            pltpu.VMEM((2 * lines, 128), bf16),
            pltpu.VMEM((2 * lines, 128), bf16),
            pltpu.VMEM((CH, TAPS * CH), bf16),
            pltpu.VMEM((2, 2 * lines, 128), f32),
            pltpu.VMEM((3, 2, HALF, 128), f32),
            pltpu.VMEM((4, 3, 6 * HALF, 128), bf16),
            pltpu.VMEM((4, 3, 6 * HALF, 128), bf16),
            pltpu.VMEM((TAPS, CH, 256), bf16),
            pltpu.VMEM((TAPS, CH, 256), bf16),
            pltpu.VMEM((TAPS, CH + 128, CH), bf16),
            pltpu.VMEM((4, CH, 6 * PITCH), bf16),
            pltpu.VMEM((3, 2, 4 * PITCH, CH), bf16),
            pltpu.VMEM((4, 3 * CH, CH), f32),
            pltpu.VMEM((3, PIECE, 128), bf16),
            pltpu.VMEM((2, PIECE, 128), bf16),
            pltpu.VMEM((2, PIECE, 128), bf16),
            pltpu.VMEM((4, 2 * HALF, CH), f32),
            pltpu.VMEM((4, 2 * HALF, CH), f32),
            pltpu.VMEM((2, HALF + 16, CH), f32),
            pltpu.VMEM((2, TALL, 128), f32),
            pltpu.SemaphoreType.DMA((3,)),
            pltpu.SemaphoreType.DMA((12,)),
            pltpu.SemaphoreType.DMA((2, 4, 2)),
            pltpu.SemaphoreType.DMA((3,)),
            pltpu.SemaphoreType.DMA((2,)),
            pltpu.SemaphoreType.DMA((2,)),
        ],
        compiler_params=pltpu.CompilerParams(
            collective_id=0, has_side_effects=True, vmem_limit_bytes=int(53.4 * 1024 * 1024)
        ),
    )(interleaved(inputs), weight.T, interleaved(cotangent))
    results = (out, ig, fg)
    out, ig, fg = pl.pallas_call(
        hand_over,
        out_shape=tuple(jax.ShapeDtypeStruct(r.shape, r.dtype) for r in results),
        in_specs=[pl.BlockSpec(memory_space=pl.ANY)] * 3,
        out_specs=(hbm, hbm, hbm),
        scratch_shapes=[pltpu.SemaphoreType.DMA((3,))],
        compiler_params=pltpu.CompilerParams(vmem_limit_bytes=1024 * 1024),
    )(*results)
    return parted(out), parted(ig), fg.reshape(-1)


def passed_along(array, axis, by):
    length = lax.axis_size(axis)
    pairs = [(i, i + by) for i in range(length) if 0 <= i + by < length]
    return lax.ppermute(array, axis, pairs)


def with_halo(array, sides, width):
    for axis, dim in sides:
        size, length = (lax.axis_size(axis), array.shape[dim])
        up = [(i, (i + 1) % size) for i in range(size - 1)]
        down = [(j, i) for i, j in up]
        last = lax.slice_in_dim(array, length - width, length, axis=dim)
        first = lax.slice_in_dim(array, 0, width, axis=dim)
        before = lax.ppermute(last, axis, up)
        after = lax.ppermute(first, axis, down)
        array = jnp.concatenate([before, array, after], axis=dim)
    return array


def on_device(inputs, weight, cotangent):
    frames = inputs.shape[0]
    rows = inputs.shape[1]
    act = jax.nn.silu(inputs.astype(jnp.float32)).astype(jnp.bfloat16)
    earlier = passed_along(act, "tm", 1)
    extended = jnp.concatenate([earlier, act], 0)
    extended = with_halo(extended, (("row", 1),), 1)
    extended = extended.reshape(frames + 2, rows + 2, WIDTH, CH)
    act_pad = jnp.pad(extended, ((0, 0), (0, 0), (1, 1), (0, 0)))
    cot_four = cotangent.reshape(frames, rows, WIDTH, CH)
    cot_flat = cot_four.reshape(-1, CH)
    output = jnp.zeros((frames * rows * WIDTH, CH), jnp.float32)
    blocks = []
    for step_t in range(3):
        for step_h in range(3):
            for step_w in range(3):
                offset = ((step_t * 3 + step_h) * 3 + step_w) * CH
                kernel = weight[offset : offset + CH]
                piece = act_pad[
                    step_t : step_t + frames, step_h : step_h + rows, step_w : step_w + WIDTH
                ].reshape(-1, CH)
                output = output + jnp.dot(piece, kernel, preferred_element_type=jnp.float32)
                blocks.append(
                    lax.dot_general(
                        piece,
                        cot_flat,
                        (((0,), (0,)), ((), ())),
                        preferred_element_type=jnp.float32,
                    )
                )
    spread = jnp.zeros((frames + 2, rows + 2, WIDTH + 2, CH), jnp.float32)
    for step_t in range(3):
        slab_weight = weight[step_t * 9 * CH : (step_t + 1) * 9 * CH]
        terms = lax.dot_general(
            cot_flat, slab_weight, (((1,), (1,)), ((), ())), preferred_element_type=jnp.float32
        )
        terms = terms.reshape(frames, rows, WIDTH, 9, CH)
        slab = jnp.zeros((frames, rows + 2, WIDTH + 2, CH), jnp.float32)
        for step_h in range(3):
            for step_w in range(3):
                slab = slab + jnp.pad(
                    terms[:, :, :, step_h * 3 + step_w],
                    ((0, 0), (step_h, 2 - step_h), (step_w, 2 - step_w), (0, 0)),
                )
        spread = spread + jnp.pad(slab, ((step_t, 2 - step_t), (0, 0), (0, 0), (0, 0)))
    inner = spread[:, :, 1 : WIDTH + 1]
    from_next = passed_along(inner[:, 0:1], "row", -1)
    from_prev = passed_along(inner[:, rows + 1 : rows + 2], "row", 1)
    center = inner[:, 1 : rows + 1]
    center = center.at[:, rows - 1 : rows].add(from_next)
    center = center.at[:, 0:1].add(from_prev)
    returned = passed_along(center[0:2], "tm", -1)
    grad_act = center[2:].at[frames - 2 :].add(returned).reshape(-1, CH)
    x_float = inputs.reshape(-1, CH).astype(jnp.float32)
    sigma = jax.nn.sigmoid(x_float)
    input_grad = (grad_act * sigma * (1.0 + x_float * (1.0 - sigma))).astype(jnp.bfloat16)
    local_filter = jnp.concatenate(blocks, 0).reshape(-1)
    frame_blocks = lax.axis_size("tm")
    row_blocks = lax.axis_size("row")
    scale = frames * frame_blocks * rows * row_blocks
    share = lax.psum_scatter(local_filter, ("tm", "row"), scatter_dimension=0, tiled=True)
    filter_grad = (share / scale).astype(jnp.bfloat16)
    shape = (frames, rows, WIDTH * CH)
    return (output.astype(jnp.bfloat16).reshape(shape), input_grad.reshape(shape), filter_grad)


def either(mesh, inputs, weight, cotangent):
    size = mesh.shape["row"]
    if mesh.shape["tm"] == 2 and size == 2 * PAIRS and inputs.shape[:2] == (2, 1):
        return fused(inputs, weight, cotangent)
    return on_device(inputs, weight, cotangent)


def solution(mesh):
    placed = (P(("grp", "tm"), "row", None), P(), P(("grp", "tm"), "row", None))
    return jax.shard_map(
        functools.partial(either, mesh),
        mesh=mesh,
        in_specs=placed,
        out_specs=(
            P(("grp", "tm"), "row", None),
            P(("grp", "tm"), "row", None),
            P(("grp", "tm", "row")),
        ),
        check_vma=False,
    )
```

```python
import functools

import jax
import jax.numpy as jnp
from jax import lax
from jax.experimental import pallas as pl
from jax.experimental.pallas import tpu as pltpu
from jax.sharding import PartitionSpec as P

CH = 192
WIDTH = 224
TAPS = 27
HALF = WIDTH // 2
LINES = WIDTH * CH // 128
PAIRS = 4
CHUNK = TAPS * CH // (4 * PAIRS)
TALL = CHUNK + 12
CUT = 176
PIECE = TALL + CUT
PITCH = 256


def fused_kernel(
    scale, x_ref, w_ref, c_ref, out_ref, ig_ref, fg_ref,
    raw, weight_in, wide, factor, act, cot, fwd_even, fwd_odd, bwd_taps, act_t, shifted, filt,
    outgoing, passing, incoming, fwd, bwd, pad, sums,
    known, fetch_sem, send_sem, recv_sem, piece_send, pass_recv, piece_recv,
):
    f32, bf16 = jnp.float32, jnp.bfloat16
    grp, tm, row = lax.axis_index("grp"), lax.axis_index("tm"), lax.axis_index("row")
    pair, side = row // 2, row % 2
    own, other_slot = 1 + side, 2 - side

    def device(t, r):
        return (grp, t, r)

    barrier = pltpu.get_barrier_semaphore()

    def greet(target):
        pl.semaphore_signal(barrier, inc=1, device_id=target, device_id_type=pl.DeviceIdType.MESH)

    fetches = [
        pltpu.make_async_copy(src, dst, fetch_sem.at[i])
        for i, (src, dst) in enumerate(
            ((x_ref, raw.at[0, own, tm]), (c_ref, raw.at[1, own, tm]), (w_ref, weight_in))
        )
    ]
    sibling = device(1 - tm, row)
    partner = device(tm, 2 * pair + 1 - side)
    greet(sibling)
    greet(partner)
    has_before, has_after = pair > 0, pair < PAIRS - 1
    part = pair // 2
    inner = (pair + part) % 2 == 1
    mate_pair = pair + 1 - 2 * (pair % 2)
    stop, end = 2 - part, 3 * (1 - part)
    for step, present in ((-1, has_before), (1, has_after)):

        @pl.when(present)
        def _():
            greet(device(tm, 2 * (pair + step) + side))

    for fetch in fetches:
        fetch.start()

    def block(index):
        return pl.ds(pl.multiple_of(index * HALF, 16), HALF)

    lanes_used = iter(range(28))

    def move(array, src_slot, dst_slot, half, target):
        copies = []
        for k in range(2):
            span = pl.ds(k * LINES, LINES)
            src = (c_ref if array else x_ref) if src_slot is None else raw.at[array, src_slot, half]
            copies.append(
                pltpu.make_async_remote_copy(
                    src_ref=src.at[span],
                    dst_ref=raw.at[array, dst_slot, half, span],
                    send_sem=send_sem.at[next(lanes_used)],
                    recv_sem=recv_sem.at[array, dst_slot, half, k],
                    device_id=target,
                    device_id_type=pl.DeviceIdType.MESH,
                )
            )
        return copies

    def arrived(array, slot, half, k):
        ref = raw.at[array, slot, half, pl.ds(k * LINES, LINES)]
        pltpu.make_async_remote_copy(
            src_ref=ref,
            dst_ref=ref,
            send_sem=send_sem.at[0],
            recv_sem=recv_sem.at[array, slot, half, k],
            device_id=sibling,
            device_id_type=pl.DeviceIdType.MESH,
        ).wait_recv()

    outer_pair = pair + 2 * side - 1
    inner_pair = pair + 1 - 2 * side
    has_outer = jnp.logical_and(outer_pair >= 0, outer_pair < PAIRS)
    has_inner = jnp.logical_and(inner_pair >= 0, inner_pair < PAIRS)
    outer_same = device(tm, 2 * outer_pair + side)
    inner_same = device(tm, 2 * inner_pair + side)
    near_slot, far_slot = 3 * (1 - side), 3 * side

    to_partner = [move(i, None, own, tm, partner) for i in range(2)]
    to_sibling = [move(i, None, own, tm, sibling) for i in range(2)]
    outward = [move(i, None, near_slot, tm, outer_same) for i in range(2)]
    onward = [move(i, other_slot, other_slot, tm, sibling) for i in range(2)]
    relayed = move(0, other_slot, far_slot, tm, inner_same)
    across = move(1, near_slot, near_slot, tm, partner)
    near = move(0, near_slot, near_slot, tm, sibling)
    far = [move(i, far_slot, far_slot, tm, sibling) for i in range(2)]

    def expand(array, slot, half, keep=False):
        wide[array] = raw[array, slot, half].astype(f32)
        for j in range(3):
            for frame in range(2):
                value = wide[array, pl.ds(2 * j + frame, HALF, stride=6), :]
                if array == 0:
                    sigma = 1.0 / (1.0 + jnp.exp(-value))
                    if keep:
                        factor[j, frame] = sigma * (1.0 + value * (1.0 - sigma))
                    act[slot, j, block(2 * half + 2 + frame), :] = (value * sigma).astype(bf16)
                else:
                    cot[slot, j, block(2 * half + frame), :] = value.astype(bf16)

    def announce(target):
        pl.semaphore_signal(
            known, inc=1, device_id=device(tm, 2 * target + side), device_id_type=pl.DeviceIdType.MESH
        )

    pl.semaphore_wait(barrier, jnp.where(inner, 4, 3))

    @pl.when(inner)
    def _():
        announce(stop)

    for i in range(2):
        for k in range(2):
            to_partner[i][k].start()

        @pl.when(has_outer)
        def _():
            for k in range(2):
                outward[i][k].start()

        for k in range(2):
            to_sibling[i][k].start()

    for i in range(2):
        fetches[i].wait()
        expand(i, own, tm, keep=i == 0)

    for slot in range(4):
        act[slot, :, 0 : 2 * HALF, :] = jnp.zeros((3, 2 * HALF, 128), bf16)
        cot[slot, :, 4 * HALF : 6 * HALF, :] = jnp.zeros((3, 2 * HALF, 128), bf16)
        act_t[slot, :, 0 : 2 * PITCH] = jnp.zeros((CH, 2 * PITCH), bf16)

    for slot, present in ((0, has_before), (3, has_after)):

        @pl.when(jnp.logical_not(present))
        def _():
            act[slot, :, 2 * HALF : 6 * HALF, :] = jnp.zeros((3, 4 * HALF, 128), bf16)
            cot[slot, :, 0 : 4 * HALF, :] = jnp.zeros((3, 4 * HALF, 128), bf16)
            act_t[slot, :, 2 * PITCH : 6 * PITCH] = jnp.zeros((CH, 4 * PITCH), bf16)


    @pl.when(inner)
    def _():
        incoming[1:3] = jnp.zeros((2, PIECE, 128), bf16)

    @pl.when(jnp.logical_not(inner))
    def _():
        incoming[3] = jnp.zeros((PIECE, 128), bf16)

    pad[:, 0:8, :] = jnp.zeros((2, 8, CH), f32)
    pad[:, HALF + 8 : HALF + 16, :] = jnp.zeros((2, 8, CH), f32)
    for i in range(8):
        shifted[:, :, i * 128 + HALF : (i + 1) * 128, :] = jnp.zeros(
            (3, 2, 128 - HALF, CH), bf16
        )
    bwd_taps[:, 0:64, :] = jnp.zeros((TAPS, 64, CH), bf16)
    bwd_taps[:, 64 + CH : 128 + CH, :] = jnp.zeros((TAPS, 64, CH), bf16)

    fetches[2].wait()
    for tap in range(TAPS):
        value = weight_in[:, tap * CH : (tap + 1) * CH]
        fwd_even[tap] = jnp.concatenate([value, jnp.zeros((CH, 64), bf16)], axis=1)
        fwd_odd[tap] = jnp.concatenate([jnp.zeros((CH, 64), bf16), value], axis=1)
        bwd_taps[tap, 64 : 64 + CH, :] = value

    def transpose(slot, half):
        for frame in range(2):
            lane = (2 * half + 2 + frame) * PITCH
            even = pl.ds(pl.multiple_of(lane, 128), 128)
            odd = pl.ds(pl.multiple_of(lane + 128, 128), 128)

            def turned(j):
                value = act[slot, j, block(2 * half + 2 + frame), :]
                return jnp.concatenate([value, jnp.zeros((128 - HALF, 128), bf16)], axis=0).T

            act_t[slot, 0:128, even] = turned(0)
            both = turned(1)
            act_t[slot, 128:CH, even] = both[0:64]
            act_t[slot, 0:64, odd] = both[64:128]
            act_t[slot, 64:CH, odd] = turned(2)

    transpose(own, tm)

    def dots(ref, slot, starts, weights, out, first):
        def side_of(start, j):
            rows_of = pl.ds(pl.multiple_of(start, 16), 2 * HALF)
            return jnp.concatenate([ref[slot, j, rows_of, :], ref[slot, j + 1, rows_of, :]], axis=1)

        for i, terms in enumerate((((0, 1), (1, 2)), ((1, 1), (0, 0)), ((0, 2),), ((1, 0),))):
            total = None
            for step_t in range(3):
                for odd, step_w in terms:
                    more = weights(side_of(starts[step_t], odd), odd, step_t, step_w)
                    total = more if total is None else total + more
            if first:
                out[i] = total
            else:
                out[i] += total

    def convolve(act_h, cot_h, first):
        def forward(value, odd, step_t, step_w):
            taps = fwd_odd if odd else fwd_even
            return lax.dot_general(
                value,
                taps[(step_t * 3 + act_h) * 3 + step_w],
                (((1,), (1,)), ((), ())),
                preferred_element_type=f32,
            )

        def backward(value, odd, step_t, step_w):
            first_row = 0 if odd else 64
            return jnp.dot(
                value,
                bwd_taps[(step_t * 3 + cot_h) * 3 + 2 - step_w, first_row : first_row + 256, :],
                preferred_element_type=f32,
            )

        starts = [(2 * tm + step_t) * HALF for step_t in range(3)]
        dots(act, side + act_h, starts, forward, fwd, first)
        dots(cot, side + 2 - cot_h, starts[::-1], backward, bwd, first)

    def shift(h, half):
        for frame in range(2):
            rows_of = block(2 * half + frame)
            mid = cot[1 + h, 1, rows_of, :]
            even = jnp.concatenate([cot[1 + h, 0, rows_of, :], mid[:, 0:64]], axis=1)
            odd = jnp.concatenate([mid[:, 64:128], cot[1 + h, 2, rows_of, :]], axis=1)
            pad[0, 8 : HALF + 8, :] = even.astype(f32)
            pad[1, 8 : HALF + 8, :] = odd.astype(f32)
            first, second = (
                pl.ds(pl.multiple_of((2 * half + frame) * PITCH + i * 128, 128), HALF)
                for i in range(2)
            )
            shifted[0, h, first, :] = odd
            shifted[0, h, second, :] = pad[0, 9 : HALF + 9, :].astype(bf16)
            shifted[1, h, first, :] = even
            shifted[1, h, second, :] = odd
            shifted[2, h, first, :] = pad[1, 7 : HALF + 7, :].astype(bf16)
            shifted[2, h, second, :] = even

    def complete(array, slot, half):
        for k in range(2):
            arrived(array, slot, half, k)
        expand(array, slot, half)
        if array == 0:
            transpose(slot, half)

    complete(0, own, 1 - tm)
    complete(1, own, 1 - tm)

    @pl.when(inner)
    def _():
        pl.semaphore_wait(known, 1)
        announce(mate_pair)


    def pass_on(array, slot, k, copies):
        arrived(array, slot, tm, k)
        for copy in copies:
            copy[k].start()

    def pass_other(k):
        pass_on(0, other_slot, k, [])

        @pl.when(has_inner)
        def _():
            relayed[k].start()

        onward[0][k].start()

    pass_other(0)
    convolve(1, 1, True)
    pass_other(1)
    expand(0, other_slot, tm)
    transpose(other_slot, tm)

    @pl.when(has_inner)
    def _():
        for k in range(2):
            pass_on(0, near_slot, k, [near])
        expand(0, near_slot, tm)
        transpose(near_slot, tm)

    for half in range(2):
        shift(side, half)
    complete(0, other_slot, 1 - tm)

    @pl.when(has_inner)
    def _():
        complete(0, near_slot, 1 - tm)

    for k in range(2):
        pass_on(1, other_slot, k, [onward[1]])

        @pl.when(has_outer)
        def _():
            pass_on(0, far_slot, k, [far[0]])

        @pl.when(has_inner)
        def _():
            pass_on(1, near_slot, k, [across])

    @pl.when(has_outer)
    def _():
        expand(0, far_slot, tm)
        transpose(far_slot, tm)

    expand(1, other_slot, tm)
    shift(1 - side, tm)

    @pl.when(has_outer)
    def _():
        complete(0, far_slot, 1 - tm)

    complete(1, other_slot, 1 - tm)
    shift(1 - side, 1 - tm)

    owners = (end, stop, mate_pair, pair)

    def shard(owner):
        return tm * 2 * PAIRS + 2 * owner + side

    def filter_sum(k):
        first_block = shard(owners[k]) * CHUNK // 16
        first_tap = first_block // (CH // 16)
        base = pl.multiple_of(first_block % (CH // 16) * 16, 16)

        def term(n):
            tap = first_tap + n
            step_t, step_h, step_w = tap // 9, tap // 3 % 3, tap % 3
            lanes = pl.ds(pl.multiple_of(step_t * PITCH, 128), 4 * PITCH)
            filt[k, n * CH : (n + 1) * CH, :] = jnp.dot(
                act_t[step_h, :, lanes], shifted[step_w, 0], preferred_element_type=f32
            ) + jnp.dot(act_t[step_h + 1, :, lanes], shifted[step_w, 1], preferred_element_type=f32)

        term(0)
        term(1)

        @pl.when(base + TALL > 2 * CH)
        def _():
            term(2)

        return base

    def folded(k, base):
        high = filt[k, pl.ds(base, TALL), 128:CH]
        return jnp.concatenate(
            [
                filt[k, pl.ds(base, TALL), 0:128],
                jnp.concatenate(
                    [
                        high[0:CUT],
                        jnp.concatenate([high[CUT:TALL], jnp.zeros((2 * CUT - TALL, 64), f32)], axis=0),
                    ],
                    axis=1,
                ),
            ],
            axis=0,
        )

    lanes_of_pieces = iter(range(7))

    def piece(k, ref, slot, recv, owner, part_of=None):
        src, dst, sem = outgoing.at[k], ref.at[slot], recv.at[slot]
        if part_of is not None:
            span = pl.ds(part_of * (PIECE // 2), PIECE // 2)
            src, dst, sem = src.at[span], dst.at[span], recv.at[slot + part_of]
        return pltpu.make_async_remote_copy(
            src_ref=src,
            dst_ref=dst,
            send_sem=piece_send.at[next(lanes_of_pieces)],
            recv_sem=sem,
            device_id=device(tm, 2 * owner + side),
            device_id_type=pl.DeviceIdType.MESH,
        )

    outer_direct = piece(0, incoming, 1, piece_recv, end)
    inner_direct = piece(0, incoming, 2, piece_recv, end)
    to_inner = [piece(1, passing, 0, pass_recv, mate_pair, i) for i in range(2)]
    summed = [piece(1, incoming, 3, piece_recv, stop, i) for i in range(2)]
    to_mate = piece(2, incoming, 0, piece_recv, mate_pair)
    bases = []
    for k in range(4):
        base = filter_sum(k)
        bases.append(base)
        if k == 0:
            outgoing[k] = folded(k, base).astype(bf16)

            @pl.when(inner)
            def _():
                inner_direct.start()

            @pl.when(jnp.logical_not(inner))
            def _():
                pl.semaphore_wait(known, 1)
                outer_direct.start()

        elif k == 1:

            @pl.when(jnp.logical_not(inner))
            def _():
                outgoing[k] = folded(k, base).astype(bf16)
                for copy in to_inner:
                    copy.start()

        elif k == 2:
            outgoing[k] = folded(k, base).astype(bf16)
            to_mate.start()

            @pl.when(has_outer)
            def _():
                for part_of in range(2):
                    pass_on(1, far_slot, part_of, [far[1]])
                expand(1, far_slot, tm)

    convolve(2 - 2 * side, 2 * side, False)

    @pl.when(has_outer)
    def _():
        for k in range(2):
            arrived(1, far_slot, 1 - tm, k)
        expand(1, far_slot, 1 - tm)

    convolve(2 * side, 2 - 2 * side, False)

    @pl.when(inner)
    def _():
        mine = folded(1, bases[1])
        for i in range(2):
            to_inner[i].wait_recv()
            span = slice(i * (PIECE // 2), (i + 1) * (PIECE // 2))
            outgoing[1, span, :] = (mine[span] + passing[0, span, :].astype(f32)).astype(bf16)
            summed[i].start()

    def finish(total, slot, weighted):
        for frame in range(2):
            span = slice(frame * HALF, (frame + 1) * HALF)
            pad[0, 8 : HALF + 8, :] = total[3, span, :]
            pad[1, 8 : HALF + 8, :] = total[2, span, :]
            even = total[0, span, :] + pad[0, 7 : HALF + 7, :]
            odd = total[1, span, :] + pad[1, 9 : HALF + 9, :]
            lanes = (
                even[:, 0:128],
                jnp.concatenate([even[:, 128:CH], odd[:, 0:64]], axis=1),
                odd[:, 64:CH],
            )
            for j in range(3):
                value = lanes[j] * factor[j, frame] if weighted else lanes[j]
                wide[slot, pl.ds(2 * j + frame, HALF, stride=6), :] = value

    finish(fwd, 0, False)
    out_ref[...] = wide[0].astype(bf16)
    finish(bwd, 1, True)
    ig_ref[...] = wide[1].astype(bf16)

    to_mate.wait_recv()
    total = folded(3, bases[3]) + incoming[0].astype(f32)

    @pl.when(inner)
    def _():
        for copy in summed:
            copy.wait_recv()

    @pl.when(jnp.logical_not(inner))
    def _():
        inner_direct.wait_recv()
        outer_direct.wait_recv()

    for i in range(1, 4):
        total = total + incoming[i].astype(f32)
    total = total / scale
    sums[0, 0:TALL, :] = total[0:TALL]
    sums[1, 0:CUT, 0:64] = total[TALL:PIECE, 0:64]
    sums[1, CUT:TALL, 0:64] = total[TALL : 2 * TALL - CUT, 64:128]
    for q in range(4):

        @pl.when(shard(pair) % 4 == q)
        def _():
            even, odd = (pl.ds(4 * q + i, CHUNK // 2, stride=2) for i in range(2))
            low = sums[0, odd, :]
            lanes = (
                sums[0, even, :],
                jnp.concatenate([sums[1, even, :][:, 0:64], low[:, 0:64]], axis=1),
                jnp.concatenate([low[:, 64:128], sums[1, odd, :][:, 0:64]], axis=1),
            )
            for j in range(3):
                wide[0, pl.ds(j, CHUNK // 2, stride=3), :] = lanes[j]

    fg_ref[...] = wide[0, 0 : CHUNK // 2 * 3, :].astype(bf16)

    for copies in to_partner + to_sibling + onward:
        for copy in copies:
            copy.wait_send()

    @pl.when(has_outer)
    def _():
        for copies in outward + far:
            for copy in copies:
                copy.wait_send()

    @pl.when(has_inner)
    def _():
        for copy in near + relayed + across:
            copy.wait_send()

    @pl.when(inner)
    def _():
        for copy in [inner_direct] + summed:
            copy.wait_send()

    @pl.when(jnp.logical_not(inner))
    def _():
        for copy in [outer_direct] + to_inner:
            copy.wait_send()

    to_mate.wait_send()


def hand_over(*refs):
    copies = [
        pltpu.make_async_copy(refs[i], refs[3 + i], refs[6].at[i]) for i in range(3)
    ]
    for copy in copies:
        copy.start()
    for copy in copies:
        copy.wait()


def fused(inputs, weight, cotangent):
    frames, rows = inputs.shape[:2]
    scale = frames * lax.axis_size("tm") * rows * lax.axis_size("row")
    lines = WIDTH * CH // 128
    vmem, hbm = (pl.BlockSpec(memory_space=m) for m in (pltpu.VMEM, pltpu.HBM))
    bf16, f32 = jnp.bfloat16, jnp.float32

    def interleaved(array):
        return array.reshape(2, lines, 128).transpose(1, 0, 2).reshape(2 * lines, 128)

    def parted(array):
        return array.reshape(lines, 2, 128).transpose(1, 0, 2).reshape(2, 1, lines * 128)

    out, ig, fg = pl.pallas_call(
        functools.partial(fused_kernel, float(scale)),
        out_shape=(
            jax.ShapeDtypeStruct((2 * lines, 128), bf16),
            jax.ShapeDtypeStruct((2 * lines, 128), bf16),
            jax.ShapeDtypeStruct((CHUNK // 2 * 3, 128), bf16),
        ),
        in_specs=[hbm, hbm, hbm],
        out_specs=(vmem, vmem, vmem),
        scratch_shapes=[
            pltpu.VMEM((2, 4, 2, 2 * lines, 128), bf16),
            pltpu.VMEM((CH, TAPS * CH), bf16),
            pltpu.VMEM((2, 2 * lines, 128), f32),
            pltpu.VMEM((3, 2, HALF, 128), f32),
            pltpu.VMEM((4, 3, 6 * HALF, 128), bf16),
            pltpu.VMEM((4, 3, 6 * HALF, 128), bf16),
            pltpu.VMEM((TAPS, CH, 256), bf16),
            pltpu.VMEM((TAPS, CH, 256), bf16),
            pltpu.VMEM((TAPS, CH + 128, CH), bf16),
            pltpu.VMEM((4, CH, 6 * PITCH), bf16),
            pltpu.VMEM((3, 2, 4 * PITCH, CH), bf16),
            pltpu.VMEM((4, 3 * CH, CH), f32),
            pltpu.VMEM((3, PIECE, 128), bf16),
            pltpu.VMEM((1, PIECE, 128), bf16),
            pltpu.VMEM((4, PIECE, 128), bf16),
            pltpu.VMEM((4, 2 * HALF, CH), f32),
            pltpu.VMEM((4, 2 * HALF, CH), f32),
            pltpu.VMEM((2, HALF + 16, CH), f32),
            pltpu.VMEM((2, TALL, 128), f32),
            pltpu.SemaphoreType.REGULAR,
            pltpu.SemaphoreType.DMA((3,)),
            pltpu.SemaphoreType.DMA((28,)),
            pltpu.SemaphoreType.DMA((2, 4, 2, 2)),
            pltpu.SemaphoreType.DMA((7,)),
            pltpu.SemaphoreType.DMA((2,)),
            pltpu.SemaphoreType.DMA((5,)),
        ],
        compiler_params=pltpu.CompilerParams(
            collective_id=0, has_side_effects=True, vmem_limit_bytes=int(53.4 * 1024 * 1024)
        ),
    )(interleaved(inputs), weight.T, interleaved(cotangent))
    results = (out, ig, fg)
    out, ig, fg = pl.pallas_call(
        hand_over,
        out_shape=tuple(jax.ShapeDtypeStruct(r.shape, r.dtype) for r in results),
        in_specs=[pl.BlockSpec(memory_space=pl.ANY)] * 3,
        out_specs=(hbm, hbm, hbm),
        scratch_shapes=[pltpu.SemaphoreType.DMA((3,))],
        compiler_params=pltpu.CompilerParams(vmem_limit_bytes=1024 * 1024),
    )(*results)
    return parted(out), parted(ig), fg.reshape(-1)


def passed_along(array, axis, by):
    length = lax.axis_size(axis)
    pairs = [(i, i + by) for i in range(length) if 0 <= i + by < length]
    return lax.ppermute(array, axis, pairs)


def with_halo(array, sides, width):
    for axis, dim in sides:
        size, length = (lax.axis_size(axis), array.shape[dim])
        up = [(i, (i + 1) % size) for i in range(size - 1)]
        down = [(j, i) for i, j in up]
        last = lax.slice_in_dim(array, length - width, length, axis=dim)
        first = lax.slice_in_dim(array, 0, width, axis=dim)
        before = lax.ppermute(last, axis, up)
        after = lax.ppermute(first, axis, down)
        array = jnp.concatenate([before, array, after], axis=dim)
    return array


def on_device(inputs, weight, cotangent):
    frames = inputs.shape[0]
    rows = inputs.shape[1]
    act = jax.nn.silu(inputs.astype(jnp.float32)).astype(jnp.bfloat16)
    earlier = passed_along(act, "tm", 1)
    extended = jnp.concatenate([earlier, act], 0)
    extended = with_halo(extended, (("row", 1),), 1)
    extended = extended.reshape(frames + 2, rows + 2, WIDTH, CH)
    act_pad = jnp.pad(extended, ((0, 0), (0, 0), (1, 1), (0, 0)))
    cot_four = cotangent.reshape(frames, rows, WIDTH, CH)
    cot_flat = cot_four.reshape(-1, CH)
    output = jnp.zeros((frames * rows * WIDTH, CH), jnp.float32)
    blocks = []
    for step_t in range(3):
        for step_h in range(3):
            for step_w in range(3):
                offset = ((step_t * 3 + step_h) * 3 + step_w) * CH
                kernel = weight[offset : offset + CH]
                piece = act_pad[
                    step_t : step_t + frames, step_h : step_h + rows, step_w : step_w + WIDTH
                ].reshape(-1, CH)
                output = output + jnp.dot(piece, kernel, preferred_element_type=jnp.float32)
                blocks.append(
                    lax.dot_general(
                        piece,
                        cot_flat,
                        (((0,), (0,)), ((), ())),
                        preferred_element_type=jnp.float32,
                    )
                )
    spread = jnp.zeros((frames + 2, rows + 2, WIDTH + 2, CH), jnp.float32)
    for step_t in range(3):
        slab_weight = weight[step_t * 9 * CH : (step_t + 1) * 9 * CH]
        terms = lax.dot_general(
            cot_flat, slab_weight, (((1,), (1,)), ((), ())), preferred_element_type=jnp.float32
        )
        terms = terms.reshape(frames, rows, WIDTH, 9, CH)
        slab = jnp.zeros((frames, rows + 2, WIDTH + 2, CH), jnp.float32)
        for step_h in range(3):
            for step_w in range(3):
                slab = slab + jnp.pad(
                    terms[:, :, :, step_h * 3 + step_w],
                    ((0, 0), (step_h, 2 - step_h), (step_w, 2 - step_w), (0, 0)),
                )
        spread = spread + jnp.pad(slab, ((step_t, 2 - step_t), (0, 0), (0, 0), (0, 0)))
    inner = spread[:, :, 1 : WIDTH + 1]
    from_next = passed_along(inner[:, 0:1], "row", -1)
    from_prev = passed_along(inner[:, rows + 1 : rows + 2], "row", 1)
    center = inner[:, 1 : rows + 1]
    center = center.at[:, rows - 1 : rows].add(from_next)
    center = center.at[:, 0:1].add(from_prev)
    returned = passed_along(center[0:2], "tm", -1)
    grad_act = center[2:].at[frames - 2 :].add(returned).reshape(-1, CH)
    x_float = inputs.reshape(-1, CH).astype(jnp.float32)
    sigma = jax.nn.sigmoid(x_float)
    input_grad = (grad_act * sigma * (1.0 + x_float * (1.0 - sigma))).astype(jnp.bfloat16)
    local_filter = jnp.concatenate(blocks, 0).reshape(-1)
    frame_blocks = lax.axis_size("tm")
    row_blocks = lax.axis_size("row")
    scale = frames * frame_blocks * rows * row_blocks
    share = lax.psum_scatter(local_filter, ("tm", "row"), scatter_dimension=0, tiled=True)
    filter_grad = (share / scale).astype(jnp.bfloat16)
    shape = (frames, rows, WIDTH * CH)
    return (output.astype(jnp.bfloat16).reshape(shape), input_grad.reshape(shape), filter_grad)


def either(mesh, inputs, weight, cotangent):
    size = mesh.shape["row"]
    if mesh.shape["tm"] == 2 and size == 2 * PAIRS and inputs.shape[:2] == (2, 1):
        return fused(inputs, weight, cotangent)
    return on_device(inputs, weight, cotangent)


def solution(mesh):
    placed = (P(("grp", "tm"), "row", None), P(), P(("grp", "tm"), "row", None))
    return jax.shard_map(
        functools.partial(either, mesh),
        mesh=mesh,
        in_specs=placed,
        out_specs=(
            P(("grp", "tm"), "row", None),
            P(("grp", "tm"), "row", None),
            P(("grp", "tm", "row")),
        ),
        check_vma=False,
    )
```

```python
import functools

import jax
import jax.numpy as jnp
from jax import lax
from jax.experimental import pallas as pl
from jax.experimental.pallas import tpu as pltpu
from jax.sharding import PartitionSpec as P

CH = 192
WIDTH = 224
TAPS = 27
HALF = WIDTH // 2
LINES = WIDTH * CH // 128
PAIRS = 4
CHUNK = TAPS * CH // (4 * PAIRS)
TALL = CHUNK + 12
CUT = 176
PIECE = TALL + CUT
ORDER = ((3, 2, 1, 0), (0, 3, 2, 1), (0, 3, 1, 2), (0, 1, 2, 3))
PITCH = 256


def fused_kernel(
    scale, x_ref, w_ref, c_ref, out_ref, ig_ref, fg_ref,
    raw, weight_in, wide, factor, act, cot, fwd_even, fwd_odd, bwd_taps, act_t, shifted, filt,
    outgoing, passing, incoming, fwd, bwd, pad, sums,
    known, fetch_sem, send_sem, recv_sem, piece_send, pass_recv, piece_recv,
):
    f32, bf16 = jnp.float32, jnp.bfloat16
    grp, tm, row = lax.axis_index("grp"), lax.axis_index("tm"), lax.axis_index("row")
    pair, side = row // 2, row % 2
    own, other_slot = 1 + side, 2 - side

    def device(t, r):
        return (grp, t, r)

    barrier = pltpu.get_barrier_semaphore()

    def greet(target):
        pl.semaphore_signal(barrier, inc=1, device_id=target, device_id_type=pl.DeviceIdType.MESH)

    fetches = [
        pltpu.make_async_copy(src, dst, fetch_sem.at[i])
        for i, (src, dst) in enumerate(
            ((x_ref, raw.at[0, own, tm]), (c_ref, raw.at[1, own, tm]), (w_ref, weight_in))
        )
    ]
    sibling = device(1 - tm, row)
    partner = device(tm, 2 * pair + 1 - side)
    greet(sibling)
    greet(partner)
    has_before, has_after = pair > 0, pair < PAIRS - 1
    part = pair // 2
    inner = (pair + part) % 2 == 1
    mate_pair = pair + 1 - 2 * (pair % 2)
    stop, end = 2 - part, 3 * (1 - part)
    for step, present in ((-1, has_before), (1, has_after)):

        @pl.when(present)
        def _():
            greet(device(tm, 2 * (pair + step) + side))

    for fetch in fetches:
        fetch.start()

    def block(index):
        return pl.ds(pl.multiple_of(index * HALF, 16), HALF)

    lanes_used = iter(range(28))

    def move(array, src_slot, dst_slot, half, target):
        copies = []
        for k in range(2):
            span = pl.ds(k * LINES, LINES)
            src = (c_ref if array else x_ref) if src_slot is None else raw.at[array, src_slot, half]
            copies.append(
                pltpu.make_async_remote_copy(
                    src_ref=src.at[span],
                    dst_ref=raw.at[array, dst_slot, half, span],
                    send_sem=send_sem.at[next(lanes_used)],
                    recv_sem=recv_sem.at[array, dst_slot, half, k],
                    device_id=target,
                    device_id_type=pl.DeviceIdType.MESH,
                )
            )
        return copies

    def arrived(array, slot, half, k):
        ref = raw.at[array, slot, half, pl.ds(k * LINES, LINES)]
        pltpu.make_async_remote_copy(
            src_ref=ref,
            dst_ref=ref,
            send_sem=send_sem.at[0],
            recv_sem=recv_sem.at[array, slot, half, k],
            device_id=sibling,
            device_id_type=pl.DeviceIdType.MESH,
        ).wait_recv()

    outer_pair = pair + 2 * side - 1
    inner_pair = pair + 1 - 2 * side
    has_outer = jnp.logical_and(outer_pair >= 0, outer_pair < PAIRS)
    has_inner = jnp.logical_and(inner_pair >= 0, inner_pair < PAIRS)
    outer_same = device(tm, 2 * outer_pair + side)
    inner_same = device(tm, 2 * inner_pair + side)
    near_slot, far_slot = 3 * (1 - side), 3 * side

    to_partner = [move(i, None, own, tm, partner) for i in range(2)]
    to_sibling = [move(i, None, own, tm, sibling) for i in range(2)]
    outward = [move(i, None, near_slot, tm, outer_same) for i in range(2)]
    onward = [move(i, other_slot, other_slot, tm, sibling) for i in range(2)]
    relayed = move(0, other_slot, far_slot, tm, inner_same)
    across = move(1, near_slot, near_slot, tm, partner)
    near = move(0, near_slot, near_slot, tm, sibling)
    far = [move(i, far_slot, far_slot, tm, sibling) for i in range(2)]

    def expand(array, slot, half, keep=False):
        wide[array] = raw[array, slot, half].astype(f32)
        for j in range(3):
            for frame in range(2):
                value = wide[array, pl.ds(2 * j + frame, HALF, stride=6), :]
                if array == 0:
                    sigma = 1.0 / (1.0 + jnp.exp(-value))
                    if keep:
                        factor[j, frame] = sigma * (1.0 + value * (1.0 - sigma))
                    act[slot, j, block(2 * half + 2 + frame), :] = (value * sigma).astype(bf16)
                else:
                    cot[slot, j, block(2 * half + frame), :] = value.astype(bf16)

    def announce(target):
        pl.semaphore_signal(
            known, inc=1, device_id=device(tm, 2 * target + side), device_id_type=pl.DeviceIdType.MESH
        )

    pl.semaphore_wait(barrier, jnp.where(inner, 4, 3))

    @pl.when(inner)
    def _():
        announce(stop)

    for i in range(2):
        for k in range(2):
            to_partner[i][k].start()

        @pl.when(has_outer)
        def _():
            for k in range(2):
                outward[i][k].start()

        for k in range(2):
            to_sibling[i][k].start()

    for i in range(2):
        fetches[i].wait()
        expand(i, own, tm, keep=i == 0)

    for slot in range(4):
        act[slot, :, 0 : 2 * HALF, :] = jnp.zeros((3, 2 * HALF, 128), bf16)
        cot[slot, :, 4 * HALF : 6 * HALF, :] = jnp.zeros((3, 2 * HALF, 128), bf16)
        act_t[slot, :, 0 : 2 * PITCH] = jnp.zeros((CH, 2 * PITCH), bf16)

    for slot, present in ((0, has_before), (3, has_after)):

        @pl.when(jnp.logical_not(present))
        def _():
            act[slot, :, 2 * HALF : 6 * HALF, :] = jnp.zeros((3, 4 * HALF, 128), bf16)
            cot[slot, :, 0 : 4 * HALF, :] = jnp.zeros((3, 4 * HALF, 128), bf16)
            act_t[slot, :, 2 * PITCH : 6 * PITCH] = jnp.zeros((CH, 4 * PITCH), bf16)


    @pl.when(inner)
    def _():
        incoming[1:3] = jnp.zeros((2, PIECE, 128), bf16)

    @pl.when(jnp.logical_not(inner))
    def _():
        incoming[3] = jnp.zeros((PIECE, 128), bf16)

    pad[:, 0:8, :] = jnp.zeros((2, 8, CH), f32)
    pad[:, HALF + 8 : HALF + 16, :] = jnp.zeros((2, 8, CH), f32)
    for i in range(8):
        shifted[:, :, i * 128 + HALF : (i + 1) * 128, :] = jnp.zeros(
            (3, 2, 128 - HALF, CH), bf16
        )
    bwd_taps[:, 0:64, :] = jnp.zeros((TAPS, 64, CH), bf16)
    bwd_taps[:, 64 + CH : 128 + CH, :] = jnp.zeros((TAPS, 64, CH), bf16)

    fetches[2].wait()
    for tap in range(TAPS):
        value = weight_in[:, tap * CH : (tap + 1) * CH]
        fwd_even[tap] = jnp.concatenate([value, jnp.zeros((CH, 64), bf16)], axis=1)
        fwd_odd[tap] = jnp.concatenate([jnp.zeros((CH, 64), bf16), value], axis=1)
        bwd_taps[tap, 64 : 64 + CH, :] = value

    def transpose(slot, half):
        for frame in range(2):
            lane = (2 * half + 2 + frame) * PITCH
            even = pl.ds(pl.multiple_of(lane, 128), 128)
            odd = pl.ds(pl.multiple_of(lane + 128, 128), 128)

            def turned(j):
                value = act[slot, j, block(2 * half + 2 + frame), :]
                return jnp.concatenate([value, jnp.zeros((128 - HALF, 128), bf16)], axis=0).T

            act_t[slot, 0:128, even] = turned(0)
            both = turned(1)
            act_t[slot, 128:CH, even] = both[0:64]
            act_t[slot, 0:64, odd] = both[64:128]
            act_t[slot, 64:CH, odd] = turned(2)

    transpose(own, tm)

    def dots(ref, slot, starts, weights, out, first):
        def side_of(start, j):
            rows_of = pl.ds(pl.multiple_of(start, 16), 2 * HALF)
            return jnp.concatenate([ref[slot, j, rows_of, :], ref[slot, j + 1, rows_of, :]], axis=1)

        for i, terms in enumerate((((0, 1), (1, 2)), ((1, 1), (0, 0)), ((0, 2),), ((1, 0),))):
            total = None
            for step_t in range(3):
                for odd, step_w in terms:
                    more = weights(side_of(starts[step_t], odd), odd, step_t, step_w)
                    total = more if total is None else total + more
            if first:
                out[i] = total
            else:
                out[i] += total

    def convolve(act_h, cot_h, first):
        def forward(value, odd, step_t, step_w):
            taps = fwd_odd if odd else fwd_even
            return lax.dot_general(
                value,
                taps[(step_t * 3 + act_h) * 3 + step_w],
                (((1,), (1,)), ((), ())),
                preferred_element_type=f32,
            )

        def backward(value, odd, step_t, step_w):
            first_row = 0 if odd else 64
            return jnp.dot(
                value,
                bwd_taps[(step_t * 3 + cot_h) * 3 + 2 - step_w, first_row : first_row + 256, :],
                preferred_element_type=f32,
            )

        starts = [(2 * tm + step_t) * HALF for step_t in range(3)]
        dots(act, side + act_h, starts, forward, fwd, first)
        dots(cot, side + 2 - cot_h, starts[::-1], backward, bwd, first)

    def shift(h, half):
        for frame in range(2):
            rows_of = block(2 * half + frame)
            mid = cot[1 + h, 1, rows_of, :]
            even = jnp.concatenate([cot[1 + h, 0, rows_of, :], mid[:, 0:64]], axis=1)
            odd = jnp.concatenate([mid[:, 64:128], cot[1 + h, 2, rows_of, :]], axis=1)
            pad[0, 8 : HALF + 8, :] = even.astype(f32)
            pad[1, 8 : HALF + 8, :] = odd.astype(f32)
            first, second = (
                pl.ds(pl.multiple_of((2 * half + frame) * PITCH + i * 128, 128), HALF)
                for i in range(2)
            )
            shifted[0, h, first, :] = odd
            shifted[0, h, second, :] = pad[0, 9 : HALF + 9, :].astype(bf16)
            shifted[1, h, first, :] = even
            shifted[1, h, second, :] = odd
            shifted[2, h, first, :] = pad[1, 7 : HALF + 7, :].astype(bf16)
            shifted[2, h, second, :] = even

    def complete(array, slot, half):
        for k in range(2):
            arrived(array, slot, half, k)
        expand(array, slot, half)
        if array == 0:
            transpose(slot, half)

    complete(0, own, 1 - tm)
    complete(1, own, 1 - tm)

    @pl.when(inner)
    def _():
        pl.semaphore_wait(known, 1)
        announce(mate_pair)


    def pass_on(array, slot, k, copies):
        arrived(array, slot, tm, k)
        for copy in copies:
            copy[k].start()

    def pass_other(k):
        pass_on(0, other_slot, k, [])

        @pl.when(has_inner)
        def _():
            relayed[k].start()

        onward[0][k].start()

    pass_other(0)
    convolve(1, 1, True)
    pass_other(1)
    expand(0, other_slot, tm)
    transpose(other_slot, tm)

    @pl.when(has_inner)
    def _():
        for k in range(2):
            pass_on(0, near_slot, k, [near])
        expand(0, near_slot, tm)
        transpose(near_slot, tm)

    for half in range(2):
        shift(side, half)
    complete(0, other_slot, 1 - tm)

    @pl.when(has_inner)
    def _():
        complete(0, near_slot, 1 - tm)

    for k in range(2):
        pass_on(1, other_slot, k, [onward[1]])

        @pl.when(has_outer)
        def _():
            pass_on(0, far_slot, k, [far[0]])

        @pl.when(has_inner)
        def _():
            pass_on(1, near_slot, k, [across])

    @pl.when(has_outer)
    def _():
        expand(0, far_slot, tm)
        transpose(far_slot, tm)

    expand(1, other_slot, tm)
    shift(1 - side, tm)

    @pl.when(has_outer)
    def _():
        complete(0, far_slot, 1 - tm)

    def at_pair(values):
        chosen = jnp.int32(values[0])
        for p in range(1, PAIRS):
            chosen = jnp.where(pair == p, jnp.int32(values[p]), chosen)
        return chosen

    owners = tuple(at_pair([ORDER[p][k] for p in range(PAIRS)]) for k in range(PAIRS))

    def shard(owner):
        return tm * 2 * PAIRS + 2 * owner + side

    def filter_sum(k, late=None):
        first_block = shard(owners[k]) * CHUNK // 16
        first_tap = first_block // (CH // 16)
        base = pl.multiple_of(first_block % (CH // 16) * 16, 16)

        def over(tap, i, half, frames):
            step_t, step_h, step_w = tap // 9, tap // 3 % 3, tap % 3
            lanes = pl.ds(pl.multiple_of((step_t + 2 * half) * PITCH, 128), frames * PITCH)
            rows_of = pl.ds(pl.multiple_of(2 * half * PITCH, 16), frames * PITCH)
            return jnp.dot(
                act_t[step_h + i, :, lanes],
                shifted[step_w, i, rows_of, :],
                preferred_element_type=f32,
            )

        def term(n):
            tap = first_tap + n
            span = slice(n * CH, (n + 1) * CH)
            if late is None:
                filt[k, span, :] = over(tap, 0, 0, 4) + over(tap, 1, 0, 4)
            elif late:
                filt[k, span, :] += over(tap, 1 - side, 1 - tm, 2)
            else:
                filt[k, span, :] = over(tap, side, 0, 4) + over(tap, 1 - side, tm, 2)

        term(0)
        term(1)

        @pl.when(base + TALL > 2 * CH)
        def _():
            term(2)

        return base

    filter_sum(0, late=False)
    complete(1, other_slot, 1 - tm)
    shift(1 - side, 1 - tm)


    def folded(k, base):
        high = filt[k, pl.ds(base, TALL), 128:CH]
        return jnp.concatenate(
            [
                filt[k, pl.ds(base, TALL), 0:128],
                jnp.concatenate(
                    [
                        high[0:CUT],
                        jnp.concatenate([high[CUT:TALL], jnp.zeros((2 * CUT - TALL, 64), f32)], axis=0),
                    ],
                    axis=1,
                ),
            ],
            axis=0,
        )

    def piece(k, ref, slot, recv, owner, part_of=None):
        src, dst, sem = outgoing.at[k], ref.at[slot], recv.at[slot]
        if part_of is not None:
            span = pl.ds(part_of * (PIECE // 2), PIECE // 2)
            src, dst, sem = src.at[span], dst.at[span], recv.at[slot + part_of]
        return pltpu.make_async_remote_copy(
            src_ref=src,
            dst_ref=dst,
            send_sem=piece_send.at[2 * k + (part_of or 0)],
            recv_sem=sem,
            device_id=device(tm, 2 * owner + side),
            device_id_type=pl.DeviceIdType.MESH,
        )

    def pieces_of(p, k):
        mate, owner = p + 1 - 2 * (p % 2), ORDER[p][k]
        if owner == mate:
            return [piece(k, incoming, 0, piece_recv, mate)]
        if owner in (0, 3):
            return [piece(k, incoming, 2 if p in (1, 2) else 1, piece_recv, owner)]
        if p in (1, 2):
            return [piece(k, incoming, 3, piece_recv, owner, i) for i in range(2)]
        return [piece(k, passing, 0, pass_recv, mate, i) for i in range(2)]

    bases = [filter_sum(0, late=True)]
    for k in range(4):
        if k > 0:
            bases.append(filter_sum(k))
        if k == 3:
            break
        outgoing[k] = folded(k, bases[k]).astype(bf16)
        for p in range(PAIRS):
            if p in (1, 2) and k == 2:
                continue

            @pl.when(pair == p)
            def _():
                if p in (0, 3) and ORDER[p][k] == 3 - p:
                    pl.semaphore_wait(known, 1)
                for copy in pieces_of(p, k):
                    copy.start()

        if k == 1:

            @pl.when(has_outer)
            def _():
                for part_of in range(2):
                    pass_on(1, far_slot, part_of, [far[1]])
                expand(1, far_slot, tm)

    convolve(2 - 2 * side, 2 * side, False)

    @pl.when(has_outer)
    def _():
        for k in range(2):
            arrived(1, far_slot, 1 - tm, k)
        expand(1, far_slot, 1 - tm)

    convolve(2 * side, 2 - 2 * side, False)

    @pl.when(inner)
    def _():
        mine = folded(2, bases[2])
        for i in range(2):
            piece(2, passing, 0, pass_recv, mate_pair, i).wait_recv()
            span = slice(i * (PIECE // 2), (i + 1) * (PIECE // 2))
            outgoing[2, span, :] = (mine[span] + passing[0, span, :].astype(f32)).astype(bf16)
            piece(2, incoming, 3, piece_recv, stop, i).start()

    def finish(total, slot, weighted):
        for frame in range(2):
            span = slice(frame * HALF, (frame + 1) * HALF)
            pad[0, 8 : HALF + 8, :] = total[3, span, :]
            pad[1, 8 : HALF + 8, :] = total[2, span, :]
            even = total[0, span, :] + pad[0, 7 : HALF + 7, :]
            odd = total[1, span, :] + pad[1, 9 : HALF + 9, :]
            lanes = (
                even[:, 0:128],
                jnp.concatenate([even[:, 128:CH], odd[:, 0:64]], axis=1),
                odd[:, 64:CH],
            )
            for j in range(3):
                value = lanes[j] * factor[j, frame] if weighted else lanes[j]
                wide[slot, pl.ds(2 * j + frame, HALF, stride=6), :] = value

    finish(fwd, 0, False)
    out_ref[...] = wide[0].astype(bf16)
    finish(bwd, 1, True)
    ig_ref[...] = wide[1].astype(bf16)

    piece(0, incoming, 0, piece_recv, mate_pair).wait_recv()
    total = folded(3, bases[3]) + incoming[0].astype(f32)

    @pl.when(inner)
    def _():
        for i in range(2):
            piece(0, incoming, 3, piece_recv, stop, i).wait_recv()

    @pl.when(jnp.logical_not(inner))
    def _():
        for slot in range(1, 3):
            piece(0, incoming, slot, piece_recv, mate_pair).wait_recv()

    for i in range(1, 4):
        total = total + incoming[i].astype(f32)
    total = total * (1.0 / scale)
    sums[0, 0:TALL, :] = total[0:TALL]
    sums[1, 0:CUT, 0:64] = total[TALL:PIECE, 0:64]
    sums[1, CUT:TALL, 0:64] = total[TALL : 2 * TALL - CUT, 64:128]
    for q in range(4):

        @pl.when(shard(pair) % 4 == q)
        def _():
            even, odd = (pl.ds(4 * q + i, CHUNK // 2, stride=2) for i in range(2))
            low = sums[0, odd, :]
            lanes = (
                sums[0, even, :],
                jnp.concatenate([sums[1, even, :][:, 0:64], low[:, 0:64]], axis=1),
                jnp.concatenate([low[:, 64:128], sums[1, odd, :][:, 0:64]], axis=1),
            )
            for j in range(3):
                wide[0, pl.ds(j, CHUNK // 2, stride=3), :] = lanes[j]

    fg_ref[...] = wide[0, 0 : CHUNK // 2 * 3, :].astype(bf16)

    for copies in to_partner + to_sibling + onward:
        for copy in copies:
            copy.wait_send()

    @pl.when(has_outer)
    def _():
        for copies in outward + far:
            for copy in copies:
                copy.wait_send()

    @pl.when(has_inner)
    def _():
        for copy in near + relayed + across:
            copy.wait_send()

    for p in range(PAIRS):

        @pl.when(pair == p)
        def _():
            for k in range(3):
                for copy in pieces_of(p, k):
                    copy.wait_send()


def hand_over(*refs):
    copies = [
        pltpu.make_async_copy(refs[i], refs[3 + i], refs[6].at[i]) for i in range(3)
    ]
    for copy in copies:
        copy.start()
    for copy in copies:
        copy.wait()


def fused(inputs, weight, cotangent):
    frames, rows = inputs.shape[:2]
    scale = frames * lax.axis_size("tm") * rows * lax.axis_size("row")
    lines = WIDTH * CH // 128
    vmem, hbm = (pl.BlockSpec(memory_space=m) for m in (pltpu.VMEM, pltpu.HBM))
    bf16, f32 = jnp.bfloat16, jnp.float32

    def interleaved(array):
        return array.reshape(2, lines, 128).transpose(1, 0, 2).reshape(2 * lines, 128)

    def parted(array):
        return array.reshape(lines, 2, 128).transpose(1, 0, 2).reshape(2, 1, lines * 128)

    out, ig, fg = pl.pallas_call(
        functools.partial(fused_kernel, float(scale)),
        out_shape=(
            jax.ShapeDtypeStruct((2 * lines, 128), bf16),
            jax.ShapeDtypeStruct((2 * lines, 128), bf16),
            jax.ShapeDtypeStruct((CHUNK // 2 * 3, 128), bf16),
        ),
        in_specs=[hbm, hbm, hbm],
        out_specs=(vmem, vmem, vmem),
        scratch_shapes=[
            pltpu.VMEM((2, 4, 2, 2 * lines, 128), bf16),
            pltpu.VMEM((CH, TAPS * CH), bf16),
            pltpu.VMEM((2, 2 * lines, 128), f32),
            pltpu.VMEM((3, 2, HALF, 128), f32),
            pltpu.VMEM((4, 3, 6 * HALF, 128), bf16),
            pltpu.VMEM((4, 3, 6 * HALF, 128), bf16),
            pltpu.VMEM((TAPS, CH, 256), bf16),
            pltpu.VMEM((TAPS, CH, 256), bf16),
            pltpu.VMEM((TAPS, CH + 128, CH), bf16),
            pltpu.VMEM((4, CH, 6 * PITCH), bf16),
            pltpu.VMEM((3, 2, 4 * PITCH, CH), bf16),
            pltpu.VMEM((4, 3 * CH, CH), f32),
            pltpu.VMEM((3, PIECE, 128), bf16),
            pltpu.VMEM((1, PIECE, 128), bf16),
            pltpu.VMEM((4, PIECE, 128), bf16),
            pltpu.VMEM((4, 2 * HALF, CH), f32),
            pltpu.VMEM((4, 2 * HALF, CH), f32),
            pltpu.VMEM((2, HALF + 16, CH), f32),
            pltpu.VMEM((2, TALL, 128), f32),
            pltpu.SemaphoreType.REGULAR,
            pltpu.SemaphoreType.DMA((3,)),
            pltpu.SemaphoreType.DMA((28,)),
            pltpu.SemaphoreType.DMA((2, 4, 2, 2)),
            pltpu.SemaphoreType.DMA((6,)),
            pltpu.SemaphoreType.DMA((2,)),
            pltpu.SemaphoreType.DMA((5,)),
        ],
        compiler_params=pltpu.CompilerParams(
            collective_id=0, has_side_effects=True, vmem_limit_bytes=int(53.4 * 1024 * 1024)
        ),
    )(interleaved(inputs), weight.T, interleaved(cotangent))
    results = (out, ig, fg)
    out, ig, fg = pl.pallas_call(
        hand_over,
        out_shape=tuple(jax.ShapeDtypeStruct(r.shape, r.dtype) for r in results),
        in_specs=[pl.BlockSpec(memory_space=pl.ANY)] * 3,
        out_specs=(hbm, hbm, hbm),
        scratch_shapes=[pltpu.SemaphoreType.DMA((3,))],
        compiler_params=pltpu.CompilerParams(vmem_limit_bytes=1024 * 1024),
    )(*results)
    return parted(out), parted(ig), fg.reshape(-1)


def passed_along(array, axis, by):
    length = lax.axis_size(axis)
    pairs = [(i, i + by) for i in range(length) if 0 <= i + by < length]
    return lax.ppermute(array, axis, pairs)


def with_halo(array, sides, width):
    for axis, dim in sides:
        size, length = (lax.axis_size(axis), array.shape[dim])
        up = [(i, (i + 1) % size) for i in range(size - 1)]
        down = [(j, i) for i, j in up]
        last = lax.slice_in_dim(array, length - width, length, axis=dim)
        first = lax.slice_in_dim(array, 0, width, axis=dim)
        before = lax.ppermute(last, axis, up)
        after = lax.ppermute(first, axis, down)
        array = jnp.concatenate([before, array, after], axis=dim)
    return array


def on_device(inputs, weight, cotangent):
    frames = inputs.shape[0]
    rows = inputs.shape[1]
    act = jax.nn.silu(inputs.astype(jnp.float32)).astype(jnp.bfloat16)
    earlier = passed_along(act, "tm", 1)
    extended = jnp.concatenate([earlier, act], 0)
    extended = with_halo(extended, (("row", 1),), 1)
    extended = extended.reshape(frames + 2, rows + 2, WIDTH, CH)
    act_pad = jnp.pad(extended, ((0, 0), (0, 0), (1, 1), (0, 0)))
    cot_four = cotangent.reshape(frames, rows, WIDTH, CH)
    cot_flat = cot_four.reshape(-1, CH)
    output = jnp.zeros((frames * rows * WIDTH, CH), jnp.float32)
    blocks = []
    for step_t in range(3):
        for step_h in range(3):
            for step_w in range(3):
                offset = ((step_t * 3 + step_h) * 3 + step_w) * CH
                kernel = weight[offset : offset + CH]
                piece = act_pad[
                    step_t : step_t + frames, step_h : step_h + rows, step_w : step_w + WIDTH
                ].reshape(-1, CH)
                output = output + jnp.dot(piece, kernel, preferred_element_type=jnp.float32)
                blocks.append(
                    lax.dot_general(
                        piece,
                        cot_flat,
                        (((0,), (0,)), ((), ())),
                        preferred_element_type=jnp.float32,
                    )
                )
    spread = jnp.zeros((frames + 2, rows + 2, WIDTH + 2, CH), jnp.float32)
    for step_t in range(3):
        slab_weight = weight[step_t * 9 * CH : (step_t + 1) * 9 * CH]
        terms = lax.dot_general(
            cot_flat, slab_weight, (((1,), (1,)), ((), ())), preferred_element_type=jnp.float32
        )
        terms = terms.reshape(frames, rows, WIDTH, 9, CH)
        slab = jnp.zeros((frames, rows + 2, WIDTH + 2, CH), jnp.float32)
        for step_h in range(3):
            for step_w in range(3):
                slab = slab + jnp.pad(
                    terms[:, :, :, step_h * 3 + step_w],
                    ((0, 0), (step_h, 2 - step_h), (step_w, 2 - step_w), (0, 0)),
                )
        spread = spread + jnp.pad(slab, ((step_t, 2 - step_t), (0, 0), (0, 0), (0, 0)))
    inner = spread[:, :, 1 : WIDTH + 1]
    from_next = passed_along(inner[:, 0:1], "row", -1)
    from_prev = passed_along(inner[:, rows + 1 : rows + 2], "row", 1)
    center = inner[:, 1 : rows + 1]
    center = center.at[:, rows - 1 : rows].add(from_next)
    center = center.at[:, 0:1].add(from_prev)
    returned = passed_along(center[0:2], "tm", -1)
    grad_act = center[2:].at[frames - 2 :].add(returned).reshape(-1, CH)
    x_float = inputs.reshape(-1, CH).astype(jnp.float32)
    sigma = jax.nn.sigmoid(x_float)
    input_grad = (grad_act * sigma * (1.0 + x_float * (1.0 - sigma))).astype(jnp.bfloat16)
    local_filter = jnp.concatenate(blocks, 0).reshape(-1)
    frame_blocks = lax.axis_size("tm")
    row_blocks = lax.axis_size("row")
    scale = frames * frame_blocks * rows * row_blocks
    share = lax.psum_scatter(local_filter, ("tm", "row"), scatter_dimension=0, tiled=True)
    filter_grad = (share / scale).astype(jnp.bfloat16)
    shape = (frames, rows, WIDTH * CH)
    return (output.astype(jnp.bfloat16).reshape(shape), input_grad.reshape(shape), filter_grad)


def either(mesh, inputs, weight, cotangent):
    size = mesh.shape["row"]
    if mesh.shape["tm"] == 2 and size == 2 * PAIRS and inputs.shape[:2] == (2, 1):
        return fused(inputs, weight, cotangent)
    return on_device(inputs, weight, cotangent)


def solution(mesh):
    placed = (P(("grp", "tm"), "row", None), P(), P(("grp", "tm"), "row", None))
    return jax.shard_map(
        functools.partial(either, mesh),
        mesh=mesh,
        in_specs=placed,
        out_specs=(
            P(("grp", "tm"), "row", None),
            P(("grp", "tm"), "row", None),
            P(("grp", "tm", "row")),
        ),
        check_vma=False,
    )
```

```python
import functools

import jax
import jax.numpy as jnp
from jax import lax
from jax.experimental import pallas as pl
from jax.experimental.pallas import tpu as pltpu
from jax.sharding import PartitionSpec as P

CH = 192
WIDTH = 224
TAPS = 27
HALF = WIDTH // 2
LINES = WIDTH * CH // 128
PAIRS = 4
CHUNK = TAPS * CH // (4 * PAIRS)
TALL = CHUNK + 12
CUT = 176
PIECE = TALL + CUT
CUTS = 2
ORDER = ((3, 2, 1, 0), (0, 3, 2, 1), (0, 3, 1, 2), (0, 1, 2, 3))
PITCH = 256


def fused_kernel(
    scale, x_ref, w_ref, c_ref, out_ref, ig_ref, fg_ref,
    raw, weight_in, wide, factor, act, cot, fwd_even, fwd_odd, bwd_taps, act_t, shifted, filt,
    outgoing, passing, incoming, fwd, bwd, pad, sums,
    known, fetch_sem, send_sem, recv_sem, piece_send, pass_recv, piece_recv,
):
    f32, bf16 = jnp.float32, jnp.bfloat16
    grp, tm, row = lax.axis_index("grp"), lax.axis_index("tm"), lax.axis_index("row")
    pair, side = row // 2, row % 2
    own, other_slot = 1 + side, 2 - side

    def device(t, r):
        return (grp, t, r)

    barrier = pltpu.get_barrier_semaphore()

    def greet(target):
        pl.semaphore_signal(barrier, inc=1, device_id=target, device_id_type=pl.DeviceIdType.MESH)

    fetches = [
        pltpu.make_async_copy(src, dst, fetch_sem.at[i])
        for i, (src, dst) in enumerate(
            ((x_ref, raw.at[0, own, tm]), (c_ref, raw.at[1, own, tm]), (w_ref, weight_in))
        )
    ]
    sibling = device(1 - tm, row)
    partner = device(tm, 2 * pair + 1 - side)
    greet(sibling)
    greet(partner)
    has_before, has_after = pair > 0, pair < PAIRS - 1
    part = pair // 2
    inner = (pair + part) % 2 == 1
    mate_pair = pair + 1 - 2 * (pair % 2)
    stop, end = 2 - part, 3 * (1 - part)
    for step, present in ((-1, has_before), (1, has_after)):

        @pl.when(present)
        def _():
            greet(device(tm, 2 * (pair + step) + side))

    for fetch in fetches:
        fetch.start()

    def block(index):
        return pl.ds(pl.multiple_of(index * HALF, 16), HALF)

    lanes_used = iter(range(28))

    def move(array, src_slot, dst_slot, half, target):
        copies = []
        for k in range(2):
            span = pl.ds(k * LINES, LINES)
            src = (c_ref if array else x_ref) if src_slot is None else raw.at[array, src_slot, half]
            copies.append(
                pltpu.make_async_remote_copy(
                    src_ref=src.at[span],
                    dst_ref=raw.at[array, dst_slot, half, span],
                    send_sem=send_sem.at[next(lanes_used)],
                    recv_sem=recv_sem.at[array, dst_slot, half, k],
                    device_id=target,
                    device_id_type=pl.DeviceIdType.MESH,
                )
            )
        return copies

    def arrived(array, slot, half, k):
        ref = raw.at[array, slot, half, pl.ds(k * LINES, LINES)]
        pltpu.make_async_remote_copy(
            src_ref=ref,
            dst_ref=ref,
            send_sem=send_sem.at[0],
            recv_sem=recv_sem.at[array, slot, half, k],
            device_id=sibling,
            device_id_type=pl.DeviceIdType.MESH,
        ).wait_recv()

    outer_pair = pair + 2 * side - 1
    inner_pair = pair + 1 - 2 * side
    has_outer = jnp.logical_and(outer_pair >= 0, outer_pair < PAIRS)
    has_inner = jnp.logical_and(inner_pair >= 0, inner_pair < PAIRS)
    outer_same = device(tm, 2 * outer_pair + side)
    inner_same = device(tm, 2 * inner_pair + side)
    near_slot, far_slot = 3 * (1 - side), 3 * side

    to_partner = [move(i, None, own, tm, partner) for i in range(2)]
    to_sibling = [move(i, None, own, tm, sibling) for i in range(2)]
    outward = [move(i, None, near_slot, tm, outer_same) for i in range(2)]
    onward = [move(i, other_slot, other_slot, tm, sibling) for i in range(2)]
    relayed = move(0, other_slot, far_slot, tm, inner_same)
    across = move(1, near_slot, near_slot, tm, partner)
    near = move(0, near_slot, near_slot, tm, sibling)
    far = [move(i, far_slot, far_slot, tm, sibling) for i in range(2)]

    def expand(array, slot, half, keep=False):
        wide[array] = raw[array, slot, half].astype(f32)
        for j in range(3):
            for frame in range(2):
                value = wide[array, pl.ds(2 * j + frame, HALF, stride=6), :]
                if array == 0:
                    sigma = 1.0 / (1.0 + jnp.exp(-value))
                    if keep:
                        factor[j, frame] = sigma * (1.0 + value * (1.0 - sigma))
                    act[slot, j, block(2 * half + 2 + frame), :] = (value * sigma).astype(bf16)
                else:
                    cot[slot, j, block(2 * half + frame), :] = value.astype(bf16)

    def announce(target):
        pl.semaphore_signal(
            known, inc=1, device_id=device(tm, 2 * target + side), device_id_type=pl.DeviceIdType.MESH
        )

    pl.semaphore_wait(barrier, jnp.where(inner, 4, 3))

    @pl.when(inner)
    def _():
        announce(stop)

    for i in range(2):
        for k in range(2):
            to_partner[i][k].start()

        @pl.when(has_outer)
        def _():
            for k in range(2):
                outward[i][k].start()

        for k in range(2):
            to_sibling[i][k].start()

    for i in range(2):
        fetches[i].wait()
        expand(i, own, tm, keep=i == 0)

    for slot in range(4):
        act[slot, :, 0 : 2 * HALF, :] = jnp.zeros((3, 2 * HALF, 128), bf16)
        cot[slot, :, 4 * HALF : 6 * HALF, :] = jnp.zeros((3, 2 * HALF, 128), bf16)
        act_t[slot, :, 0 : 2 * PITCH] = jnp.zeros((CH, 2 * PITCH), bf16)

    for slot, present in ((0, has_before), (3, has_after)):

        @pl.when(jnp.logical_not(present))
        def _():
            act[slot, :, 2 * HALF : 6 * HALF, :] = jnp.zeros((3, 4 * HALF, 128), bf16)
            cot[slot, :, 0 : 4 * HALF, :] = jnp.zeros((3, 4 * HALF, 128), bf16)
            act_t[slot, :, 2 * PITCH : 6 * PITCH] = jnp.zeros((CH, 4 * PITCH), bf16)


    @pl.when(inner)
    def _():
        incoming[1:3] = jnp.zeros((2, PIECE, 128), bf16)

    @pl.when(jnp.logical_not(inner))
    def _():
        incoming[3] = jnp.zeros((PIECE, 128), bf16)

    pad[:, 0:8, :] = jnp.zeros((2, 8, CH), f32)
    pad[:, HALF + 8 : HALF + 16, :] = jnp.zeros((2, 8, CH), f32)
    for i in range(8):
        shifted[:, :, i * 128 + HALF : (i + 1) * 128, :] = jnp.zeros(
            (3, 2, 128 - HALF, CH), bf16
        )
    bwd_taps[:, 0:64, :] = jnp.zeros((TAPS, 64, CH), bf16)
    bwd_taps[:, 64 + CH : 128 + CH, :] = jnp.zeros((TAPS, 64, CH), bf16)

    fetches[2].wait()
    for tap in range(TAPS):
        value = weight_in[:, tap * CH : (tap + 1) * CH]
        fwd_even[tap] = jnp.concatenate([value, jnp.zeros((CH, 64), bf16)], axis=1)
        fwd_odd[tap] = jnp.concatenate([jnp.zeros((CH, 64), bf16), value], axis=1)
        bwd_taps[tap, 64 : 64 + CH, :] = value

    def transpose(slot, half):
        for frame in range(2):
            lane = (2 * half + 2 + frame) * PITCH
            even = pl.ds(pl.multiple_of(lane, 128), 128)
            odd = pl.ds(pl.multiple_of(lane + 128, 128), 128)

            def turned(j):
                value = act[slot, j, block(2 * half + 2 + frame), :]
                return jnp.concatenate([value, jnp.zeros((128 - HALF, 128), bf16)], axis=0).T

            act_t[slot, 0:128, even] = turned(0)
            both = turned(1)
            act_t[slot, 128:CH, even] = both[0:64]
            act_t[slot, 0:64, odd] = both[64:128]
            act_t[slot, 64:CH, odd] = turned(2)

    transpose(own, tm)

    def dots(ref, slot, starts, weights, out, first):
        def side_of(start, j):
            rows_of = pl.ds(pl.multiple_of(start, 16), 2 * HALF)
            return jnp.concatenate([ref[slot, j, rows_of, :], ref[slot, j + 1, rows_of, :]], axis=1)

        for i, terms in enumerate((((0, 1), (1, 2)), ((1, 1), (0, 0)), ((0, 2),), ((1, 0),))):
            total = None
            for step_t in range(3):
                for odd, step_w in terms:
                    more = weights(side_of(starts[step_t], odd), odd, step_t, step_w)
                    total = more if total is None else total + more
            if first:
                out[i] = total
            else:
                out[i] += total

    def convolve(act_h, cot_h, first):
        def forward(value, odd, step_t, step_w):
            taps = fwd_odd if odd else fwd_even
            return lax.dot_general(
                value,
                taps[(step_t * 3 + act_h) * 3 + step_w],
                (((1,), (1,)), ((), ())),
                preferred_element_type=f32,
            )

        def backward(value, odd, step_t, step_w):
            first_row = 0 if odd else 64
            return jnp.dot(
                value,
                bwd_taps[(step_t * 3 + cot_h) * 3 + 2 - step_w, first_row : first_row + 256, :],
                preferred_element_type=f32,
            )

        starts = [(2 * tm + step_t) * HALF for step_t in range(3)]
        dots(act, side + act_h, starts, forward, fwd, first)
        dots(cot, side + 2 - cot_h, starts[::-1], backward, bwd, first)

    def shift(h, half):
        for frame in range(2):
            rows_of = block(2 * half + frame)
            mid = cot[1 + h, 1, rows_of, :]
            even = jnp.concatenate([cot[1 + h, 0, rows_of, :], mid[:, 0:64]], axis=1)
            odd = jnp.concatenate([mid[:, 64:128], cot[1 + h, 2, rows_of, :]], axis=1)
            pad[0, 8 : HALF + 8, :] = even.astype(f32)
            pad[1, 8 : HALF + 8, :] = odd.astype(f32)
            first, second = (
                pl.ds(pl.multiple_of((2 * half + frame) * PITCH + i * 128, 128), HALF)
                for i in range(2)
            )
            shifted[0, h, first, :] = odd
            shifted[0, h, second, :] = pad[0, 9 : HALF + 9, :].astype(bf16)
            shifted[1, h, first, :] = even
            shifted[1, h, second, :] = odd
            shifted[2, h, first, :] = pad[1, 7 : HALF + 7, :].astype(bf16)
            shifted[2, h, second, :] = even

    def complete(array, slot, half):
        for k in range(2):
            arrived(array, slot, half, k)
        expand(array, slot, half)
        if array == 0:
            transpose(slot, half)

    complete(0, own, 1 - tm)
    complete(1, own, 1 - tm)

    @pl.when(inner)
    def _():
        pl.semaphore_wait(known, 1)
        announce(mate_pair)


    def pass_on(array, slot, k, copies):
        arrived(array, slot, tm, k)
        for copy in copies:
            copy[k].start()

    def pass_other(k):
        pass_on(0, other_slot, k, [])

        @pl.when(has_inner)
        def _():
            relayed[k].start()

        onward[0][k].start()

    pass_other(0)
    pass_other(1)
    expand(0, other_slot, tm)
    transpose(other_slot, tm)

    @pl.when(has_inner)
    def _():
        for k in range(2):
            pass_on(0, near_slot, k, [near])
        expand(0, near_slot, tm)
        transpose(near_slot, tm)

    for half in range(2):
        shift(side, half)
    complete(0, other_slot, 1 - tm)

    @pl.when(has_inner)
    def _():
        complete(0, near_slot, 1 - tm)

    for k in range(2):
        pass_on(1, other_slot, k, [onward[1]])

        @pl.when(has_outer)
        def _():
            pass_on(0, far_slot, k, [far[0]])

        @pl.when(has_inner)
        def _():
            pass_on(1, near_slot, k, [across])

    @pl.when(has_outer)
    def _():
        expand(0, far_slot, tm)
        transpose(far_slot, tm)

    expand(1, other_slot, tm)
    shift(1 - side, tm)

    @pl.when(has_outer)
    def _():
        complete(0, far_slot, 1 - tm)

    def at_pair(values):
        chosen = jnp.int32(values[0])
        for p in range(1, PAIRS):
            chosen = jnp.where(pair == p, jnp.int32(values[p]), chosen)
        return chosen

    owners = tuple(at_pair([ORDER[p][k] for p in range(PAIRS)]) for k in range(PAIRS))

    def shard(owner):
        return tm * 2 * PAIRS + 2 * owner + side

    def filter_sum(k, late=None):
        first_block = shard(owners[k]) * CHUNK // 16
        first_tap = first_block // (CH // 16)
        base = pl.multiple_of(first_block % (CH // 16) * 16, 16)

        def over(tap, i, half, frames):
            step_t, step_h, step_w = tap // 9, tap // 3 % 3, tap % 3
            lanes = pl.ds(pl.multiple_of((step_t + 2 * half) * PITCH, 128), frames * PITCH)
            rows_of = pl.ds(pl.multiple_of(2 * half * PITCH, 16), frames * PITCH)
            return jnp.dot(
                act_t[step_h + i, :, lanes],
                shifted[step_w, i, rows_of, :],
                preferred_element_type=f32,
            )

        def term(n):
            tap = first_tap + n
            span = slice(n * CH, (n + 1) * CH)
            if late is None:
                filt[k, span, :] = over(tap, 0, 0, 4) + over(tap, 1, 0, 4)
            elif late:
                filt[k, span, :] += over(tap, 1 - side, 1 - tm, 2)
            else:
                filt[k, span, :] = over(tap, side, 0, 4) + over(tap, 1 - side, tm, 2)

        term(0)
        term(1)

        @pl.when(base + TALL > 2 * CH)
        def _():
            term(2)

        return base

    filter_sum(0, late=False)
    complete(1, other_slot, 1 - tm)
    shift(1 - side, 1 - tm)


    def folded(k, base):
        high = filt[k, pl.ds(base, TALL), 128:CH]
        return jnp.concatenate(
            [
                filt[k, pl.ds(base, TALL), 0:128],
                jnp.concatenate(
                    [
                        high[0:CUT],
                        jnp.concatenate([high[CUT:TALL], jnp.zeros((2 * CUT - TALL, 64), f32)], axis=0),
                    ],
                    axis=1,
                ),
            ],
            axis=0,
        )

    def piece(k, ref, slot, recv, owner, part_of=None):
        src, dst, sem = outgoing.at[k], ref.at[slot], recv.at[slot]
        if part_of is not None:
            span = pl.ds(part_of * (PIECE // CUTS), PIECE // CUTS)
            src, dst, sem = src.at[span], dst.at[span], recv.at[slot + part_of]
        return pltpu.make_async_remote_copy(
            src_ref=src,
            dst_ref=dst,
            send_sem=piece_send.at[CUTS * k + (part_of or 0)],
            recv_sem=sem,
            device_id=device(tm, 2 * owner + side),
            device_id_type=pl.DeviceIdType.MESH,
        )

    def pieces_of(p, k):
        mate, owner = p + 1 - 2 * (p % 2), ORDER[p][k]
        if owner == mate:
            return [piece(k, incoming, 0, piece_recv, mate)]
        if owner in (0, 3):
            return [piece(k, incoming, 2 if p in (1, 2) else 1, piece_recv, owner)]
        if p in (1, 2):
            return [piece(k, incoming, 3, piece_recv, owner, i) for i in range(CUTS)]
        return [piece(k, passing, 0, pass_recv, mate, i) for i in range(CUTS)]

    bases = [filter_sum(0, late=True)]
    for k in range(4):
        if k > 0:
            bases.append(filter_sum(k))
        if k == 3:
            break
        outgoing[k] = folded(k, bases[k]).astype(bf16)
        for p in range(PAIRS):
            if p in (1, 2) and k == 2:
                continue

            @pl.when(pair == p)
            def _():
                if p in (0, 3) and ORDER[p][k] == 3 - p:
                    pl.semaphore_wait(known, 1)
                for copy in pieces_of(p, k):
                    copy.start()

        if k == 0:
            convolve(1, 1, True)
        if k == 1:

            @pl.when(has_outer)
            def _():
                for part_of in range(2):
                    pass_on(1, far_slot, part_of, [far[1]])
                expand(1, far_slot, tm)

    convolve(2 - 2 * side, 2 * side, False)

    @pl.when(has_outer)
    def _():
        for k in range(2):
            arrived(1, far_slot, 1 - tm, k)
        expand(1, far_slot, 1 - tm)

    @pl.when(inner)
    def _():
        mine = folded(2, bases[2])
        for i in range(CUTS):
            piece(2, passing, 0, pass_recv, mate_pair, i).wait_recv()
            span = slice(i * (PIECE // CUTS), (i + 1) * (PIECE // CUTS))
            outgoing[2, span, :] = (mine[span] + passing[0, span, :].astype(f32)).astype(bf16)
            piece(2, incoming, 3, piece_recv, stop, i).start()

    convolve(2 * side, 2 - 2 * side, False)

    def finish(total, slot, weighted):
        for frame in range(2):
            span = slice(frame * HALF, (frame + 1) * HALF)
            pad[0, 8 : HALF + 8, :] = total[3, span, :]
            pad[1, 8 : HALF + 8, :] = total[2, span, :]
            even = total[0, span, :] + pad[0, 7 : HALF + 7, :]
            odd = total[1, span, :] + pad[1, 9 : HALF + 9, :]
            lanes = (
                even[:, 0:128],
                jnp.concatenate([even[:, 128:CH], odd[:, 0:64]], axis=1),
                odd[:, 64:CH],
            )
            for j in range(3):
                value = lanes[j] * factor[j, frame] if weighted else lanes[j]
                wide[slot, pl.ds(2 * j + frame, HALF, stride=6), :] = value

    finish(fwd, 0, False)
    out_ref[...] = wide[0].astype(bf16)
    finish(bwd, 1, True)
    ig_ref[...] = wide[1].astype(bf16)

    piece(0, incoming, 0, piece_recv, mate_pair).wait_recv()
    total = folded(3, bases[3]) + incoming[0].astype(f32)

    @pl.when(inner)
    def _():
        for i in range(CUTS):
            piece(0, incoming, 3, piece_recv, stop, i).wait_recv()

    @pl.when(jnp.logical_not(inner))
    def _():
        for slot in range(1, 3):
            piece(0, incoming, slot, piece_recv, mate_pair).wait_recv()

    for i in range(1, 4):
        total = total + incoming[i].astype(f32)
    total = total * (1.0 / scale)
    sums[0, 0:TALL, :] = total[0:TALL]
    sums[1, 0:CUT, 0:64] = total[TALL:PIECE, 0:64]
    sums[1, CUT:TALL, 0:64] = total[TALL : 2 * TALL - CUT, 64:128]
    for q in range(4):

        @pl.when(shard(pair) % 4 == q)
        def _():
            even, odd = (pl.ds(4 * q + i, CHUNK // 2, stride=2) for i in range(2))
            low = sums[0, odd, :]
            lanes = (
                sums[0, even, :],
                jnp.concatenate([sums[1, even, :][:, 0:64], low[:, 0:64]], axis=1),
                jnp.concatenate([low[:, 64:128], sums[1, odd, :][:, 0:64]], axis=1),
            )
            for j in range(3):
                wide[0, pl.ds(j, CHUNK // 2, stride=3), :] = lanes[j]

    fg_ref[...] = wide[0, 0 : CHUNK // 2 * 3, :].astype(bf16)

    for copies in to_partner + to_sibling + onward:
        for copy in copies:
            copy.wait_send()

    @pl.when(has_outer)
    def _():
        for copies in outward + far:
            for copy in copies:
                copy.wait_send()

    @pl.when(has_inner)
    def _():
        for copy in near + relayed + across:
            copy.wait_send()

    for p in range(PAIRS):

        @pl.when(pair == p)
        def _():
            for k in range(3):
                for copy in pieces_of(p, k):
                    copy.wait_send()


def hand_over(*refs):
    copies = [
        pltpu.make_async_copy(refs[i], refs[3 + i], refs[6].at[i]) for i in range(3)
    ]
    for copy in copies:
        copy.start()
    for copy in copies:
        copy.wait()


def fused(inputs, weight, cotangent):
    frames, rows = inputs.shape[:2]
    scale = frames * lax.axis_size("tm") * rows * lax.axis_size("row")
    lines = WIDTH * CH // 128
    vmem, hbm = (pl.BlockSpec(memory_space=m) for m in (pltpu.VMEM, pltpu.HBM))
    bf16, f32 = jnp.bfloat16, jnp.float32

    def interleaved(array):
        return array.reshape(2, lines, 128).transpose(1, 0, 2).reshape(2 * lines, 128)

    def parted(array):
        return array.reshape(lines, 2, 128).transpose(1, 0, 2).reshape(2, 1, lines * 128)

    out, ig, fg = pl.pallas_call(
        functools.partial(fused_kernel, float(scale)),
        out_shape=(
            jax.ShapeDtypeStruct((2 * lines, 128), bf16),
            jax.ShapeDtypeStruct((2 * lines, 128), bf16),
            jax.ShapeDtypeStruct((CHUNK // 2 * 3, 128), bf16),
        ),
        in_specs=[hbm, hbm, hbm],
        out_specs=(vmem, vmem, vmem),
        scratch_shapes=[
            pltpu.VMEM((2, 4, 2, 2 * lines, 128), bf16),
            pltpu.VMEM((CH, TAPS * CH), bf16),
            pltpu.VMEM((2, 2 * lines, 128), f32),
            pltpu.VMEM((3, 2, HALF, 128), f32),
            pltpu.VMEM((4, 3, 6 * HALF, 128), bf16),
            pltpu.VMEM((4, 3, 6 * HALF, 128), bf16),
            pltpu.VMEM((TAPS, CH, 256), bf16),
            pltpu.VMEM((TAPS, CH, 256), bf16),
            pltpu.VMEM((TAPS, CH + 128, CH), bf16),
            pltpu.VMEM((4, CH, 6 * PITCH), bf16),
            pltpu.VMEM((3, 2, 4 * PITCH, CH), bf16),
            pltpu.VMEM((4, 3 * CH, CH), f32),
            pltpu.VMEM((3, PIECE, 128), bf16),
            pltpu.VMEM((1, PIECE, 128), bf16),
            pltpu.VMEM((4, PIECE, 128), bf16),
            pltpu.VMEM((4, 2 * HALF, CH), f32),
            pltpu.VMEM((4, 2 * HALF, CH), f32),
            pltpu.VMEM((2, HALF + 16, CH), f32),
            pltpu.VMEM((2, TALL, 128), f32),
            pltpu.SemaphoreType.REGULAR,
            pltpu.SemaphoreType.DMA((3,)),
            pltpu.SemaphoreType.DMA((28,)),
            pltpu.SemaphoreType.DMA((2, 4, 2, 2)),
            pltpu.SemaphoreType.DMA((3 * CUTS,)),
            pltpu.SemaphoreType.DMA((CUTS,)),
            pltpu.SemaphoreType.DMA((3 + CUTS,)),
        ],
        compiler_params=pltpu.CompilerParams(
            collective_id=0, has_side_effects=True, vmem_limit_bytes=int(53.4 * 1024 * 1024)
        ),
    )(interleaved(inputs), weight.T, interleaved(cotangent))
    results = (out, ig, fg)
    out, ig, fg = pl.pallas_call(
        hand_over,
        out_shape=tuple(jax.ShapeDtypeStruct(r.shape, r.dtype) for r in results),
        in_specs=[pl.BlockSpec(memory_space=pl.ANY)] * 3,
        out_specs=(hbm, hbm, hbm),
        scratch_shapes=[pltpu.SemaphoreType.DMA((3,))],
        compiler_params=pltpu.CompilerParams(vmem_limit_bytes=1024 * 1024),
    )(*results)
    return parted(out), parted(ig), fg.reshape(-1)


def passed_along(array, axis, by):
    length = lax.axis_size(axis)
    pairs = [(i, i + by) for i in range(length) if 0 <= i + by < length]
    return lax.ppermute(array, axis, pairs)


def with_halo(array, sides, width):
    for axis, dim in sides:
        size, length = (lax.axis_size(axis), array.shape[dim])
        up = [(i, (i + 1) % size) for i in range(size - 1)]
        down = [(j, i) for i, j in up]
        last = lax.slice_in_dim(array, length - width, length, axis=dim)
        first = lax.slice_in_dim(array, 0, width, axis=dim)
        before = lax.ppermute(last, axis, up)
        after = lax.ppermute(first, axis, down)
        array = jnp.concatenate([before, array, after], axis=dim)
    return array


def on_device(inputs, weight, cotangent):
    frames = inputs.shape[0]
    rows = inputs.shape[1]
    act = jax.nn.silu(inputs.astype(jnp.float32)).astype(jnp.bfloat16)
    earlier = passed_along(act, "tm", 1)
    extended = jnp.concatenate([earlier, act], 0)
    extended = with_halo(extended, (("row", 1),), 1)
    extended = extended.reshape(frames + 2, rows + 2, WIDTH, CH)
    act_pad = jnp.pad(extended, ((0, 0), (0, 0), (1, 1), (0, 0)))
    cot_four = cotangent.reshape(frames, rows, WIDTH, CH)
    cot_flat = cot_four.reshape(-1, CH)
    output = jnp.zeros((frames * rows * WIDTH, CH), jnp.float32)
    blocks = []
    for step_t in range(3):
        for step_h in range(3):
            for step_w in range(3):
                offset = ((step_t * 3 + step_h) * 3 + step_w) * CH
                kernel = weight[offset : offset + CH]
                piece = act_pad[
                    step_t : step_t + frames, step_h : step_h + rows, step_w : step_w + WIDTH
                ].reshape(-1, CH)
                output = output + jnp.dot(piece, kernel, preferred_element_type=jnp.float32)
                blocks.append(
                    lax.dot_general(
                        piece,
                        cot_flat,
                        (((0,), (0,)), ((), ())),
                        preferred_element_type=jnp.float32,
                    )
                )
    spread = jnp.zeros((frames + 2, rows + 2, WIDTH + 2, CH), jnp.float32)
    for step_t in range(3):
        slab_weight = weight[step_t * 9 * CH : (step_t + 1) * 9 * CH]
        terms = lax.dot_general(
            cot_flat, slab_weight, (((1,), (1,)), ((), ())), preferred_element_type=jnp.float32
        )
        terms = terms.reshape(frames, rows, WIDTH, 9, CH)
        slab = jnp.zeros((frames, rows + 2, WIDTH + 2, CH), jnp.float32)
        for step_h in range(3):
            for step_w in range(3):
                slab = slab + jnp.pad(
                    terms[:, :, :, step_h * 3 + step_w],
                    ((0, 0), (step_h, 2 - step_h), (step_w, 2 - step_w), (0, 0)),
                )
        spread = spread + jnp.pad(slab, ((step_t, 2 - step_t), (0, 0), (0, 0), (0, 0)))
    inner = spread[:, :, 1 : WIDTH + 1]
    from_next = passed_along(inner[:, 0:1], "row", -1)
    from_prev = passed_along(inner[:, rows + 1 : rows + 2], "row", 1)
    center = inner[:, 1 : rows + 1]
    center = center.at[:, rows - 1 : rows].add(from_next)
    center = center.at[:, 0:1].add(from_prev)
    returned = passed_along(center[0:2], "tm", -1)
    grad_act = center[2:].at[frames - 2 :].add(returned).reshape(-1, CH)
    x_float = inputs.reshape(-1, CH).astype(jnp.float32)
    sigma = jax.nn.sigmoid(x_float)
    input_grad = (grad_act * sigma * (1.0 + x_float * (1.0 - sigma))).astype(jnp.bfloat16)
    local_filter = jnp.concatenate(blocks, 0).reshape(-1)
    frame_blocks = lax.axis_size("tm")
    row_blocks = lax.axis_size("row")
    scale = frames * frame_blocks * rows * row_blocks
    share = lax.psum_scatter(local_filter, ("tm", "row"), scatter_dimension=0, tiled=True)
    filter_grad = (share / scale).astype(jnp.bfloat16)
    shape = (frames, rows, WIDTH * CH)
    return (output.astype(jnp.bfloat16).reshape(shape), input_grad.reshape(shape), filter_grad)


def either(mesh, inputs, weight, cotangent):
    size = mesh.shape["row"]
    if mesh.shape["tm"] == 2 and size == 2 * PAIRS and inputs.shape[:2] == (2, 1):
        return fused(inputs, weight, cotangent)
    return on_device(inputs, weight, cotangent)


def solution(mesh):
    placed = (P(("grp", "tm"), "row", None), P(), P(("grp", "tm"), "row", None))
    return jax.shard_map(
        functools.partial(either, mesh),
        mesh=mesh,
        in_specs=placed,
        out_specs=(
            P(("grp", "tm"), "row", None),
            P(("grp", "tm"), "row", None),
            P(("grp", "tm", "row")),
        ),
        check_vma=False,
    )
```

```python
import functools

import jax
import jax.numpy as jnp
from jax import lax
from jax.experimental import pallas as pl
from jax.experimental.pallas import tpu as pltpu
from jax.sharding import PartitionSpec as P

CH = 192
WIDTH = 224
TAPS = 27
HALF = WIDTH // 2
LINES = WIDTH * CH // 128
PAIRS = 4
CHUNK = TAPS * CH // (4 * PAIRS)
TALL = CHUNK + 12
CUT = 176
PIECE = TALL + CUT
CUTS = 4
ORDER = ((3, 2, 1, 0), (0, 3, 2, 1), (0, 3, 1, 2), (0, 1, 2, 3))
PITCH = 256


def fused_kernel(
    scale, x_ref, w_ref, c_ref, out_ref, ig_ref, fg_ref,
    raw, weight_in, wide, factor, act, cot, fwd_even, fwd_odd, bwd_taps, act_t, shifted, filt,
    outgoing, passing, incoming, fwd, bwd, pad, sums,
    known, fetch_sem, send_sem, recv_sem, piece_send, pass_recv, piece_recv,
):
    f32, bf16 = jnp.float32, jnp.bfloat16
    grp, tm, row = lax.axis_index("grp"), lax.axis_index("tm"), lax.axis_index("row")
    pair, side = row // 2, row % 2
    own, other_slot = 1 + side, 2 - side

    def device(t, r):
        return (grp, t, r)

    barrier = pltpu.get_barrier_semaphore()

    def greet(target):
        pl.semaphore_signal(barrier, inc=1, device_id=target, device_id_type=pl.DeviceIdType.MESH)

    fetches = [
        pltpu.make_async_copy(src, dst, fetch_sem.at[i])
        for i, (src, dst) in enumerate(
            ((x_ref, raw.at[0, own, tm]), (c_ref, raw.at[1, own, tm]), (w_ref, weight_in))
        )
    ]
    sibling = device(1 - tm, row)
    partner = device(tm, 2 * pair + 1 - side)
    greet(sibling)
    greet(partner)
    has_before, has_after = pair > 0, pair < PAIRS - 1
    part = pair // 2
    inner = (pair + part) % 2 == 1
    mate_pair = pair + 1 - 2 * (pair % 2)
    stop, end = 2 - part, 3 * (1 - part)
    for step, present in ((-1, has_before), (1, has_after)):

        @pl.when(present)
        def _():
            greet(device(tm, 2 * (pair + step) + side))

    for fetch in fetches:
        fetch.start()

    def block(index):
        return pl.ds(pl.multiple_of(index * HALF, 16), HALF)

    lanes_used = iter(range(28))

    def move(array, src_slot, dst_slot, half, target):
        copies = []
        for k in range(2):
            span = pl.ds(k * LINES, LINES)
            src = (c_ref if array else x_ref) if src_slot is None else raw.at[array, src_slot, half]
            copies.append(
                pltpu.make_async_remote_copy(
                    src_ref=src.at[span],
                    dst_ref=raw.at[array, dst_slot, half, span],
                    send_sem=send_sem.at[next(lanes_used)],
                    recv_sem=recv_sem.at[array, dst_slot, half, k],
                    device_id=target,
                    device_id_type=pl.DeviceIdType.MESH,
                )
            )
        return copies

    def arrived(array, slot, half, k):
        ref = raw.at[array, slot, half, pl.ds(k * LINES, LINES)]
        pltpu.make_async_remote_copy(
            src_ref=ref,
            dst_ref=ref,
            send_sem=send_sem.at[0],
            recv_sem=recv_sem.at[array, slot, half, k],
            device_id=sibling,
            device_id_type=pl.DeviceIdType.MESH,
        ).wait_recv()

    outer_pair = pair + 2 * side - 1
    inner_pair = pair + 1 - 2 * side
    has_outer = jnp.logical_and(outer_pair >= 0, outer_pair < PAIRS)
    has_inner = jnp.logical_and(inner_pair >= 0, inner_pair < PAIRS)
    outer_same = device(tm, 2 * outer_pair + side)
    inner_same = device(tm, 2 * inner_pair + side)
    near_slot, far_slot = 3 * (1 - side), 3 * side

    to_partner = [move(i, None, own, tm, partner) for i in range(2)]
    to_sibling = [move(i, None, own, tm, sibling) for i in range(2)]
    outward = [move(i, None, near_slot, tm, outer_same) for i in range(2)]
    onward = [move(i, other_slot, other_slot, tm, sibling) for i in range(2)]
    relayed = move(0, other_slot, far_slot, tm, inner_same)
    across = move(1, near_slot, near_slot, tm, partner)
    near = move(0, near_slot, near_slot, tm, sibling)
    far = [move(i, far_slot, far_slot, tm, sibling) for i in range(2)]

    def expand(array, slot, half, keep=False):
        wide[array] = raw[array, slot, half].astype(f32)
        for j in range(3):
            for frame in range(2):
                value = wide[array, pl.ds(2 * j + frame, HALF, stride=6), :]
                if array == 0:
                    sigma = 1.0 / (1.0 + jnp.exp(-value))
                    if keep:
                        factor[j, frame] = sigma * (1.0 + value * (1.0 - sigma))
                    act[slot, j, block(2 * half + 2 + frame), :] = (value * sigma).astype(bf16)
                else:
                    cot[slot, j, block(2 * half + frame), :] = value.astype(bf16)

    def announce(target):
        pl.semaphore_signal(
            known, inc=1, device_id=device(tm, 2 * target + side), device_id_type=pl.DeviceIdType.MESH
        )

    pl.semaphore_wait(barrier, jnp.where(inner, 4, 3))

    @pl.when(inner)
    def _():
        announce(stop)

    for i in range(2):
        for k in range(2):
            to_partner[i][k].start()

        @pl.when(has_outer)
        def _():
            for k in range(2):
                outward[i][k].start()

        for k in range(2):
            to_sibling[i][k].start()

    for i in range(2):
        fetches[i].wait()
        expand(i, own, tm, keep=i == 0)

    for slot in range(4):
        act[slot, :, 0 : 2 * HALF, :] = jnp.zeros((3, 2 * HALF, 128), bf16)
        cot[slot, :, 4 * HALF : 6 * HALF, :] = jnp.zeros((3, 2 * HALF, 128), bf16)
        act_t[slot, :, 0 : 2 * PITCH] = jnp.zeros((CH, 2 * PITCH), bf16)

    for slot, present in ((0, has_before), (3, has_after)):

        @pl.when(jnp.logical_not(present))
        def _():
            act[slot, :, 2 * HALF : 6 * HALF, :] = jnp.zeros((3, 4 * HALF, 128), bf16)
            cot[slot, :, 0 : 4 * HALF, :] = jnp.zeros((3, 4 * HALF, 128), bf16)
            act_t[slot, :, 2 * PITCH : 6 * PITCH] = jnp.zeros((CH, 4 * PITCH), bf16)


    @pl.when(inner)
    def _():
        incoming[1:3] = jnp.zeros((2, PIECE, 128), bf16)

    @pl.when(jnp.logical_not(inner))
    def _():
        incoming[3] = jnp.zeros((PIECE, 128), bf16)

    pad[:, 0:8, :] = jnp.zeros((2, 8, CH), f32)
    pad[:, HALF + 8 : HALF + 16, :] = jnp.zeros((2, 8, CH), f32)
    for i in range(8):
        shifted[:, :, i * 128 + HALF : (i + 1) * 128, :] = jnp.zeros(
            (3, 2, 128 - HALF, CH), bf16
        )
    bwd_taps[:, 0:64, :] = jnp.zeros((TAPS, 64, CH), bf16)
    bwd_taps[:, 64 + CH : 128 + CH, :] = jnp.zeros((TAPS, 64, CH), bf16)

    fetches[2].wait()
    for tap in range(TAPS):
        value = weight_in[:, tap * CH : (tap + 1) * CH]
        fwd_even[tap] = jnp.concatenate([value, jnp.zeros((CH, 64), bf16)], axis=1)
        fwd_odd[tap] = jnp.concatenate([jnp.zeros((CH, 64), bf16), value], axis=1)
        bwd_taps[tap, 64 : 64 + CH, :] = value

    def transpose(slot, half):
        for frame in range(2):
            lane = (2 * half + 2 + frame) * PITCH
            even = pl.ds(pl.multiple_of(lane, 128), 128)
            odd = pl.ds(pl.multiple_of(lane + 128, 128), 128)

            def turned(j):
                value = act[slot, j, block(2 * half + 2 + frame), :]
                return jnp.concatenate([value, jnp.zeros((128 - HALF, 128), bf16)], axis=0).T

            act_t[slot, 0:128, even] = turned(0)
            both = turned(1)
            act_t[slot, 128:CH, even] = both[0:64]
            act_t[slot, 0:64, odd] = both[64:128]
            act_t[slot, 64:CH, odd] = turned(2)

    transpose(own, tm)

    def dots(ref, slot, starts, weights, out, first):
        def side_of(start, j):
            rows_of = pl.ds(pl.multiple_of(start, 16), 2 * HALF)
            return jnp.concatenate([ref[slot, j, rows_of, :], ref[slot, j + 1, rows_of, :]], axis=1)

        for i, terms in enumerate((((0, 1), (1, 2)), ((1, 1), (0, 0)), ((0, 2),), ((1, 0),))):
            total = None
            for step_t in range(3):
                for odd, step_w in terms:
                    more = weights(side_of(starts[step_t], odd), odd, step_t, step_w)
                    total = more if total is None else total + more
            if first:
                out[i] = total
            else:
                out[i] += total

    def convolve(act_h, cot_h, first):
        def forward(value, odd, step_t, step_w):
            taps = fwd_odd if odd else fwd_even
            return lax.dot_general(
                value,
                taps[(step_t * 3 + act_h) * 3 + step_w],
                (((1,), (1,)), ((), ())),
                preferred_element_type=f32,
            )

        def backward(value, odd, step_t, step_w):
            first_row = 0 if odd else 64
            return jnp.dot(
                value,
                bwd_taps[(step_t * 3 + cot_h) * 3 + 2 - step_w, first_row : first_row + 256, :],
                preferred_element_type=f32,
            )

        starts = [(2 * tm + step_t) * HALF for step_t in range(3)]
        dots(act, side + act_h, starts, forward, fwd, first)
        dots(cot, side + 2 - cot_h, starts[::-1], backward, bwd, first)

    def shift(h, half):
        for frame in range(2):
            rows_of = block(2 * half + frame)
            mid = cot[1 + h, 1, rows_of, :]
            even = jnp.concatenate([cot[1 + h, 0, rows_of, :], mid[:, 0:64]], axis=1)
            odd = jnp.concatenate([mid[:, 64:128], cot[1 + h, 2, rows_of, :]], axis=1)
            pad[0, 8 : HALF + 8, :] = even.astype(f32)
            pad[1, 8 : HALF + 8, :] = odd.astype(f32)
            first, second = (
                pl.ds(pl.multiple_of((2 * half + frame) * PITCH + i * 128, 128), HALF)
                for i in range(2)
            )
            shifted[0, h, first, :] = odd
            shifted[0, h, second, :] = pad[0, 9 : HALF + 9, :].astype(bf16)
            shifted[1, h, first, :] = even
            shifted[1, h, second, :] = odd
            shifted[2, h, first, :] = pad[1, 7 : HALF + 7, :].astype(bf16)
            shifted[2, h, second, :] = even

    def complete(array, slot, half):
        for k in range(2):
            arrived(array, slot, half, k)
        expand(array, slot, half)
        if array == 0:
            transpose(slot, half)

    complete(0, own, 1 - tm)
    complete(1, own, 1 - tm)

    @pl.when(inner)
    def _():
        pl.semaphore_wait(known, 1)
        announce(mate_pair)


    def pass_on(array, slot, k, copies):
        arrived(array, slot, tm, k)
        for copy in copies:
            copy[k].start()

    def pass_other(k):
        pass_on(0, other_slot, k, [])

        @pl.when(has_inner)
        def _():
            relayed[k].start()

        onward[0][k].start()

    pass_other(0)
    pass_other(1)
    expand(0, other_slot, tm)
    transpose(other_slot, tm)

    @pl.when(has_inner)
    def _():
        for k in range(2):
            pass_on(0, near_slot, k, [near])
        expand(0, near_slot, tm)
        transpose(near_slot, tm)

    for half in range(2):
        shift(side, half)
    complete(0, other_slot, 1 - tm)

    @pl.when(has_inner)
    def _():
        complete(0, near_slot, 1 - tm)

    for k in range(2):
        pass_on(1, other_slot, k, [onward[1]])

        @pl.when(has_outer)
        def _():
            pass_on(0, far_slot, k, [far[0]])

        @pl.when(has_inner)
        def _():
            pass_on(1, near_slot, k, [across])

    @pl.when(has_outer)
    def _():
        expand(0, far_slot, tm)
        transpose(far_slot, tm)

    expand(1, other_slot, tm)
    shift(1 - side, tm)

    @pl.when(has_outer)
    def _():
        complete(0, far_slot, 1 - tm)

    def at_pair(values):
        chosen = jnp.int32(values[0])
        for p in range(1, PAIRS):
            chosen = jnp.where(pair == p, jnp.int32(values[p]), chosen)
        return chosen

    owners = tuple(at_pair([ORDER[p][k] for p in range(PAIRS)]) for k in range(PAIRS))

    def shard(owner):
        return tm * 2 * PAIRS + 2 * owner + side

    def filter_sum(k, late=None):
        first_block = shard(owners[k]) * CHUNK // 16
        first_tap = first_block // (CH // 16)
        base = pl.multiple_of(first_block % (CH // 16) * 16, 16)

        def over(tap, i, half, frames):
            step_t, step_h, step_w = tap // 9, tap // 3 % 3, tap % 3
            lanes = pl.ds(pl.multiple_of((step_t + 2 * half) * PITCH, 128), frames * PITCH)
            rows_of = pl.ds(pl.multiple_of(2 * half * PITCH, 16), frames * PITCH)
            return jnp.dot(
                act_t[step_h + i, :, lanes],
                shifted[step_w, i, rows_of, :],
                preferred_element_type=f32,
            )

        def term(n):
            tap = first_tap + n
            span = slice(n * CH, (n + 1) * CH)
            if late is None:
                filt[k, span, :] = over(tap, 0, 0, 4) + over(tap, 1, 0, 4)
            elif late:
                filt[k, span, :] += over(tap, 1 - side, 1 - tm, 2)
            else:
                filt[k, span, :] = over(tap, side, 0, 4) + over(tap, 1 - side, tm, 2)

        term(0)
        term(1)

        @pl.when(base + TALL > 2 * CH)
        def _():
            term(2)

        return base

    filter_sum(0, late=False)
    complete(1, other_slot, 1 - tm)
    shift(1 - side, 1 - tm)


    def folded(k, base):
        high = filt[k, pl.ds(base, TALL), 128:CH]
        return jnp.concatenate(
            [
                filt[k, pl.ds(base, TALL), 0:128],
                jnp.concatenate(
                    [
                        high[0:CUT],
                        jnp.concatenate([high[CUT:TALL], jnp.zeros((2 * CUT - TALL, 64), f32)], axis=0),
                    ],
                    axis=1,
                ),
            ],
            axis=0,
        )

    def piece(k, ref, slot, recv, owner, part_of=None):
        src, dst, sem = outgoing.at[k], ref.at[slot], recv.at[slot]
        if part_of is not None:
            span = pl.ds(part_of * (PIECE // CUTS), PIECE // CUTS)
            src, dst, sem = src.at[span], dst.at[span], recv.at[slot + part_of]
        return pltpu.make_async_remote_copy(
            src_ref=src,
            dst_ref=dst,
            send_sem=piece_send.at[CUTS * k + (part_of or 0)],
            recv_sem=sem,
            device_id=device(tm, 2 * owner + side),
            device_id_type=pl.DeviceIdType.MESH,
        )

    def pieces_of(p, k):
        mate, owner = p + 1 - 2 * (p % 2), ORDER[p][k]
        if owner == mate:
            return [piece(k, incoming, 0, piece_recv, mate)]
        if owner in (0, 3):
            return [piece(k, incoming, 2 if p in (1, 2) else 1, piece_recv, owner)]
        if p in (1, 2):
            return [piece(k, incoming, 3, piece_recv, owner, i) for i in range(CUTS)]
        return [piece(k, passing, 0, pass_recv, mate, i) for i in range(CUTS)]

    bases = [filter_sum(0, late=True)]
    for k in range(4):
        if k > 0:
            bases.append(filter_sum(k))
        if k == 3:
            break
        outgoing[k] = folded(k, bases[k]).astype(bf16)
        for p in range(PAIRS):
            if p in (1, 2) and k == 2:
                continue

            @pl.when(pair == p)
            def _():
                if p in (0, 3) and ORDER[p][k] == 3 - p:
                    pl.semaphore_wait(known, 1)
                for copy in pieces_of(p, k):
                    copy.start()

        if k == 0:
            convolve(1, 1, True)
        if k == 1:

            @pl.when(has_outer)
            def _():
                for part_of in range(2):
                    pass_on(1, far_slot, part_of, [far[1]])
                expand(1, far_slot, tm)

    convolve(2 - 2 * side, 2 * side, False)

    @pl.when(has_outer)
    def _():
        for k in range(2):
            arrived(1, far_slot, 1 - tm, k)
        expand(1, far_slot, 1 - tm)

    @pl.when(inner)
    def _():
        mine = folded(2, bases[2])
        for i in range(CUTS):
            piece(2, passing, 0, pass_recv, mate_pair, i).wait_recv()
            span = slice(i * (PIECE // CUTS), (i + 1) * (PIECE // CUTS))
            outgoing[2, span, :] = (mine[span] + passing[0, span, :].astype(f32)).astype(bf16)
            piece(2, incoming, 3, piece_recv, stop, i).start()

    convolve(2 * side, 2 - 2 * side, False)

    def finish(total, slot, weighted):
        for frame in range(2):
            span = slice(frame * HALF, (frame + 1) * HALF)
            pad[0, 8 : HALF + 8, :] = total[3, span, :]
            pad[1, 8 : HALF + 8, :] = total[2, span, :]
            even = total[0, span, :] + pad[0, 7 : HALF + 7, :]
            odd = total[1, span, :] + pad[1, 9 : HALF + 9, :]
            lanes = (
                even[:, 0:128],
                jnp.concatenate([even[:, 128:CH], odd[:, 0:64]], axis=1),
                odd[:, 64:CH],
            )
            for j in range(3):
                value = lanes[j] * factor[j, frame] if weighted else lanes[j]
                wide[slot, pl.ds(2 * j + frame, HALF, stride=6), :] = value

    finish(fwd, 0, False)
    out_ref[...] = wide[0].astype(bf16)
    finish(bwd, 1, True)
    ig_ref[...] = wide[1].astype(bf16)

    piece(0, incoming, 0, piece_recv, mate_pair).wait_recv()
    total = folded(3, bases[3]) + incoming[0].astype(f32)

    @pl.when(inner)
    def _():
        for i in range(CUTS):
            piece(0, incoming, 3, piece_recv, stop, i).wait_recv()

    @pl.when(jnp.logical_not(inner))
    def _():
        for slot in range(1, 3):
            piece(0, incoming, slot, piece_recv, mate_pair).wait_recv()

    for i in range(1, 4):
        total = total + incoming[i].astype(f32)
    total = total * (1.0 / scale)
    sums[0, 0:TALL, :] = total[0:TALL]
    sums[1, 0:CUT, 0:64] = total[TALL:PIECE, 0:64]
    sums[1, CUT:TALL, 0:64] = total[TALL : 2 * TALL - CUT, 64:128]
    for q in range(4):

        @pl.when(shard(pair) % 4 == q)
        def _():
            even, odd = (pl.ds(4 * q + i, CHUNK // 2, stride=2) for i in range(2))
            low = sums[0, odd, :]
            lanes = (
                sums[0, even, :],
                jnp.concatenate([sums[1, even, :][:, 0:64], low[:, 0:64]], axis=1),
                jnp.concatenate([low[:, 64:128], sums[1, odd, :][:, 0:64]], axis=1),
            )
            for j in range(3):
                wide[0, pl.ds(j, CHUNK // 2, stride=3), :] = lanes[j]

    fg_ref[...] = wide[0, 0 : CHUNK // 2 * 3, :].astype(bf16)

    for copies in to_partner + to_sibling + onward:
        for copy in copies:
            copy.wait_send()

    @pl.when(has_outer)
    def _():
        for copies in outward + far:
            for copy in copies:
                copy.wait_send()

    @pl.when(has_inner)
    def _():
        for copy in near + relayed + across:
            copy.wait_send()

    for p in range(PAIRS):

        @pl.when(pair == p)
        def _():
            for k in range(3):
                for copy in pieces_of(p, k):
                    copy.wait_send()


def hand_over(*refs):
    copies = [
        pltpu.make_async_copy(refs[i], refs[3 + i], refs[6].at[i]) for i in range(3)
    ]
    for copy in copies:
        copy.start()
    for copy in copies:
        copy.wait()


def fused(inputs, weight, cotangent):
    frames, rows = inputs.shape[:2]
    scale = frames * lax.axis_size("tm") * rows * lax.axis_size("row")
    lines = WIDTH * CH // 128
    vmem, hbm = (pl.BlockSpec(memory_space=m) for m in (pltpu.VMEM, pltpu.HBM))
    bf16, f32 = jnp.bfloat16, jnp.float32

    def interleaved(array):
        return array.reshape(2, lines, 128).transpose(1, 0, 2).reshape(2 * lines, 128)

    def parted(array):
        return array.reshape(lines, 2, 128).transpose(1, 0, 2).reshape(2, 1, lines * 128)

    out, ig, fg = pl.pallas_call(
        functools.partial(fused_kernel, float(scale)),
        out_shape=(
            jax.ShapeDtypeStruct((2 * lines, 128), bf16),
            jax.ShapeDtypeStruct((2 * lines, 128), bf16),
            jax.ShapeDtypeStruct((CHUNK // 2 * 3, 128), bf16),
        ),
        in_specs=[hbm, hbm, hbm],
        out_specs=(vmem, vmem, vmem),
        scratch_shapes=[
            pltpu.VMEM((2, 4, 2, 2 * lines, 128), bf16),
            pltpu.VMEM((CH, TAPS * CH), bf16),
            pltpu.VMEM((2, 2 * lines, 128), f32),
            pltpu.VMEM((3, 2, HALF, 128), f32),
            pltpu.VMEM((4, 3, 6 * HALF, 128), bf16),
            pltpu.VMEM((4, 3, 6 * HALF, 128), bf16),
            pltpu.VMEM((TAPS, CH, 256), bf16),
            pltpu.VMEM((TAPS, CH, 256), bf16),
            pltpu.VMEM((TAPS, CH + 128, CH), bf16),
            pltpu.VMEM((4, CH, 6 * PITCH), bf16),
            pltpu.VMEM((3, 2, 4 * PITCH, CH), bf16),
            pltpu.VMEM((4, 3 * CH, CH), f32),
            pltpu.VMEM((3, PIECE, 128), bf16),
            pltpu.VMEM((1, PIECE, 128), bf16),
            pltpu.VMEM((4, PIECE, 128), bf16),
            pltpu.VMEM((4, 2 * HALF, CH), f32),
            pltpu.VMEM((4, 2 * HALF, CH), f32),
            pltpu.VMEM((2, HALF + 16, CH), f32),
            pltpu.VMEM((2, TALL, 128), f32),
            pltpu.SemaphoreType.REGULAR,
            pltpu.SemaphoreType.DMA((3,)),
            pltpu.SemaphoreType.DMA((28,)),
            pltpu.SemaphoreType.DMA((2, 4, 2, 2)),
            pltpu.SemaphoreType.DMA((3 * CUTS,)),
            pltpu.SemaphoreType.DMA((CUTS,)),
            pltpu.SemaphoreType.DMA((3 + CUTS,)),
        ],
        compiler_params=pltpu.CompilerParams(
            collective_id=0, has_side_effects=True, vmem_limit_bytes=int(53.4 * 1024 * 1024)
        ),
    )(interleaved(inputs), weight.T, interleaved(cotangent))
    results = (out, ig, fg)
    out, ig, fg = pl.pallas_call(
        hand_over,
        out_shape=tuple(jax.ShapeDtypeStruct(r.shape, r.dtype) for r in results),
        in_specs=[pl.BlockSpec(memory_space=pl.ANY)] * 3,
        out_specs=(hbm, hbm, hbm),
        scratch_shapes=[pltpu.SemaphoreType.DMA((3,))],
        compiler_params=pltpu.CompilerParams(vmem_limit_bytes=1024 * 1024),
    )(*results)
    return parted(out), parted(ig), fg.reshape(-1)


def passed_along(array, axis, by):
    length = lax.axis_size(axis)
    pairs = [(i, i + by) for i in range(length) if 0 <= i + by < length]
    return lax.ppermute(array, axis, pairs)


def with_halo(array, sides, width):
    for axis, dim in sides:
        size, length = (lax.axis_size(axis), array.shape[dim])
        up = [(i, (i + 1) % size) for i in range(size - 1)]
        down = [(j, i) for i, j in up]
        last = lax.slice_in_dim(array, length - width, length, axis=dim)
        first = lax.slice_in_dim(array, 0, width, axis=dim)
        before = lax.ppermute(last, axis, up)
        after = lax.ppermute(first, axis, down)
        array = jnp.concatenate([before, array, after], axis=dim)
    return array


def on_device(inputs, weight, cotangent):
    frames = inputs.shape[0]
    rows = inputs.shape[1]
    act = jax.nn.silu(inputs.astype(jnp.float32)).astype(jnp.bfloat16)
    earlier = passed_along(act, "tm", 1)
    extended = jnp.concatenate([earlier, act], 0)
    extended = with_halo(extended, (("row", 1),), 1)
    extended = extended.reshape(frames + 2, rows + 2, WIDTH, CH)
    act_pad = jnp.pad(extended, ((0, 0), (0, 0), (1, 1), (0, 0)))
    cot_four = cotangent.reshape(frames, rows, WIDTH, CH)
    cot_flat = cot_four.reshape(-1, CH)
    output = jnp.zeros((frames * rows * WIDTH, CH), jnp.float32)
    blocks = []
    for step_t in range(3):
        for step_h in range(3):
            for step_w in range(3):
                offset = ((step_t * 3 + step_h) * 3 + step_w) * CH
                kernel = weight[offset : offset + CH]
                piece = act_pad[
                    step_t : step_t + frames, step_h : step_h + rows, step_w : step_w + WIDTH
                ].reshape(-1, CH)
                output = output + jnp.dot(piece, kernel, preferred_element_type=jnp.float32)
                blocks.append(
                    lax.dot_general(
                        piece,
                        cot_flat,
                        (((0,), (0,)), ((), ())),
                        preferred_element_type=jnp.float32,
                    )
                )
    spread = jnp.zeros((frames + 2, rows + 2, WIDTH + 2, CH), jnp.float32)
    for step_t in range(3):
        slab_weight = weight[step_t * 9 * CH : (step_t + 1) * 9 * CH]
        terms = lax.dot_general(
            cot_flat, slab_weight, (((1,), (1,)), ((), ())), preferred_element_type=jnp.float32
        )
        terms = terms.reshape(frames, rows, WIDTH, 9, CH)
        slab = jnp.zeros((frames, rows + 2, WIDTH + 2, CH), jnp.float32)
        for step_h in range(3):
            for step_w in range(3):
                slab = slab + jnp.pad(
                    terms[:, :, :, step_h * 3 + step_w],
                    ((0, 0), (step_h, 2 - step_h), (step_w, 2 - step_w), (0, 0)),
                )
        spread = spread + jnp.pad(slab, ((step_t, 2 - step_t), (0, 0), (0, 0), (0, 0)))
    inner = spread[:, :, 1 : WIDTH + 1]
    from_next = passed_along(inner[:, 0:1], "row", -1)
    from_prev = passed_along(inner[:, rows + 1 : rows + 2], "row", 1)
    center = inner[:, 1 : rows + 1]
    center = center.at[:, rows - 1 : rows].add(from_next)
    center = center.at[:, 0:1].add(from_prev)
    returned = passed_along(center[0:2], "tm", -1)
    grad_act = center[2:].at[frames - 2 :].add(returned).reshape(-1, CH)
    x_float = inputs.reshape(-1, CH).astype(jnp.float32)
    sigma = jax.nn.sigmoid(x_float)
    input_grad = (grad_act * sigma * (1.0 + x_float * (1.0 - sigma))).astype(jnp.bfloat16)
    local_filter = jnp.concatenate(blocks, 0).reshape(-1)
    frame_blocks = lax.axis_size("tm")
    row_blocks = lax.axis_size("row")
    scale = frames * frame_blocks * rows * row_blocks
    share = lax.psum_scatter(local_filter, ("tm", "row"), scatter_dimension=0, tiled=True)
    filter_grad = (share / scale).astype(jnp.bfloat16)
    shape = (frames, rows, WIDTH * CH)
    return (output.astype(jnp.bfloat16).reshape(shape), input_grad.reshape(shape), filter_grad)


def either(mesh, inputs, weight, cotangent):
    size = mesh.shape["row"]
    if mesh.shape["tm"] == 2 and size == 2 * PAIRS and inputs.shape[:2] == (2, 1):
        return fused(inputs, weight, cotangent)
    return on_device(inputs, weight, cotangent)


def solution(mesh):
    placed = (P(("grp", "tm"), "row", None), P(), P(("grp", "tm"), "row", None))
    return jax.shard_map(
        functools.partial(either, mesh),
        mesh=mesh,
        in_specs=placed,
        out_specs=(
            P(("grp", "tm"), "row", None),
            P(("grp", "tm"), "row", None),
            P(("grp", "tm", "row")),
        ),
        check_vma=False,
    )
```

```python
import functools

import jax
import jax.numpy as jnp
from jax import lax
from jax.experimental import pallas as pl
from jax.experimental.pallas import tpu as pltpu
from jax.sharding import PartitionSpec as P

CH = 192
WIDTH = 224
TAPS = 27
HALF = WIDTH // 2
LINES = WIDTH * CH // 128
PAIRS = 4
CHUNK = TAPS * CH // (4 * PAIRS)
TALL = CHUNK + 12
CUT = 176
PIECE = TALL + CUT
CUTS = 4
ORDER = ((3, 2, 1, 0), (0, 3, 2, 1), (0, 3, 1, 2), (0, 1, 2, 3))
PITCH = 256


def fused_kernel(
    scale, x_ref, w_ref, c_ref, out_ref, ig_ref, fg_ref,
    raw, weight_in, wide, factor, act, cot, fwd_even, fwd_odd, bwd_taps, act_t, shifted, filt,
    outgoing, passing, incoming, fwd, bwd, pad, sums,
    known, fetch_sem, send_sem, recv_sem, piece_send, pass_recv, piece_recv,
):
    f32, bf16 = jnp.float32, jnp.bfloat16
    grp, tm, row = lax.axis_index("grp"), lax.axis_index("tm"), lax.axis_index("row")
    pair, side = row // 2, row % 2
    own, other_slot = 1 + side, 2 - side

    def device(t, r):
        return (grp, t, r)

    barrier = pltpu.get_barrier_semaphore()

    def greet(target):
        pl.semaphore_signal(barrier, inc=1, device_id=target, device_id_type=pl.DeviceIdType.MESH)

    fetches = [
        pltpu.make_async_copy(src, dst, fetch_sem.at[i])
        for i, (src, dst) in enumerate(
            ((x_ref, raw.at[0, own, tm]), (c_ref, raw.at[1, own, tm]), (w_ref, weight_in))
        )
    ]
    sibling = device(1 - tm, row)
    partner = device(tm, 2 * pair + 1 - side)
    greet(sibling)
    greet(partner)
    has_before, has_after = pair > 0, pair < PAIRS - 1
    part = pair // 2
    inner = (pair + part) % 2 == 1
    mate_pair = pair + 1 - 2 * (pair % 2)
    stop, end = 2 - part, 3 * (1 - part)
    for step, present in ((-1, has_before), (1, has_after)):

        @pl.when(present)
        def _():
            greet(device(tm, 2 * (pair + step) + side))

    for fetch in fetches:
        fetch.start()

    def block(index):
        return pl.ds(pl.multiple_of(index * HALF, 16), HALF)

    lanes_used = iter(range(28))

    def move(array, src_slot, dst_slot, half, target):
        copies = []
        for k in range(2):
            span = pl.ds(k * LINES, LINES)
            src = (c_ref if array else x_ref) if src_slot is None else raw.at[array, src_slot, half]
            copies.append(
                pltpu.make_async_remote_copy(
                    src_ref=src.at[span],
                    dst_ref=raw.at[array, dst_slot, half, span],
                    send_sem=send_sem.at[next(lanes_used)],
                    recv_sem=recv_sem.at[array, dst_slot, half, k],
                    device_id=target,
                    device_id_type=pl.DeviceIdType.MESH,
                )
            )
        return copies

    def arrived(array, slot, half, k):
        ref = raw.at[array, slot, half, pl.ds(k * LINES, LINES)]
        pltpu.make_async_remote_copy(
            src_ref=ref,
            dst_ref=ref,
            send_sem=send_sem.at[0],
            recv_sem=recv_sem.at[array, slot, half, k],
            device_id=sibling,
            device_id_type=pl.DeviceIdType.MESH,
        ).wait_recv()

    outer_pair = pair + 2 * side - 1
    inner_pair = pair + 1 - 2 * side
    has_outer = jnp.logical_and(outer_pair >= 0, outer_pair < PAIRS)
    has_inner = jnp.logical_and(inner_pair >= 0, inner_pair < PAIRS)
    outer_same = device(tm, 2 * outer_pair + side)
    inner_same = device(tm, 2 * inner_pair + side)
    near_slot, far_slot = 3 * (1 - side), 3 * side

    to_partner = [move(i, None, own, tm, partner) for i in range(2)]
    to_sibling = [move(i, None, own, tm, sibling) for i in range(2)]
    outward = [move(i, None, near_slot, tm, outer_same) for i in range(2)]
    onward = [move(i, other_slot, other_slot, tm, sibling) for i in range(2)]
    relayed = move(0, other_slot, far_slot, tm, inner_same)
    across = move(1, near_slot, near_slot, tm, partner)
    near = move(0, near_slot, near_slot, tm, sibling)
    far = [move(i, far_slot, far_slot, tm, sibling) for i in range(2)]

    def expand(array, slot, half, keep=False):
        wide[array] = raw[array, slot, half].astype(f32)
        for j in range(3):
            for frame in range(2):
                value = wide[array, pl.ds(2 * j + frame, HALF, stride=6), :]
                if array == 0:
                    sigma = 1.0 / (1.0 + jnp.exp(-value))
                    if keep:
                        factor[j, frame] = sigma * (1.0 + value * (1.0 - sigma))
                    act[slot, j, block(2 * half + 2 + frame), :] = (value * sigma).astype(bf16)
                else:
                    cot[slot, j, block(2 * half + frame), :] = value.astype(bf16)

    def announce(target):
        pl.semaphore_signal(
            known, inc=1, device_id=device(tm, 2 * target + side), device_id_type=pl.DeviceIdType.MESH
        )

    pl.semaphore_wait(barrier, jnp.where(inner, 4, 3))

    @pl.when(inner)
    def _():
        announce(stop)

    for i in range(2):
        for k in range(2):
            to_partner[i][k].start()

        @pl.when(has_outer)
        def _():
            for k in range(2):
                outward[i][k].start()

        for k in range(2):
            to_sibling[i][k].start()

    for i in range(2):
        fetches[i].wait()
        expand(i, own, tm, keep=i == 0)

    for slot in range(4):
        act[slot, :, 0 : 2 * HALF, :] = jnp.zeros((3, 2 * HALF, 128), bf16)
        cot[slot, :, 4 * HALF : 6 * HALF, :] = jnp.zeros((3, 2 * HALF, 128), bf16)
        act_t[slot, :, 0 : 2 * PITCH] = jnp.zeros((CH, 2 * PITCH), bf16)

    for slot, present in ((0, has_before), (3, has_after)):

        @pl.when(jnp.logical_not(present))
        def _():
            act[slot, :, 2 * HALF : 6 * HALF, :] = jnp.zeros((3, 4 * HALF, 128), bf16)
            cot[slot, :, 0 : 4 * HALF, :] = jnp.zeros((3, 4 * HALF, 128), bf16)
            act_t[slot, :, 2 * PITCH : 6 * PITCH] = jnp.zeros((CH, 4 * PITCH), bf16)


    @pl.when(inner)
    def _():
        incoming[1:3] = jnp.zeros((2, PIECE, 128), bf16)

    @pl.when(jnp.logical_not(inner))
    def _():
        incoming[3] = jnp.zeros((PIECE, 128), bf16)

    pad[:, 0:8, :] = jnp.zeros((2, 8, CH), f32)
    pad[:, HALF + 8 : HALF + 16, :] = jnp.zeros((2, 8, CH), f32)
    for i in range(8):
        shifted[:, :, i * 128 + HALF : (i + 1) * 128, :] = jnp.zeros(
            (3, 2, 128 - HALF, CH), bf16
        )
    bwd_taps[:, 0:64, :] = jnp.zeros((TAPS, 64, CH), bf16)
    bwd_taps[:, 64 + CH : 128 + CH, :] = jnp.zeros((TAPS, 64, CH), bf16)

    fetches[2].wait()
    for tap in range(TAPS):
        value = weight_in[:, tap * CH : (tap + 1) * CH]
        fwd_even[tap] = jnp.concatenate([value, jnp.zeros((CH, 64), bf16)], axis=1)
        fwd_odd[tap] = jnp.concatenate([jnp.zeros((CH, 64), bf16), value], axis=1)
        bwd_taps[tap, 64 : 64 + CH, :] = value

    def transpose(slot, half):
        for frame in range(2):
            lane = (2 * half + 2 + frame) * PITCH
            even = pl.ds(pl.multiple_of(lane, 128), 128)
            odd = pl.ds(pl.multiple_of(lane + 128, 128), 128)

            def turned(j):
                value = act[slot, j, block(2 * half + 2 + frame), :]
                return jnp.concatenate([value, jnp.zeros((128 - HALF, 128), bf16)], axis=0).T

            act_t[slot, 0:128, even] = turned(0)
            both = turned(1)
            act_t[slot, 128:CH, even] = both[0:64]
            act_t[slot, 0:64, odd] = both[64:128]
            act_t[slot, 64:CH, odd] = turned(2)

    transpose(own, tm)

    def dots(ref, slot, starts, weights, out, first):
        def side_of(start, j):
            rows_of = pl.ds(pl.multiple_of(start, 16), 2 * HALF)
            return jnp.concatenate([ref[slot, j, rows_of, :], ref[slot, j + 1, rows_of, :]], axis=1)

        for i, terms in enumerate((((0, 1), (1, 2)), ((1, 1), (0, 0)), ((0, 2),), ((1, 0),))):
            total = None
            for step_t in range(3):
                for odd, step_w in terms:
                    more = weights(side_of(starts[step_t], odd), odd, step_t, step_w)
                    total = more if total is None else total + more
            if first:
                out[i] = total
            else:
                out[i] += total

    def convolve(act_h, cot_h, first):
        def forward(value, odd, step_t, step_w):
            taps = fwd_odd if odd else fwd_even
            return lax.dot_general(
                value,
                taps[(step_t * 3 + act_h) * 3 + step_w],
                (((1,), (1,)), ((), ())),
                preferred_element_type=f32,
            )

        def backward(value, odd, step_t, step_w):
            first_row = 0 if odd else 64
            return jnp.dot(
                value,
                bwd_taps[(step_t * 3 + cot_h) * 3 + 2 - step_w, first_row : first_row + 256, :],
                preferred_element_type=f32,
            )

        starts = [(2 * tm + step_t) * HALF for step_t in range(3)]
        dots(act, side + act_h, starts, forward, fwd, first)
        dots(cot, side + 2 - cot_h, starts[::-1], backward, bwd, first)

    def shift(h, half):
        for frame in range(2):
            rows_of = block(2 * half + frame)
            mid = cot[1 + h, 1, rows_of, :]
            even = jnp.concatenate([cot[1 + h, 0, rows_of, :], mid[:, 0:64]], axis=1)
            odd = jnp.concatenate([mid[:, 64:128], cot[1 + h, 2, rows_of, :]], axis=1)
            pad[0, 8 : HALF + 8, :] = even.astype(f32)
            pad[1, 8 : HALF + 8, :] = odd.astype(f32)
            first, second = (
                pl.ds(pl.multiple_of((2 * half + frame) * PITCH + i * 128, 128), HALF)
                for i in range(2)
            )
            shifted[0, h, first, :] = odd
            shifted[0, h, second, :] = pad[0, 9 : HALF + 9, :].astype(bf16)
            shifted[1, h, first, :] = even
            shifted[1, h, second, :] = odd
            shifted[2, h, first, :] = pad[1, 7 : HALF + 7, :].astype(bf16)
            shifted[2, h, second, :] = even

    def complete(array, slot, half):
        for k in range(2):
            arrived(array, slot, half, k)
        expand(array, slot, half)
        if array == 0:
            transpose(slot, half)

    complete(0, own, 1 - tm)
    complete(1, own, 1 - tm)

    @pl.when(inner)
    def _():
        pl.semaphore_wait(known, 1)
        announce(mate_pair)


    def pass_on(array, slot, k, copies):
        arrived(array, slot, tm, k)
        for copy in copies:
            copy[k].start()

    def pass_other(k):
        pass_on(0, other_slot, k, [])

        @pl.when(has_inner)
        def _():
            relayed[k].start()

        onward[0][k].start()

    pass_other(0)
    pass_other(1)
    expand(0, other_slot, tm)
    transpose(other_slot, tm)

    @pl.when(has_inner)
    def _():
        for k in range(2):
            pass_on(0, near_slot, k, [near])
        expand(0, near_slot, tm)
        transpose(near_slot, tm)

    for half in range(2):
        shift(side, half)
    complete(0, other_slot, 1 - tm)

    @pl.when(has_inner)
    def _():
        complete(0, near_slot, 1 - tm)

    for k in range(2):
        pass_on(1, other_slot, k, [onward[1]])

        @pl.when(has_outer)
        def _():
            pass_on(0, far_slot, k, [far[0]])

        @pl.when(has_inner)
        def _():
            pass_on(1, near_slot, k, [across])

    @pl.when(has_outer)
    def _():
        expand(0, far_slot, tm)
        transpose(far_slot, tm)

    expand(1, other_slot, tm)
    shift(1 - side, tm)

    @pl.when(has_outer)
    def _():
        complete(0, far_slot, 1 - tm)

    def at_pair(values):
        chosen = jnp.int32(values[0])
        for p in range(1, PAIRS):
            chosen = jnp.where(pair == p, jnp.int32(values[p]), chosen)
        return chosen

    owners = tuple(at_pair([ORDER[p][k] for p in range(PAIRS)]) for k in range(PAIRS))

    def shard(owner):
        return tm * 2 * PAIRS + 2 * owner + side

    def filter_sum(k, late=None):
        first_block = shard(owners[k]) * CHUNK // 16
        first_tap = first_block // (CH // 16)
        base = pl.multiple_of(first_block % (CH // 16) * 16, 16)

        def over(tap, i, half, frames):
            step_t, step_h, step_w = tap // 9, tap // 3 % 3, tap % 3
            lanes = pl.ds(pl.multiple_of((step_t + 2 * half) * PITCH, 128), frames * PITCH)
            rows_of = pl.ds(pl.multiple_of(2 * half * PITCH, 16), frames * PITCH)
            return jnp.dot(
                act_t[step_h + i, :, lanes],
                shifted[step_w, i, rows_of, :],
                preferred_element_type=f32,
            )

        def term(n):
            tap = first_tap + n
            span = slice(n * CH, (n + 1) * CH)
            if late is None:
                filt[k, span, :] = over(tap, 0, 0, 4) + over(tap, 1, 0, 4)
            elif late:
                filt[k, span, :] += over(tap, 1 - side, 1 - tm, 2)
            else:
                filt[k, span, :] = over(tap, side, 0, 4) + over(tap, 1 - side, tm, 2)

        term(0)
        term(1)

        @pl.when(base + TALL > 2 * CH)
        def _():
            term(2)

        return base

    filter_sum(0, late=False)
    complete(1, other_slot, 1 - tm)
    shift(1 - side, 1 - tm)


    def folded(k, base):
        high = filt[k, pl.ds(base, TALL), 128:CH]
        return jnp.concatenate(
            [
                filt[k, pl.ds(base, TALL), 0:128],
                jnp.concatenate(
                    [
                        high[0:CUT],
                        jnp.concatenate([high[CUT:TALL], jnp.zeros((2 * CUT - TALL, 64), f32)], axis=0),
                    ],
                    axis=1,
                ),
            ],
            axis=0,
        )

    def piece(k, ref, slot, recv, owner, part_of=None):
        src, dst, sem = outgoing.at[k], ref.at[slot], recv.at[slot]
        if part_of is not None:
            span = pl.ds(part_of * (PIECE // CUTS), PIECE // CUTS)
            src, dst, sem = src.at[span], dst.at[span], recv.at[slot + part_of]
        return pltpu.make_async_remote_copy(
            src_ref=src,
            dst_ref=dst,
            send_sem=piece_send.at[CUTS * k + (part_of or 0)],
            recv_sem=sem,
            device_id=device(tm, 2 * owner + side),
            device_id_type=pl.DeviceIdType.MESH,
        )

    def pieces_of(p, k):
        mate, owner = p + 1 - 2 * (p % 2), ORDER[p][k]
        if owner == mate:
            return [piece(k, incoming, 0, piece_recv, mate)]
        if owner in (0, 3):
            return [piece(k, incoming, 2 if p in (1, 2) else 1, piece_recv, owner)]
        if p in (1, 2):
            return [piece(k, incoming, 3, piece_recv, owner, i) for i in range(CUTS)]
        return [piece(k, passing, 0, pass_recv, mate, i) for i in range(CUTS)]

    bases = [filter_sum(0, late=True)]
    for k in range(4):
        if k > 0:
            bases.append(filter_sum(k))
        if k == 3:
            break
        outgoing[k] = folded(k, bases[k]).astype(bf16)
        for p in range(PAIRS):
            if p in (1, 2) and k == 2:
                continue

            @pl.when(pair == p)
            def _():
                if p in (0, 3) and ORDER[p][k] == 3 - p:
                    pl.semaphore_wait(known, 1)
                for copy in pieces_of(p, k):
                    copy.start()

        if k == 0:
            convolve(1, 1, True)
        if k == 1:

            @pl.when(has_outer)
            def _():
                for part_of in range(2):
                    pass_on(1, far_slot, part_of, [far[1]])
                expand(1, far_slot, tm)

    @pl.when(has_outer)
    def _():
        for k in range(2):
            arrived(1, far_slot, 1 - tm, k)
        expand(1, far_slot, 1 - tm)

    @pl.when(inner)
    def _():
        mine = folded(2, bases[2])
        for i in range(CUTS):
            piece(2, passing, 0, pass_recv, mate_pair, i).wait_recv()
            span = slice(i * (PIECE // CUTS), (i + 1) * (PIECE // CUTS))
            outgoing[2, span, :] = (mine[span] + passing[0, span, :].astype(f32)).astype(bf16)
            piece(2, incoming, 3, piece_recv, stop, i).start()

    convolve(2 - 2 * side, 2 * side, False)

    convolve(2 * side, 2 - 2 * side, False)

    def finish(total, slot, weighted):
        for frame in range(2):
            span = slice(frame * HALF, (frame + 1) * HALF)
            pad[0, 8 : HALF + 8, :] = total[3, span, :]
            pad[1, 8 : HALF + 8, :] = total[2, span, :]
            even = total[0, span, :] + pad[0, 7 : HALF + 7, :]
            odd = total[1, span, :] + pad[1, 9 : HALF + 9, :]
            lanes = (
                even[:, 0:128],
                jnp.concatenate([even[:, 128:CH], odd[:, 0:64]], axis=1),
                odd[:, 64:CH],
            )
            for j in range(3):
                value = lanes[j] * factor[j, frame] if weighted else lanes[j]
                wide[slot, pl.ds(2 * j + frame, HALF, stride=6), :] = value

    finish(fwd, 0, False)
    out_ref[...] = wide[0].astype(bf16)
    finish(bwd, 1, True)
    ig_ref[...] = wide[1].astype(bf16)

    piece(0, incoming, 0, piece_recv, mate_pair).wait_recv()
    total = folded(3, bases[3]) + incoming[0].astype(f32)

    @pl.when(inner)
    def _():
        for i in range(CUTS):
            piece(0, incoming, 3, piece_recv, stop, i).wait_recv()

    @pl.when(jnp.logical_not(inner))
    def _():
        for slot in range(1, 3):
            piece(0, incoming, slot, piece_recv, mate_pair).wait_recv()

    for i in range(1, 4):
        total = total + incoming[i].astype(f32)
    total = total * (1.0 / scale)
    sums[0, 0:TALL, :] = total[0:TALL]
    sums[1, 0:CUT, 0:64] = total[TALL:PIECE, 0:64]
    sums[1, CUT:TALL, 0:64] = total[TALL : 2 * TALL - CUT, 64:128]
    for q in range(4):

        @pl.when(shard(pair) % 4 == q)
        def _():
            even, odd = (pl.ds(4 * q + i, CHUNK // 2, stride=2) for i in range(2))
            low = sums[0, odd, :]
            lanes = (
                sums[0, even, :],
                jnp.concatenate([sums[1, even, :][:, 0:64], low[:, 0:64]], axis=1),
                jnp.concatenate([low[:, 64:128], sums[1, odd, :][:, 0:64]], axis=1),
            )
            for j in range(3):
                wide[0, pl.ds(j, CHUNK // 2, stride=3), :] = lanes[j]

    fg_ref[...] = wide[0, 0 : CHUNK // 2 * 3, :].astype(bf16)

    for copies in to_partner + to_sibling + onward:
        for copy in copies:
            copy.wait_send()

    @pl.when(has_outer)
    def _():
        for copies in outward + far:
            for copy in copies:
                copy.wait_send()

    @pl.when(has_inner)
    def _():
        for copy in near + relayed + across:
            copy.wait_send()

    for p in range(PAIRS):

        @pl.when(pair == p)
        def _():
            for k in range(3):
                for copy in pieces_of(p, k):
                    copy.wait_send()


def hand_over(*refs):
    copies = [
        pltpu.make_async_copy(refs[i], refs[3 + i], refs[6].at[i]) for i in range(3)
    ]
    for copy in copies:
        copy.start()
    for copy in copies:
        copy.wait()


def fused(inputs, weight, cotangent):
    frames, rows = inputs.shape[:2]
    scale = frames * lax.axis_size("tm") * rows * lax.axis_size("row")
    lines = WIDTH * CH // 128
    vmem, hbm = (pl.BlockSpec(memory_space=m) for m in (pltpu.VMEM, pltpu.HBM))
    bf16, f32 = jnp.bfloat16, jnp.float32

    def interleaved(array):
        return array.reshape(2, lines, 128).transpose(1, 0, 2).reshape(2 * lines, 128)

    def parted(array):
        return array.reshape(lines, 2, 128).transpose(1, 0, 2).reshape(2, 1, lines * 128)

    out, ig, fg = pl.pallas_call(
        functools.partial(fused_kernel, float(scale)),
        out_shape=(
            jax.ShapeDtypeStruct((2 * lines, 128), bf16),
            jax.ShapeDtypeStruct((2 * lines, 128), bf16),
            jax.ShapeDtypeStruct((CHUNK // 2 * 3, 128), bf16),
        ),
        in_specs=[hbm, hbm, hbm],
        out_specs=(vmem, vmem, vmem),
        scratch_shapes=[
            pltpu.VMEM((2, 4, 2, 2 * lines, 128), bf16),
            pltpu.VMEM((CH, TAPS * CH), bf16),
            pltpu.VMEM((2, 2 * lines, 128), f32),
            pltpu.VMEM((3, 2, HALF, 128), f32),
            pltpu.VMEM((4, 3, 6 * HALF, 128), bf16),
            pltpu.VMEM((4, 3, 6 * HALF, 128), bf16),
            pltpu.VMEM((TAPS, CH, 256), bf16),
            pltpu.VMEM((TAPS, CH, 256), bf16),
            pltpu.VMEM((TAPS, CH + 128, CH), bf16),
            pltpu.VMEM((4, CH, 6 * PITCH), bf16),
            pltpu.VMEM((3, 2, 4 * PITCH, CH), bf16),
            pltpu.VMEM((4, 3 * CH, CH), f32),
            pltpu.VMEM((3, PIECE, 128), bf16),
            pltpu.VMEM((1, PIECE, 128), bf16),
            pltpu.VMEM((4, PIECE, 128), bf16),
            pltpu.VMEM((4, 2 * HALF, CH), f32),
            pltpu.VMEM((4, 2 * HALF, CH), f32),
            pltpu.VMEM((2, HALF + 16, CH), f32),
            pltpu.VMEM((2, TALL, 128), f32),
            pltpu.SemaphoreType.REGULAR,
            pltpu.SemaphoreType.DMA((3,)),
            pltpu.SemaphoreType.DMA((28,)),
            pltpu.SemaphoreType.DMA((2, 4, 2, 2)),
            pltpu.SemaphoreType.DMA((3 * CUTS,)),
            pltpu.SemaphoreType.DMA((CUTS,)),
            pltpu.SemaphoreType.DMA((3 + CUTS,)),
        ],
        compiler_params=pltpu.CompilerParams(
            collective_id=0, has_side_effects=True, vmem_limit_bytes=int(53.4 * 1024 * 1024)
        ),
    )(interleaved(inputs), weight.T, interleaved(cotangent))
    results = (out, ig, fg)
    out, ig, fg = pl.pallas_call(
        hand_over,
        out_shape=tuple(jax.ShapeDtypeStruct(r.shape, r.dtype) for r in results),
        in_specs=[pl.BlockSpec(memory_space=pl.ANY)] * 3,
        out_specs=(hbm, hbm, hbm),
        scratch_shapes=[pltpu.SemaphoreType.DMA((3,))],
        compiler_params=pltpu.CompilerParams(vmem_limit_bytes=1024 * 1024),
    )(*results)
    return parted(out), parted(ig), fg.reshape(-1)


def passed_along(array, axis, by):
    length = lax.axis_size(axis)
    pairs = [(i, i + by) for i in range(length) if 0 <= i + by < length]
    return lax.ppermute(array, axis, pairs)


def with_halo(array, sides, width):
    for axis, dim in sides:
        size, length = (lax.axis_size(axis), array.shape[dim])
        up = [(i, (i + 1) % size) for i in range(size - 1)]
        down = [(j, i) for i, j in up]
        last = lax.slice_in_dim(array, length - width, length, axis=dim)
        first = lax.slice_in_dim(array, 0, width, axis=dim)
        before = lax.ppermute(last, axis, up)
        after = lax.ppermute(first, axis, down)
        array = jnp.concatenate([before, array, after], axis=dim)
    return array


def on_device(inputs, weight, cotangent):
    frames = inputs.shape[0]
    rows = inputs.shape[1]
    act = jax.nn.silu(inputs.astype(jnp.float32)).astype(jnp.bfloat16)
    earlier = passed_along(act, "tm", 1)
    extended = jnp.concatenate([earlier, act], 0)
    extended = with_halo(extended, (("row", 1),), 1)
    extended = extended.reshape(frames + 2, rows + 2, WIDTH, CH)
    act_pad = jnp.pad(extended, ((0, 0), (0, 0), (1, 1), (0, 0)))
    cot_four = cotangent.reshape(frames, rows, WIDTH, CH)
    cot_flat = cot_four.reshape(-1, CH)
    output = jnp.zeros((frames * rows * WIDTH, CH), jnp.float32)
    blocks = []
    for step_t in range(3):
        for step_h in range(3):
            for step_w in range(3):
                offset = ((step_t * 3 + step_h) * 3 + step_w) * CH
                kernel = weight[offset : offset + CH]
                piece = act_pad[
                    step_t : step_t + frames, step_h : step_h + rows, step_w : step_w + WIDTH
                ].reshape(-1, CH)
                output = output + jnp.dot(piece, kernel, preferred_element_type=jnp.float32)
                blocks.append(
                    lax.dot_general(
                        piece,
                        cot_flat,
                        (((0,), (0,)), ((), ())),
                        preferred_element_type=jnp.float32,
                    )
                )
    spread = jnp.zeros((frames + 2, rows + 2, WIDTH + 2, CH), jnp.float32)
    for step_t in range(3):
        slab_weight = weight[step_t * 9 * CH : (step_t + 1) * 9 * CH]
        terms = lax.dot_general(
            cot_flat, slab_weight, (((1,), (1,)), ((), ())), preferred_element_type=jnp.float32
        )
        terms = terms.reshape(frames, rows, WIDTH, 9, CH)
        slab = jnp.zeros((frames, rows + 2, WIDTH + 2, CH), jnp.float32)
        for step_h in range(3):
            for step_w in range(3):
                slab = slab + jnp.pad(
                    terms[:, :, :, step_h * 3 + step_w],
                    ((0, 0), (step_h, 2 - step_h), (step_w, 2 - step_w), (0, 0)),
                )
        spread = spread + jnp.pad(slab, ((step_t, 2 - step_t), (0, 0), (0, 0), (0, 0)))
    inner = spread[:, :, 1 : WIDTH + 1]
    from_next = passed_along(inner[:, 0:1], "row", -1)
    from_prev = passed_along(inner[:, rows + 1 : rows + 2], "row", 1)
    center = inner[:, 1 : rows + 1]
    center = center.at[:, rows - 1 : rows].add(from_next)
    center = center.at[:, 0:1].add(from_prev)
    returned = passed_along(center[0:2], "tm", -1)
    grad_act = center[2:].at[frames - 2 :].add(returned).reshape(-1, CH)
    x_float = inputs.reshape(-1, CH).astype(jnp.float32)
    sigma = jax.nn.sigmoid(x_float)
    input_grad = (grad_act * sigma * (1.0 + x_float * (1.0 - sigma))).astype(jnp.bfloat16)
    local_filter = jnp.concatenate(blocks, 0).reshape(-1)
    frame_blocks = lax.axis_size("tm")
    row_blocks = lax.axis_size("row")
    scale = frames * frame_blocks * rows * row_blocks
    share = lax.psum_scatter(local_filter, ("tm", "row"), scatter_dimension=0, tiled=True)
    filter_grad = (share / scale).astype(jnp.bfloat16)
    shape = (frames, rows, WIDTH * CH)
    return (output.astype(jnp.bfloat16).reshape(shape), input_grad.reshape(shape), filter_grad)


def either(mesh, inputs, weight, cotangent):
    size = mesh.shape["row"]
    if mesh.shape["tm"] == 2 and size == 2 * PAIRS and inputs.shape[:2] == (2, 1):
        return fused(inputs, weight, cotangent)
    return on_device(inputs, weight, cotangent)


def solution(mesh):
    placed = (P(("grp", "tm"), "row", None), P(), P(("grp", "tm"), "row", None))
    return jax.shard_map(
        functools.partial(either, mesh),
        mesh=mesh,
        in_specs=placed,
        out_specs=(
            P(("grp", "tm"), "row", None),
            P(("grp", "tm"), "row", None),
            P(("grp", "tm", "row")),
        ),
        check_vma=False,
    )
```
